512 devices in a mesh: lat: 16 (over y_hi, x), lon: 32 (over z, y_lo, core).
Axes of the slice: x: 4, y: 8 (y_hi: 4, y_lo: 2; y = y_hi * 2 + y_lo), z: 8, core: 2. Of those that a mesh axis runs over, the one named last changes fastest.
Arguments:
- tokens: bfloat16 [128, 1024, 1024], P('lat', 'lon'), may hold values from -40 to 40
- ln_gain: float32 [1024], replicated, may hold values from 0.1 to 1.9
- w_qkv: bfloat16 [1024, 1536], replicated, may hold values from -0.34375 to 0.34375
- bias_table: float32 [8, 225], replicated, may hold values from -4 to 4
- bias_index: int32 [64, 64], replicated, may hold values from 0 to 224
- cap_group: int32 [2, 256, 4, 1], P(None, 'lon'), may hold values from 0 to 31; in each aligned block of 32 rows (0 to 31, 32 to 63, ..., all dimensions but the last counted through in order) at most 2 rows name the same one
Outputs:
- mixed: bfloat16 [128, 1024, 512], P('lat', 'lon')
The draws below stay inside these ranges and needn't reach their ends.
Inputs may be any that keep to these rules, and one draw needn't show every extreme that they name: `cap_group`: within one pole, the 32 tiles of one longitude sector name any one group at most 2 times, and some sector names some group exactly 2 times.
All inputs are finite; a program needn't handle non-finite values.
Results may differ from the reference program's by a relative error of at most 0.0079.
Values may be sent and summed in bfloat16 or wider, within the bound.
No kernel may reach another device: no remote copies, remote signals or barrier semaphores. Data moves between devices by JAX's collectives and lax.ppermute only.
A program may use at most 128 MiB of HBM per device.

```python
import math
import jax
import jax.numpy as jnp
import numpy as np
from jax import lax

D = 1024
HEADS = 8
HD = 64
WIN = 8
TW = 4
CAP = 4
HW = 512
HALF = 4
BIAS_ROWS = 225
H = 128
W = 1024
TCOLS = 256
TILES_DEV = 32
MOST = 2
N_LON = 32


def draw_tokens(key, part):
    key_rows, key_cols, key_main = jax.random.split(key, 3)
    low = math.log(0.3)
    high = math.log(3.0)
    row_scale = jnp.exp(jax.random.uniform(key_rows, (H, W, 1), jnp.float32, low, high))
    col_scale = jnp.exp(jax.random.uniform(key_cols, (D,), jnp.float32, low, high))
    base = jnp.clip(jax.random.normal(key_main, (H, W, D), jnp.float32), -4.0, 4.0)
    return (base * row_scale * col_scale).astype(jnp.bfloat16)


def draw_w_qkv(key, part):
    key_main = jax.random.fold_in(jax.random.fold_in(key, 7), 0)
    full = jnp.clip(jax.random.normal(key_main, (D, 3 * HW), jnp.float32), -4.0, 4.0) * D ** (-0.5)
    return full.astype(jnp.bfloat16)


def touch_ends(entries, rng, least, top_value):
    spot = [jax.random.randint(jax.random.fold_in(rng, axis), (), 0, length) for axis, length in enumerate(entries.shape)]
    main_axis = entries.shape.index(max(entries.shape))
    neighbour = spot[:main_axis] + [(spot[main_axis] + 1) % entries.shape[main_axis]] + spot[main_axis + 1:]
    return entries.at[tuple(spot)].set(least).at[tuple(neighbour)].set(top_value)


def shared_out(rng, own, number, rows, number_of, top, most, slope):
    ranking = jax.random.permutation(rng, number_of)
    crowded, usual = load_shares(number_of, rows * top, most, slope, True), load_shares(number_of, rows * top, most, slope, False)
    places = jnp.arange(number_of)

    def named(tallies, turn):
        used = int((tallies > 0).sum())
        fixed = max(1, used // 4)
        moved = fixed + (places - fixed + turn * (used - fixed)) % max(1, number_of - fixed)
        return jnp.zeros((number_of,), jnp.int32).at[ranking[jnp.where(places < fixed, places, moved)]].set(jnp.asarray(tallies, jnp.int32))

    tallies = jnp.where(number % 4 == 0, named(crowded, number // 4), named(usual, number - number // 4 - 1))
    mixed = jax.random.permutation(jax.random.fold_in(own, 3), number_of)
    donor, taker = mixed[0:number_of // 2 * 2:2], mixed[1:number_of // 2 * 2:2]
    room = jnp.minimum(tallies[donor] - 1, most - tallies[taker]) // 2
    room = jnp.where((donor == ranking[0]) | (taker == ranking[0]) | (tallies[taker] == 0), 0, jnp.maximum(room, 0))
    moved = jax.random.randint(jax.random.fold_in(own, 4), (number_of // 2,), 0, 1 << 20) % (room + 1)
    tallies = tallies.at[donor].add(-moved).at[taker].add(moved)
    members = jnp.searchsorted(jnp.cumsum(tallies), jnp.arange(rows * top), side="right").astype(jnp.int32)
    table = members.reshape(top, rows).T
    table = table[jax.random.permutation(jax.random.fold_in(own, 1), rows)]
    turn = jax.random.randint(jax.random.fold_in(own, 2), (rows, 1), 0, top)
    return jnp.take_along_axis(table, (jnp.arange(top)[None, :] + turn) % top, axis=1)


def load_shares(count, total, most, skew, full):
    loads = [(1 << 20) // math.isqrt(standing ** skew) + 1 for standing in range(1, count + 1)]
    largest = most if full else min(most, max(-(-total // count), total * loads[0] // sum(loads)))
    least = 1 if total - largest >= count - 1 else 0
    holding, spare = [largest] + [least] * (count - 1), total - largest - least * (count - 1)
    while spare > 0:
        movable = [i for i in range(1, count) if holding[i] < largest] or [i for i in range(1, count) if holding[i] < most]
        pool, remaining = sum([loads[i] for i in movable]), spare
        for i in movable:
            more = min(most - holding[i], max(1, remaining * loads[i] // pool), spare)
            holding[i] = holding[i] + more
            spare = spare - more
    return np.array(holding)


def centred(own_key, extent, deviation, limit, kind=jnp.bfloat16):
    drawn = jax.random.normal(own_key, extent, jnp.float32) * deviation
    return jnp.minimum(jnp.maximum(drawn, -limit), limit).astype(kind)


def setup_inputs(seed: int = 0) -> dict:
    key_list = jax.random.split(jax.random.key(seed), 7)
    tokens = draw_tokens(jax.random.fold_in(key_list[6], 71), 0)
    ln_gain = jnp.clip(1.0 + 0.18 * jax.random.normal(key_list[1], (D,), jnp.float32), 0.1, 1.9)
    w_qkv = draw_w_qkv(jax.random.fold_in(key_list[6], 71), 0)
    bias_table = centred(key_list[3], (HEADS, BIAS_ROWS), 1.0, 4.0, jnp.float32)
    bias_index = touch_ends(jax.random.randint(key_list[4], (WIN * WIN, WIN * WIN), 0, BIAS_ROWS), jax.random.fold_in(key_list[4], 1), 0, BIAS_ROWS - 1).astype(jnp.int32)
    cap_group_keys = jax.random.split(jax.random.fold_in(key_list[5], 1), 2 * TCOLS * CAP // TILES_DEV)
    cap_group_turns = jax.random.permutation(jax.random.fold_in(key_list[5], 3), 2 * TCOLS * CAP // TILES_DEV)
    cap_group = jax.vmap(lambda own, number: shared_out(jax.random.fold_in(key_list[5], 2), own, number, TILES_DEV, N_LON, 1, MOST, 2))(cap_group_keys, cap_group_turns).reshape((2, TCOLS, CAP, 1))
    return dict(tokens=tokens, ln_gain=ln_gain, w_qkv=w_qkv, bias_table=bias_table, bias_index=bias_index, cap_group=cap_group)


epsilon = 1e-05
masked_score = -1e+30

def layer_norm(row_tokens, ln_gain):
    values = row_tokens.astype(jnp.float32)
    center = lax.optimization_barrier(jnp.mean(values, axis=-1, keepdims=True))
    spread = lax.optimization_barrier(jnp.mean(jnp.square(values - center), axis=-1, keepdims=True))
    return ((values - center) * lax.rsqrt(spread + epsilon) * ln_gain).astype(jnp.bfloat16)

def softmax_bf16(scores):
    highest = lax.optimization_barrier(jnp.max(scores, axis=-1, keepdims=True))
    raised = jnp.exp(scores - highest)
    return (raised / lax.optimization_barrier(jnp.sum(raised, axis=-1, keepdims=True))).astype(jnp.bfloat16)

def reference(tokens, ln_gain, w_qkv, bias_table, bias_index, cap_group):
    att_scale = HD ** (-0.5)

    def project_row(row_tokens):
        return jnp.dot(layer_norm(row_tokens, ln_gain), w_qkv, preferred_element_type=jnp.float32).astype(jnp.bfloat16)
    projected = lax.map(project_row, tokens)
    position_bias = bias_table[:, bias_index]
    shifted = jnp.roll(projected, HALF, axis=1)
    padded = jnp.pad(shifted, ((HALF, HALF), (0, 0), (0, 0)))
    strip_count = (H + WIN) // WIN
    strips = padded.reshape(strip_count, WIN, W, 3 * HW)

    def strip_attention(strip_item):
        strip_rows, strip_index = strip_item
        windows = strip_rows.reshape(WIN, W // WIN, WIN, 3 * HW).transpose(1, 0, 2, 3)
        windows = windows.reshape(W // WIN, WIN * WIN, 3 * HW).astype(jnp.float32)
        win_q = windows[:, :, :HW].reshape(-1, WIN * WIN, HEADS, HD)
        win_k = windows[:, :, HW:2 * HW].reshape(-1, WIN * WIN, HEADS, HD)
        win_v = windows[:, :, 2 * HW:].reshape(-1, WIN * WIN, HEADS, HD)
        scores = jnp.einsum('wqhd,wkhd->whqk', win_q, win_k) * att_scale + position_bias[None]
        row_pos = strip_index * WIN + jnp.arange(WIN * WIN, dtype=jnp.int32) // WIN
        valid = (row_pos >= HALF) & (row_pos < H + HALF)
        scores = jnp.where(valid[None, None, None, :], scores, masked_score)
        weights = softmax_bf16(scores).astype(jnp.float32)
        mixed_out = jnp.einsum('whqk,wkhd->wqhd', weights, win_v)
        mixed_out = mixed_out.reshape(W // WIN, WIN, WIN, HW).transpose(1, 0, 2, 3)
        return mixed_out.reshape(WIN, W, HW)
    win_strips = lax.map(strip_attention, (strips, jnp.arange(strip_count, dtype=jnp.int32)))
    win_out = win_strips.reshape(H + WIN, W, HW)[HALF:HALF + H]
    win_out = jnp.roll(win_out, -HALF, axis=1)

    def cap_pole(pole_rows, groups):
        token_group = jnp.repeat(groups.T, TW, axis=1).reshape(-1)
        flat_rows = pole_rows.reshape(CAP * W, 3 * HW).astype(jnp.float32)
        cap_keys = flat_rows[:, HW:2 * HW].reshape(-1, HEADS, HD)
        cap_values = flat_rows[:, 2 * HW:].reshape(-1, HEADS, HD)
        block_rows = math.gcd(CAP * W, 512)

        def one_block(block_start):
            query_block = lax.dynamic_slice_in_dim(flat_rows, block_start, block_rows, 0)[:, :HW]
            query_block = query_block.reshape(block_rows, HEADS, HD)
            group_block = lax.dynamic_slice_in_dim(token_group, block_start, block_rows, 0)
            scores = jnp.einsum('qhd,khd->hqk', query_block, cap_keys) * att_scale
            same_group = group_block[:, None] == token_group[None, :]
            scores = jnp.where(same_group[None], scores, masked_score)
            weights = softmax_bf16(scores).astype(jnp.float32)
            return jnp.einsum('hqk,khd->qhd', weights, cap_values).reshape(block_rows, HW)
        block_starts = jnp.arange(0, CAP * W, block_rows, dtype=jnp.int32)
        return lax.map(one_block, block_starts).reshape(CAP, W, HW).astype(jnp.bfloat16)
    north = cap_pole(projected[:CAP], cap_group[0, :, :, 0])
    south = cap_pole(projected[H - CAP:], cap_group[1, :, :, 0])
    win_out = win_out.at[:CAP].add(north.astype(jnp.float32))
    win_out = win_out.at[H - CAP:].add(south.astype(jnp.float32))
    return win_out.astype(jnp.bfloat16)
```

```python
import functools

import jax
import jax.numpy as jnp
from jax import lax
from jax.experimental import pallas as pl
from jax.experimental.pallas import tpu as pltpu
from jax.sharding import PartitionSpec as P

D = 1024
HEADS = 8
HD = 64
WIN = 8
TW = 4
CAP = 4
RH = 8
RW = 32
HW = 512
HALF = 4
BIAS_ROWS = 225
TILES_DEV = 32
GROUPS = 32
MOST = 2
SLOT_TOKENS = GROUPS * MOST * TW
CAP_TOKENS = CAP * RW
N_WIN = 10
WIN_B = 5
WTOK = WIN * WIN
QROWS = HALF * WIN

epsilon = 1e-05
masked_score = -1e30
EMPTY = 128.0
EMPTY_ABOVE = 64.0

VMEM = pltpu.VMEM
SMEM = pltpu.SMEM


def vspec():
    return pl.BlockSpec(memory_space=VMEM)


def sspec():
    return pl.BlockSpec(memory_space=SMEM)


def aspec():
    return pl.BlockSpec(memory_space=pl.ANY)


def norm_rows(values, gain):
    center = jnp.mean(values, axis=-1, keepdims=True)
    shifted = values - center
    spread = jnp.mean(jnp.square(shifted), axis=-1, keepdims=True)
    return shifted * lax.rsqrt(spread + epsilon) * gain


def slot_rows(group_ref, pole, lane):
    row = lane // RW
    col = lane % RW
    tile = (col // TW) * CAP + row
    group = jnp.zeros_like(lane)
    for t in range(TILES_DEV):
        group = jnp.where(tile == t, group_ref[pole, t], group)
    rank = jnp.zeros_like(lane)
    for t in range(TILES_DEV):
        same = (group == group_ref[pole, t]) & (tile > t)
        rank = rank + same.astype(jnp.int32)
    return (group * MOST + rank) * TW + col % TW


def pack_kernel(group_ref, tokens_ref, send_ref, rows, sem):
    north = lax.axis_index("lat") == 0
    pole = jnp.where(north, 0, 1)
    start = jnp.where(north, 0, RH - CAP)
    copy = pltpu.make_async_copy(tokens_ref.at[pl.ds(start, CAP)], rows, sem)
    copy.start()
    lane = lax.broadcasted_iota(jnp.int32, (8, CAP_TOKENS), 1)
    slot = slot_rows(group_ref, pole, lane)[0:1]
    copy.wait()
    x = rows[...].reshape(CAP_TOKENS, D)
    step = 64
    for i in range(0, SLOT_TOKENS, step):
        hit = lax.broadcasted_iota(jnp.int32, (step, CAP_TOKENS), 0) + i == slot
        hot = hit.astype(jnp.float32)
        filled = jnp.max(hot, axis=1, keepdims=True) > 0.5
        moved = jnp.dot(hot.astype(jnp.bfloat16), x, preferred_element_type=jnp.float32)
        send_ref[i : i + step, :] = jnp.where(filled, moved, EMPTY).astype(jnp.bfloat16)


def edge_kernel(group_ref, own_ref, north_ref, south_ref, left_ref, right_ref, undo_ref):
    lower = lax.broadcasted_iota(jnp.int32, (8, D), 0) < HALF

    def two(ref, i, base):
        first = [ref[i, 0:8].astype(jnp.float32), ref[i + 1, 0:8].astype(jnp.float32)]
        last = [ref[i, 24:32].astype(jnp.float32), ref[i + 1, 24:32].astype(jnp.float32)]
        head = jnp.where(lower, first[0], pltpu.roll(first[1], HALF, 0))
        tail = jnp.where(lower, pltpu.roll(last[0], HALF, 0), last[1])
        return head, tail

    pairs = [(north_ref, 0), (north_ref, 2)]
    pairs += [(own_ref, i) for i in range(0, RH, 2)]
    pairs += [(south_ref, 0), (south_ref, 2)]
    for n in range(0, len(pairs), 2):
        heads, tails = zip(*[two(ref, i, 0) for ref, i in pairs[n : n + 2]])
        left_ref[n * 8 : n * 8 + 16] = jnp.concatenate(heads, 0).astype(jnp.bfloat16)
        right_ref[n * 8 : n * 8 + 16] = jnp.concatenate(tails, 0).astype(jnp.bfloat16)

    lat = lax.axis_index("lat")
    north = lat == 0
    polar = north | (lat == lax.axis_size("lat") - 1)
    pole = jnp.where(north, 0, 1)
    token = lax.broadcasted_iota(jnp.int32, (CAP_TOKENS, 128), 0)
    slot = slot_rows(group_ref, pole, token)
    slot = jnp.where(polar, slot, -1)
    for i in range(0, SLOT_TOKENS, 128):
        hit = lax.broadcasted_iota(jnp.int32, (CAP_TOKENS, 128), 1) + i == slot
        undo_ref[:, i : i + 128] = hit.astype(jnp.float32).astype(jnp.bfloat16)


def cap_kernel(x_ref, gain_ref, w_ref, out_ref, normed, qkv, w, sem):
    n = SLOT_TOKENS
    copy = pltpu.make_async_copy(w_ref, w, sem)
    copy.start()
    gain = gain_ref[...]
    for i in range(0, n, 32):
        normed[i : i + 32] = norm_rows(x_ref[i : i + 32].astype(jnp.float32), gain).astype(jnp.bfloat16)
    pick = (lax.broadcasted_iota(jnp.int32, (8, 128), 1) == 0).astype(jnp.bfloat16)
    first = lax.dot_general(
        pick, x_ref[:, 0:128], (((1,), (1,)), ((), ())), preferred_element_type=jnp.float32
    )
    empty = jnp.where(first[0:1] > EMPTY_ABOVE, masked_score, 0.0)
    copy.wait()
    for j in range(0, 3 * HW, 256):
        part = jnp.dot(normed[...], w[:, j : j + 256], preferred_element_type=jnp.float32)
        qkv[:, j : j + 256] = part.astype(jnp.bfloat16)
    low = lax.broadcasted_iota(jnp.int32, (n, 128), 1) < HD
    for pair in range(HEADS // 2):
        at = pair * 128
        q = qkv[:, at : at + 128] * jnp.bfloat16(HD ** (-0.5))
        k = qkv[:, HW + at : HW + at + 128]
        v = qkv[:, 2 * HW + at : 2 * HW + at + 128]
        mixed = []
        for half in range(2):
            mine = low if half == 0 else jnp.logical_not(low)
            qh = jnp.where(mine, q, jnp.zeros_like(q))
            s = lax.dot_general(qh, k, (((1,), (1,)), ((), ())), preferred_element_type=jnp.float32)
            s = s + empty
            raised = jnp.exp(s - jnp.max(s, axis=-1, keepdims=True))
            weights = (raised * (1.0 / jnp.sum(raised, axis=-1, keepdims=True))).astype(jnp.bfloat16)
            mixed.append(jnp.dot(weights, v, preferred_element_type=jnp.float32))
        out_ref[:, at : at + 128] = jnp.where(low, mixed[0], mixed[1]).astype(jnp.bfloat16)


def window_kernel(
    own_ref, north_ref, south_ref, left_ref, right_ref, gain_ref, table_ref, index_ref, w_ref,
    out_ref, xs, xq, kv, qs, bias, scores, weights, wout, edges, w, sem,
):
    copy = pltpu.make_async_copy(w_ref, w, sem)
    copy.start()
    lat = lax.axis_index("lat")
    gain = gain_ref[...]

    lane = lax.broadcasted_iota(jnp.int32, (8, 128), 1)
    first = lane < WTOK
    key_row = (lane % WTOK) // WIN
    off_north = (lat == 0) & (key_row < HALF)
    off_south = (lat == lax.axis_size("lat") - 1) & (key_row >= HALF)
    tables = []
    for h in range(HEADS):
        tables.append([jnp.broadcast_to(table_ref[h : h + 1, c : c + 128], (8, 128)) for c in (0, 128)])
    for a in range(2):
        off = off_north if a == 0 else off_south
        for i in range(0, QROWS, 8):
            at = (QROWS if a == 0 else 0) + i
            idx = index_ref[at : at + 8, :]
            inner = idx & 127
            high = idx >= 128
            for h4 in range(4):
                found = []
                for h in (h4, h4 + 4):
                    lo = jnp.take_along_axis(tables[h][0], inner, axis=1)
                    hi = jnp.take_along_axis(tables[h][1], inner, axis=1)
                    found.append(jnp.where(high, hi, lo))
                value = jnp.where(first, found[0], found[1])
                to = a * 128 + h4 * QROWS + i
                bias[to : to + 8, :] = jnp.where(off, masked_score, value)

    for side, ref in enumerate((left_ref, right_ref)):
        for i in range(0, 64, 32):
            edges[side, i : i + 32] = norm_rows(ref[i : i + 32].astype(jnp.float32), gain)
    lower = lax.broadcasted_iota(jnp.int32, (8, D), 0) < HALF
    rows = [(north_ref, i) for i in range(HALF)] + [(own_ref, i) for i in range(RH)]
    rows += [(south_ref, i) for i in range(HALF)]
    for r in range(0, RH + WIN, 2):
        blocks = [[], []]
        for k in range(2):
            ref, i = rows[r + k]
            normed = norm_rows(ref[i].astype(jnp.float32), gain)
            turned = [pltpu.roll(normed[j * 8 : j * 8 + 8], HALF, 0) for j in range(4)]
            lo = edges[0, r * 4 : r * 4 + 8]
            hi = edges[1, r * 4 : r * 4 + 8]
            if k == 0:
                hi = pltpu.roll(hi, HALF, 0)
            else:
                lo = pltpu.roll(lo, HALF, 0)
            seq = [lo] + turned + [hi]
            blocks[k] = [jnp.where(lower, seq[b], seq[b + 1]) for b in range(WIN_B)]
        a, wr = r // WIN, r % WIN
        for b in range(WIN_B):
            both = jnp.concatenate([blocks[0][b], blocks[1][b]], 0).astype(jnp.bfloat16)
            to = (a * WIN_B + b) * WTOK + wr * WIN
            xs[to : to + 16] = both
            if (wr >= HALF) == (a == 0):
                to = (a * WIN_B + b) * QROWS + (wr % HALF) * WIN
                xq[to : to + 16] = both
    copy.wait()

    for j in range(0, HW, 256):
        part = jnp.dot(xq[...], w[:, j : j + 256], preferred_element_type=jnp.float32)
        qs[:, j : j + 256] = part.astype(jnp.bfloat16)
    for j in range(0, 2 * HW, 256):
        part = jnp.dot(xs[...], w[:, HW + j : HW + j + 256], preferred_element_type=jnp.float32)
        kv[:, j : j + 256] = part.astype(jnp.bfloat16)

    head = lax.broadcasted_iota(jnp.int32, (QROWS, HW), 1) // HD % 4
    blank = jnp.zeros((WTOK, HW // 2), jnp.bfloat16)

    def two_groups(x):
        top = jnp.concatenate([x[:, : HW // 2], blank], 1)
        low = jnp.concatenate([blank, x[:, HW // 2 :]], 1)
        return jnp.concatenate([top, low], 0)

    for n in range(N_WIN):
        q = qs[n * QROWS : n * QROWS + QROWS] * jnp.bfloat16(HD ** (-0.5))
        spread = jnp.concatenate([jnp.where(head == h, q, jnp.zeros_like(q)) for h in range(4)], 0)
        k = two_groups(kv[n * WTOK : n * WTOK + WTOK, 0:HW])
        s = lax.dot_general(spread, k, (((1,), (1,)), ((), ())), preferred_element_type=jnp.float32)
        a = n // WIN_B
        scores[n * 128 : n * 128 + 128] = s + bias[a * 128 : a * 128 + 128]
    left = lax.broadcasted_iota(jnp.int32, (128, 128), 1) < WTOK
    for n in range(N_WIN):
        s = scores[n * 128 : n * 128 + 128]
        top0 = jnp.max(jnp.where(left, s, -jnp.inf), axis=-1, keepdims=True)
        top1 = jnp.max(jnp.where(left, -jnp.inf, s), axis=-1, keepdims=True)
        raised = jnp.exp(s - jnp.where(left, top0, top1))
        sum0 = jnp.sum(jnp.where(left, raised, 0.0), axis=-1, keepdims=True)
        sum1 = jnp.sum(jnp.where(left, 0.0, raised), axis=-1, keepdims=True)
        share = jnp.where(left, 1.0 / sum0, 1.0 / sum1)
        weights[n * 128 : n * 128 + 128] = (raised * share).astype(jnp.bfloat16)
    for n in range(N_WIN):
        v = two_groups(kv[n * WTOK : n * WTOK + WTOK, HW : 2 * HW])
        o = jnp.dot(weights[n * 128 : n * 128 + 128], v, preferred_element_type=jnp.float32)
        total = o[0:QROWS]
        for h in range(1, 4):
            total = jnp.where(head == h, o[h * QROWS : h * QROWS + QROWS], total)
        wout[n] = total
    lower = lax.broadcasted_iota(jnp.int32, (8, HW), 0) < HALF
    for r in range(RH):
        a, wr = r // HALF, r % HALF
        turned = [
            pltpu.roll(wout[a * WIN_B + b, wr * WIN : wr * WIN + WIN], HALF, 0) for b in range(WIN_B)
        ]
        for j in range(4):
            to = r * RW + j * 8
            out_ref[to : to + 8] = jnp.where(lower, turned[j], turned[j + 1])


def join_kernel(win_ref, back_ref, undo_ref, out_ref):
    north = lax.axis_index("lat") == 0
    cap = jnp.dot(undo_ref[...], back_ref[...], preferred_element_type=jnp.float32)
    top = win_ref[0:CAP_TOKENS] + jnp.where(north, cap, 0.0)
    low = win_ref[CAP_TOKENS:] + jnp.where(north, 0.0, cap)
    out_ref[0:CAP_TOKENS] = top.astype(jnp.bfloat16)
    out_ref[CAP_TOKENS:] = low.astype(jnp.bfloat16)


def sds(shape, dtype):
    return jax.ShapeDtypeStruct(shape, dtype)


def call(kernel, name, outs, ins, out_specs, scratch, mib, flops, nbytes, trans=0):
    return pl.pallas_call(
        kernel,
        name=name,
        out_shape=outs,
        in_specs=ins,
        out_specs=out_specs,
        scratch_shapes=scratch,
        compiler_params=pltpu.CompilerParams(vmem_limit_bytes=mib << 20),
        cost_estimate=pl.CostEstimate(flops=flops, bytes_accessed=nbytes, transcendentals=trans),
    )


def exchange(block):
    return lax.all_to_all(block, "lon", split_axis=0, concat_axis=0, tiled=True)


def local(tokens, ln_gain, w_qkv, bias_table, bias_index, cap_group):
    lat_count = lax.axis_size("lat")
    lon_count = lax.axis_size("lon")
    bf16, f32 = jnp.bfloat16, jnp.float32
    gain = ln_gain.reshape(1, D)
    groups = cap_group.reshape(2, TILES_DEV)

    packed = call(
        pack_kernel, "pack", sds((SLOT_TOKENS, D), bf16),
        [sspec(), aspec()], vspec(),
        [VMEM((CAP, RW, D), bf16), pltpu.SemaphoreType.DMA],
        8, 2 * SLOT_TOKENS * CAP_TOKENS * D, 1 << 20,
    )(groups, tokens)
    arrived = exchange(packed.reshape(lon_count, MOST * TW, D)).reshape(SLOT_TOKENS, D)

    down = [(i, i + 1) for i in range(lat_count - 1)]
    up = [(i + 1, i) for i in range(lat_count - 1)]
    east = [(i, (i + 1) % lon_count) for i in range(lon_count)]
    west = [((i + 1) % lon_count, i) for i in range(lon_count)]
    tied, _ = lax.optimization_barrier((tokens, packed))
    north = lax.ppermute(tied[RH - HALF :], "lat", down)
    south = lax.ppermute(tied[:HALF], "lat", up)
    head, tail, undo = call(
        edge_kernel, "edges",
        (sds((64, D), bf16), sds((64, D), bf16), sds((CAP_TOKENS, SLOT_TOKENS), bf16)),
        [sspec(), vspec(), vspec(), vspec()], (vspec(), vspec(), vspec()), [],
        8, 1 << 20, 3 << 19,
    )(groups, tokens, north, south)
    left = lax.ppermute(tail, "lon", east)
    right = lax.ppermute(head, "lon", west)

    cap_result = call(
        cap_kernel, "caps", sds((SLOT_TOKENS, HW), bf16),
        [vspec(), vspec(), aspec()], vspec(),
        [VMEM((SLOT_TOKENS, D), bf16), VMEM((SLOT_TOKENS, 3 * HW), bf16), VMEM((D, 3 * HW), bf16), pltpu.SemaphoreType.DMA],
        20, 1100 << 20, 4 << 20, 1 << 19,
    )(arrived, gain, w_qkv)
    returned = exchange(cap_result.reshape(lon_count, MOST * TW, HW)).reshape(SLOT_TOKENS, HW)

    table = jnp.pad(bias_table, ((0, 0), (0, 256 - BIAS_ROWS)))
    index = jnp.concatenate([bias_index, bias_index], axis=1)
    own, _ = lax.optimization_barrier((tokens, cap_result))
    win_out = call(
        window_kernel, "windows", sds((RH * RW, HW), f32),
        [vspec()] * 8 + [aspec()], vspec(),
        [
            VMEM((N_WIN * WTOK, D), bf16),
            VMEM((N_WIN * QROWS, D), bf16),
            VMEM((N_WIN * WTOK, 2 * HW), bf16),
            VMEM((N_WIN * QROWS, HW), bf16),
            VMEM((2 * 128, 128), f32),
            VMEM((N_WIN * 128, 128), f32),
            VMEM((N_WIN * 128, 128), bf16),
            VMEM((N_WIN, QROWS, HW), f32),
            VMEM((2, 64, D), f32),
            VMEM((D, 3 * HW), bf16),
            pltpu.SemaphoreType.DMA,
        ],
        28, 2300 << 20, 6 << 20, 1 << 18,
    )(own, north, south, left, right, gain, table, index, w_qkv)
    mixed = call(
        join_kernel, "join", sds((RH * RW, HW), bf16),
        [vspec()] * 3, vspec(), [],
        8, 2 * CAP_TOKENS * SLOT_TOKENS * HW, 1 << 20,
    )(win_out, returned, undo)
    return mixed.reshape(RH, RW, HW)


def solution(mesh):
    placed = (P("lat", "lon", None), P(), P(), P(), P(), P(None, "lon", None, None))
    return jax.shard_map(
        local, mesh=mesh, in_specs=placed, out_specs=P("lat", "lon", None), check_vma=False
    )
```

```python
import jax
import jax.numpy as jnp
from jax import lax
from jax.experimental import pallas as pl
from jax.experimental.pallas import tpu as pltpu
from jax.sharding import PartitionSpec as P


D = 1024
HEADS = 8
HD = 64
WIN = 8
TW = 4
CAP = 4
RH = 8
RW = 32
HW = 512
HALF = 4
BIAS_ROWS = 225
TILES_DEV = 32
TILE_COLS = RW // TW
GROUPS = 32
MOST = 2
SLOT_TOKENS = GROUPS * MOST * TW
CAP_TOKENS = CAP * RW
N_WIN = 10
WIN_B = 5
WTOK = WIN * WIN
QROWS = HALF * WIN

epsilon = 1e-05
masked_score = -1e30
EMPTY = 128.0
EMPTY_ABOVE = 64.0

ALL_VMEM = 67043328
SOME_VMEM = 24 << 20

VMEM = pltpu.VMEM
SMEM = pltpu.SMEM


def vspec():
    return pl.BlockSpec(memory_space=VMEM)


def aspec():
    return pl.BlockSpec(memory_space=pl.ANY)


def hspec():
    return pl.BlockSpec(memory_space=pltpu.HBM)


def norm_rows(values, gain):
    center = jnp.mean(values, axis=-1, keepdims=True)
    shifted = values - center
    spread = jnp.mean(jnp.square(shifted), axis=-1, keepdims=True)
    return shifted * lax.rsqrt(spread + epsilon) * gain


def slot_rows(group_ref, pole, lane):
    tile = lane // TW
    names = [group_ref[pole, t // TILE_COLS, 0, t % TILE_COLS] for t in range(TILES_DEV)]
    group = jnp.zeros_like(lane)
    for t in range(TILES_DEV):
        group = jnp.where(tile == t, names[t], group)
    rank = jnp.zeros_like(lane)
    for t in range(TILES_DEV):
        same = (group == names[t]) & (tile > t)
        rank = rank + same.astype(jnp.int32)
    return (group * MOST + rank) * TW + lane % TW


PACK_STEP = 64


def pack_kernel(names_ref, tokens_ref, send_ref, group_ref, rows, out, name_sem, sem, out_sem):
    north = lax.axis_index("lat") == 0
    pole = jnp.where(north, 0, 1)
    start = jnp.where(north, 0, RH - CAP)
    names = pltpu.make_async_copy(names_ref, group_ref, name_sem)
    names.start()
    copy = pltpu.make_async_copy(tokens_ref.at[pl.ds(start, CAP)], rows, sem)
    copy.start()
    names.wait()
    lane = lax.broadcasted_iota(jnp.int32, (8, CAP_TOKENS), 1)
    slot = slot_rows(group_ref, pole, lane)[0:1]
    copy.wait()
    x = rows[...].reshape(CAP_TOKENS, D)
    sends = []
    for n in range(SLOT_TOKENS // PACK_STEP):
        at = pl.ds(n * PACK_STEP, PACK_STEP)
        hit = lax.broadcasted_iota(jnp.int32, (PACK_STEP, CAP_TOKENS), 0) + n * PACK_STEP == slot
        hot = hit.astype(jnp.float32)
        filled = jnp.max(hot, axis=1, keepdims=True) > 0.5
        moved = jnp.dot(hot.astype(jnp.bfloat16), x, preferred_element_type=jnp.float32)
        out[at, :] = jnp.where(filled, moved, EMPTY).astype(jnp.bfloat16)
        sends.append(pltpu.make_async_copy(out.at[at], send_ref.at[at], out_sem.at[n]))
        sends[n].start()
    for send in sends:
        send.wait()


def edge_kernel(own_ref, head_ref, tail_ref):
    lower = lax.broadcasted_iota(jnp.int32, (8, D), 0) < HALF
    for r in range(0, RH, 4):
        heads, tails = [], []
        for i in (r, r + 2):
            first = [own_ref[i + k, 0:8].astype(jnp.float32) for k in range(2)]
            last = [own_ref[i + k, 24:32].astype(jnp.float32) for k in range(2)]
            heads.append(jnp.where(lower, first[0], pltpu.roll(first[1], HALF, 0)))
            tails.append(jnp.where(lower, pltpu.roll(last[0], HALF, 0), last[1]))
        head_ref[r * 4 : r * 4 + 16] = jnp.concatenate(heads, 0).astype(jnp.bfloat16)
        tail_ref[r * 4 : r * 4 + 16] = jnp.concatenate(tails, 0).astype(jnp.bfloat16)


def undo_kernel(names_ref, undo_ref, group_ref, name_sem):
    names = pltpu.make_async_copy(names_ref, group_ref, name_sem)
    names.start()
    lat = lax.axis_index("lat")
    north = lat == 0
    polar = north | (lat == lax.axis_size("lat") - 1)
    pole = jnp.where(north, 0, 1)
    token = lax.broadcasted_iota(jnp.int32, (CAP_TOKENS, 128), 0)
    names.wait()
    slot = slot_rows(group_ref, pole, token)
    slot = jnp.where(polar, slot, -1)
    for i in range(0, SLOT_TOKENS, 128):
        hit = lax.broadcasted_iota(jnp.int32, (CAP_TOKENS, 128), 1) + i == slot
        undo_ref[:, i : i + 128] = hit.astype(jnp.float32).astype(jnp.bfloat16)


RIM_SIDE = HALF * HALF
RIM = HALF * RW + 2 * RIM_SIDE


def rim_kernel(own_ref, left_ref, right_ref, up_ref, down_ref, sem):
    copies = []
    for n, (out, first) in enumerate(((up_ref, 0), (down_ref, RH - HALF))):
        for r in range(HALF):
            at = pl.ds(r * RW, RW)
            copies.append(pltpu.make_async_copy(own_ref.at[first + r], out.at[at], sem.at[n * 6 + r]))
        for k, side in enumerate((left_ref, right_ref)):
            at = pl.ds(HALF * RW + k * RIM_SIDE, RIM_SIDE)
            part = side.at[pl.ds(first * HALF, RIM_SIDE)]
            copies.append(pltpu.make_async_copy(part, out.at[at], sem.at[n * 6 + 4 + k]))
    for copy in copies:
        copy.start()
    for copy in copies:
        copy.wait()


W_STEP = 256


def cap_norm_kernel(x_ref, gain_ref, normed, empty_ref):
    gain = gain_ref[...]
    for i in range(0, SLOT_TOKENS, 32):
        normed[i : i + 32] = norm_rows(x_ref[i : i + 32].astype(jnp.float32), gain).astype(jnp.bfloat16)
    pick = (lax.broadcasted_iota(jnp.int32, (8, 128), 1) == 0).astype(jnp.bfloat16)
    first = lax.dot_general(
        pick, x_ref[:, 0:128], (((1,), (1,)), ((), ())), preferred_element_type=jnp.float32
    )
    empty_ref[...] = jnp.where(first > EMPTY_ABOVE, masked_score, 0.0)


def cap_kernel(normed, empty_ref, w_ref, out_ref, qkv):
    n = SLOT_TOKENS
    empty = empty_ref[0:1]
    for j in range(0, 3 * HW, W_STEP):
        w = w_ref[:, j : j + W_STEP]
        part = jnp.dot(normed[...], w, preferred_element_type=jnp.float32)
        qkv[:, j : j + W_STEP] = part.astype(jnp.bfloat16)
    low = lax.broadcasted_iota(jnp.int32, (n, 128), 1) < HD
    for pair in range(HEADS // 2):
        at = pair * 128
        q = qkv[:, at : at + 128] * jnp.bfloat16(HD ** (-0.5))
        k = qkv[:, HW + at : HW + at + 128]
        v = qkv[:, 2 * HW + at : 2 * HW + at + 128]
        mixed = []
        for half in range(2):
            mine = low if half == 0 else jnp.logical_not(low)
            qh = jnp.where(mine, q, jnp.zeros_like(q))
            s = lax.dot_general(qh, k, (((1,), (1,)), ((), ())), preferred_element_type=jnp.float32)
            s = s + empty
            raised = jnp.exp(s - jnp.max(s, axis=-1, keepdims=True))
            weights = (raised * (1.0 / jnp.sum(raised, axis=-1, keepdims=True))).astype(jnp.bfloat16)
            mixed.append(jnp.dot(weights, v, preferred_element_type=jnp.float32))
        out_ref[:, at : at + 128] = jnp.where(low, mixed[0], mixed[1]).astype(jnp.bfloat16)


def bias_kernel(table_ref, index_ref, bias_ref):
    lat = lax.axis_index("lat")
    lane = lax.broadcasted_iota(jnp.int32, (8, 128), 1)
    first = lane < WTOK
    key_row = (lane % WTOK) // WIN
    off_north = (lat == 0) & (key_row < HALF)
    off_south = (lat == lax.axis_size("lat") - 1) & (key_row >= HALF)
    tables = []
    for h in range(HEADS):
        parts = [table_ref[h : h + 1, c : c + 128] for c in (0, BIAS_ROWS - 128)]
        tables.append([jnp.broadcast_to(part, (8, 128)) for part in parts])
    for a in range(2):
        off = off_north if a == 0 else off_south
        for i in range(0, QROWS, 8):
            at = (QROWS if a == 0 else 0) + i
            idx = index_ref[at : at + 8, :]
            idx = jnp.concatenate([idx, idx], axis=1)
            high = idx >= 128
            inner = jnp.where(high, idx - (BIAS_ROWS - 128), idx)
            for h4 in range(4):
                found = []
                for h in (h4, h4 + 4):
                    lo = jnp.take_along_axis(tables[h][0], inner, axis=1)
                    hi = jnp.take_along_axis(tables[h][1], inner, axis=1)
                    found.append(jnp.where(high, hi, lo))
                value = jnp.where(first, found[0], found[1])
                to = a * 128 + h4 * QROWS + i
                bias_ref[to : to + 8, :] = jnp.where(off, masked_score, value)


def window_kernel(
    own_ref, north_ref, south_ref, left_ref, right_ref, gain_ref, bias, w_ref,
    out_ref, xs, xq, kv, qs, scores, weights, wout, edges,
):
    gain = gain_ref[...]

    for side, ref in enumerate((left_ref, right_ref)):
        at = HALF * RW + side * RIM_SIDE
        for to, x in (
            (0, north_ref[at : at + RIM_SIDE]),
            (RIM_SIDE, ref[...]),
            (3 * RIM_SIDE, south_ref[at : at + RIM_SIDE]),
        ):
            edges[side, to : to + x.shape[0]] = norm_rows(x.astype(jnp.float32), gain)
    lower = lax.broadcasted_iota(jnp.int32, (8, D), 0) < HALF
    rows = [(north_ref, i) for i in range(HALF)] + [(own_ref, i) for i in range(RH)]
    rows += [(south_ref, i) for i in range(HALF)]
    for r in range(0, RH + WIN, 2):
        blocks = [[], []]
        for k in range(2):
            ref, i = rows[r + k]
            x = ref[i] if ref is own_ref else ref[i * RW : i * RW + RW]
            normed = norm_rows(x.astype(jnp.float32), gain)
            turned = [pltpu.roll(normed[j * 8 : j * 8 + 8], HALF, 0) for j in range(4)]
            lo = edges[0, r * 4 : r * 4 + 8]
            hi = edges[1, r * 4 : r * 4 + 8]
            if k == 0:
                hi = pltpu.roll(hi, HALF, 0)
            else:
                lo = pltpu.roll(lo, HALF, 0)
            seq = [lo] + turned + [hi]
            blocks[k] = [jnp.where(lower, seq[b], seq[b + 1]) for b in range(WIN_B)]
        a, wr = r // WIN, r % WIN
        for b in range(WIN_B):
            both = jnp.concatenate([blocks[0][b], blocks[1][b]], 0).astype(jnp.bfloat16)
            to = (a * WIN_B + b) * WTOK + wr * WIN
            xs[to : to + 16] = both
            if (wr >= HALF) == (a == 0):
                to = (a * WIN_B + b) * QROWS + (wr % HALF) * WIN
                xq[to : to + 16] = both

    for j in range(0, 3 * HW, W_STEP):
        w = w_ref[:, j : j + W_STEP]
        if j < HW:
            qs[:, j : j + W_STEP] = jnp.dot(xq[...], w, preferred_element_type=jnp.float32).astype(jnp.bfloat16)
        else:
            part = jnp.dot(xs[...], w, preferred_element_type=jnp.float32)
            kv[:, j - HW : j - HW + W_STEP] = part.astype(jnp.bfloat16)

    head = lax.broadcasted_iota(jnp.int32, (QROWS, HW), 1) // HD % 4
    blank = jnp.zeros((WTOK, HW // 2), jnp.bfloat16)

    def two_groups(x):
        top = jnp.concatenate([x[:, : HW // 2], blank], 1)
        low = jnp.concatenate([blank, x[:, HW // 2 :]], 1)
        return jnp.concatenate([top, low], 0)

    for n in range(N_WIN):
        q = qs[n * QROWS : n * QROWS + QROWS] * jnp.bfloat16(HD ** (-0.5))
        spread = jnp.concatenate([jnp.where(head == h, q, jnp.zeros_like(q)) for h in range(4)], 0)
        k = two_groups(kv[n * WTOK : n * WTOK + WTOK, 0:HW])
        s = lax.dot_general(spread, k, (((1,), (1,)), ((), ())), preferred_element_type=jnp.float32)
        a = n // WIN_B
        scores[n * 128 : n * 128 + 128] = s + bias[a * 128 : a * 128 + 128]
    left = lax.broadcasted_iota(jnp.int32, (128, 128), 1) < WTOK
    for n in range(N_WIN):
        s = scores[n * 128 : n * 128 + 128]
        top0 = jnp.max(jnp.where(left, s, -jnp.inf), axis=-1, keepdims=True)
        top1 = jnp.max(jnp.where(left, -jnp.inf, s), axis=-1, keepdims=True)
        raised = jnp.exp(s - jnp.where(left, top0, top1))
        sum0 = jnp.sum(jnp.where(left, raised, 0.0), axis=-1, keepdims=True)
        sum1 = jnp.sum(jnp.where(left, 0.0, raised), axis=-1, keepdims=True)
        share = jnp.where(left, 1.0 / sum0, 1.0 / sum1)
        weights[n * 128 : n * 128 + 128] = (raised * share).astype(jnp.bfloat16)
    for n in range(N_WIN):
        v = two_groups(kv[n * WTOK : n * WTOK + WTOK, HW : 2 * HW])
        o = jnp.dot(weights[n * 128 : n * 128 + 128], v, preferred_element_type=jnp.float32)
        total = o[0:QROWS]
        for h in range(1, 4):
            total = jnp.where(head == h, o[h * QROWS : h * QROWS + QROWS], total)
        wout[n] = total
    lower = lax.broadcasted_iota(jnp.int32, (8, HW), 0) < HALF
    for r in range(RH):
        a, wr = r // HALF, r % HALF
        turned = [
            pltpu.roll(wout[a * WIN_B + b, wr * WIN : wr * WIN + WIN], HALF, 0) for b in range(WIN_B)
        ]
        for j in range(4):
            to = r * RW + j * 8
            out_ref[to : to + 8] = jnp.where(lower, turned[j], turned[j + 1])


def join_kernel(win_ref, back_ref, undo_ref, out_ref):
    north = lax.axis_index("lat") == 0
    cap = jnp.dot(undo_ref[...], back_ref[...], preferred_element_type=jnp.float32)
    top = win_ref[0:CAP_TOKENS] + jnp.where(north, cap, 0.0)
    low = win_ref[CAP_TOKENS:] + jnp.where(north, 0.0, cap)
    out_ref[0:CAP_TOKENS] = top.astype(jnp.bfloat16)
    out_ref[CAP_TOKENS:] = low.astype(jnp.bfloat16)


def sds(shape, dtype):
    return jax.ShapeDtypeStruct(shape, dtype)


def call(kernel, outs, ins, out_specs, scratch, vmem, flops, nbytes, trans=0):
    return pl.pallas_call(
        kernel,
        out_shape=outs,
        in_specs=ins,
        out_specs=out_specs,
        scratch_shapes=scratch,
        compiler_params=pltpu.CompilerParams(vmem_limit_bytes=vmem),
        cost_estimate=pl.CostEstimate(flops=flops, bytes_accessed=nbytes, transcendentals=trans),
    )


def exchange(block):
    return lax.all_to_all(block, "lon", split_axis=0, concat_axis=0, tiled=True)


def layer(tokens, ln_gain, w_qkv, bias_table, bias_index, cap_group):
    lat_count = lax.axis_size("lat")
    lon_count = lax.axis_size("lon")
    bf16, f32 = jnp.bfloat16, jnp.float32
    gain = ln_gain.reshape(1, D)
    groups = cap_group.transpose(0, 2, 3, 1)

    packed = call(
        pack_kernel, sds((SLOT_TOKENS, D), bf16),
        [aspec(), hspec()], hspec(),
        [
            SMEM((2, CAP, 1, TILE_COLS), jnp.int32),
            VMEM((CAP, RW, D), bf16),
            VMEM((SLOT_TOKENS, D), bf16),
            pltpu.SemaphoreType.DMA,
            pltpu.SemaphoreType.DMA,
            pltpu.SemaphoreType.DMA((SLOT_TOKENS // PACK_STEP,)),
        ],
        ALL_VMEM, 2 * SLOT_TOKENS * CAP_TOKENS * D, 1 << 20,
    )(groups, tokens)
    arrived = exchange(packed.reshape(lon_count, MOST * TW, D)).reshape(SLOT_TOKENS, D)

    down = [(i, i + 1) for i in range(lat_count - 1)]
    up = [(i + 1, i) for i in range(lat_count - 1)]
    east = [(i, (i + 1) % lon_count) for i in range(lon_count)]
    west = [((i + 1) % lon_count, i) for i in range(lon_count)]
    side = sds((RH * HALF, D), bf16)
    head, tail = call(
        edge_kernel, (side, side), [vspec()], (vspec(), vspec()), [],
        SOME_VMEM, 1 << 18, 3 << 18,
    )(tokens)
    left = lax.ppermute(tail, "lon", east)
    right = lax.ppermute(head, "lon", west)
    undo = call(
        undo_kernel, sds((CAP_TOKENS, SLOT_TOKENS), bf16), [aspec()], vspec(),
        [SMEM((2, CAP, 1, TILE_COLS), jnp.int32), pltpu.SemaphoreType.DMA],
        SOME_VMEM, 1 << 18, 1 << 16,
    )(groups)
    rim = sds((RIM, D), bf16)
    to_north, to_south = call(
        rim_kernel, (rim, rim), [aspec(), aspec(), aspec()], (vspec(), vspec()),
        [pltpu.SemaphoreType.DMA((12,))],
        SOME_VMEM, 1 << 10, 3 << 19,
    )(tokens, left, right)
    north = lax.ppermute(to_south, "lat", down)
    south = lax.ppermute(to_north, "lat", up)

    bias = call(
        bias_kernel, sds((2 * 128, 128), f32),
        [vspec(), vspec()], vspec(), [],
        SOME_VMEM, 1 << 18, 1 << 18,
    )(bias_table, bias_index)

    normed, empty = call(
        cap_norm_kernel, (sds((SLOT_TOKENS, D), bf16), sds((8, SLOT_TOKENS), f32)),
        [vspec()] * 2, (vspec(), vspec()), [],
        SOME_VMEM, 8 << 20, 3 << 20,
    )(arrived, gain)
    cap_result = call(
        cap_kernel, sds((SLOT_TOKENS, HW), bf16),
        [vspec()] * 3, vspec(), [VMEM((SLOT_TOKENS, 3 * HW), bf16)],
        SOME_VMEM, 1100 << 20, 4 << 20, 1 << 19,
    )(normed, empty, w_qkv)
    returned = exchange(cap_result.reshape(lon_count, MOST * TW, HW)).reshape(SLOT_TOKENS, HW)

    win_out = call(
        window_kernel, sds((RH * RW, HW), f32),
        [vspec()] * 8, vspec(),
        [
            VMEM((N_WIN * WTOK, D), bf16),
            VMEM((N_WIN * QROWS, D), bf16),
            VMEM((N_WIN * WTOK, 2 * HW), bf16),
            VMEM((N_WIN * QROWS, HW), bf16),
            VMEM((N_WIN * 128, 128), f32),
            VMEM((N_WIN * 128, 128), bf16),
            VMEM((N_WIN, QROWS, HW), f32),
            VMEM((2, 64, D), f32),
        ],
        SOME_VMEM, 2300 << 20, 6 << 20, 1 << 18,
    )(tokens, north, south, left, right, gain, bias, w_qkv)
    mixed = call(
        join_kernel, sds((RH * RW, HW), bf16),
        [vspec()] * 3, vspec(), [],
        8 << 20, 2 * CAP_TOKENS * SLOT_TOKENS * HW, 1 << 20,
    )(win_out, returned, undo)
    return mixed.reshape(RH, RW, HW)


def solution(mesh):
    placed = (P("lat", "lon", None), P(), P(), P(), P(), P(None, "lon", None, None))
    return jax.shard_map(
        layer, mesh=mesh, in_specs=placed, out_specs=P("lat", "lon", None), check_vma=False
    )
```

```python
import jax
import jax.numpy as jnp
from jax import lax
from jax.experimental import pallas as pl
from jax.experimental.pallas import tpu as pltpu
from jax.sharding import PartitionSpec as P


D = 1024
HEADS = 8
HD = 64
WIN = 8
TW = 4
CAP = 4
RH = 8
RW = 32
HW = 512
HALF = 4
BIAS_ROWS = 225
TILES_DEV = 32
TILE_COLS = RW // TW
GROUPS = 32
MOST = 2
SLOT_TOKENS = GROUPS * MOST * TW
CAP_TOKENS = CAP * RW
N_WIN = 10
WIN_B = 5
WTOK = WIN * WIN
QROWS = HALF * WIN

epsilon = 1e-05
masked_score = -1e30
EMPTY = 128.0
EMPTY_ABOVE = 64.0

ALL_VMEM = 67043328
PACK_VMEM = ALL_VMEM - 409600
SOME_VMEM = 24 << 20

VMEM = pltpu.VMEM
SMEM = pltpu.SMEM


def vspec():
    return pl.BlockSpec(memory_space=VMEM)


def aspec():
    return pl.BlockSpec(memory_space=pl.ANY)


def hspec():
    return pl.BlockSpec(memory_space=pltpu.HBM)


def norm_rows(values, gain):
    center = jnp.mean(values, axis=-1, keepdims=True)
    shifted = values - center
    spread = jnp.mean(jnp.square(shifted), axis=-1, keepdims=True)
    return shifted * lax.rsqrt(spread + epsilon) * gain


def slot_rows(group_ref, pole, lane):
    tile = lane // TW
    names = [group_ref[pole, t // TILE_COLS, 0, t % TILE_COLS] for t in range(TILES_DEV)]
    group = jnp.zeros_like(lane)
    for t in range(TILES_DEV):
        group = jnp.where(tile == t, names[t], group)
    rank = jnp.zeros_like(lane)
    for t in range(TILES_DEV):
        same = (group == names[t]) & (tile > t)
        rank = rank + same.astype(jnp.int32)
    return (group * MOST + rank) * TW + lane % TW


PACK_STEP = 64


def pack_kernel(
    names_ref, tokens_ref, send_ref, hot_ref, head_ref, tail_ref,
    group_ref, rows, edge, out, name_sem, sem, edge_sem, out_sem,
):
    north = lax.axis_index("lat") == 0
    pole = jnp.where(north, 0, 1)
    start = jnp.where(north, 0, RH - CAP)
    names = pltpu.make_async_copy(names_ref, group_ref, name_sem)
    names.start()
    copy = pltpu.make_async_copy(tokens_ref.at[pl.ds(start, CAP)], rows, sem)
    copy.start()
    edges = [
        pltpu.make_async_copy(tokens_ref.at[:, pl.ds(k * (RW - 8), 8)], edge.at[k], edge_sem.at[k])
        for k in range(2)
    ]
    for each in edges:
        each.start()
    names.wait()
    lane = lax.broadcasted_iota(jnp.int32, (8, CAP_TOKENS), 1)
    slot = slot_rows(group_ref, pole, lane)[0:1]
    copy.wait()
    x = rows[...].reshape(CAP_TOKENS, D)
    sends = []
    for n in range(SLOT_TOKENS // PACK_STEP):
        at = pl.ds(n * PACK_STEP, PACK_STEP)
        hit = lax.broadcasted_iota(jnp.int32, (PACK_STEP, CAP_TOKENS), 0) + n * PACK_STEP == slot
        hot = hit.astype(jnp.float32)
        filled = jnp.max(hot, axis=1, keepdims=True) > 0.5
        hot = hot.astype(jnp.bfloat16)
        hot_ref[at, :] = hot
        moved = jnp.dot(hot, x, preferred_element_type=jnp.float32)
        out[at, :] = jnp.where(filled, moved, EMPTY).astype(jnp.bfloat16)
        sends.append(pltpu.make_async_copy(out.at[at], send_ref.at[at], out_sem.at[n]))
        sends[n].start()
    for each in edges:
        each.wait()
    lower = lax.broadcasted_iota(jnp.int32, (8, D), 0) < HALF
    for r in range(0, RH, 4):
        heads, tails = [], []
        for i in (r, r + 2):
            first = [edge[0, i + k].astype(jnp.float32) for k in range(2)]
            last = [edge[1, i + k].astype(jnp.float32) for k in range(2)]
            heads.append(jnp.where(lower, first[0], pltpu.roll(first[1], HALF, 0)))
            tails.append(jnp.where(lower, pltpu.roll(last[0], HALF, 0), last[1]))
        head_ref[r * 4 : r * 4 + 16] = jnp.concatenate(heads, 0).astype(jnp.bfloat16)
        tail_ref[r * 4 : r * 4 + 16] = jnp.concatenate(tails, 0).astype(jnp.bfloat16)
    for send in sends:
        send.wait()


RIM_SIDE = HALF * HALF
RIM = HALF * RW + 2 * RIM_SIDE


def row_kernel(own_ref, gain_in, up_ref, down_ref, gain_ref):
    gain_ref[...] = gain_in[...]
    for out, first in ((up_ref, 0), (down_ref, RH - HALF)):
        for r in range(HALF):
            out[r * RW : r * RW + RW] = own_ref[first + r]


def rim_kernel(left_ref, right_ref, up_in, down_in, up_ref, down_ref):
    for out, first in ((up_ref, 0), (down_ref, RH - HALF)):
        for k, side in enumerate((left_ref, right_ref)):
            at = HALF * RW + k * RIM_SIDE
            out[at : at + RIM_SIDE] = side[first * HALF : first * HALF + RIM_SIDE]


W_STEP = 256


def cap_kernel(x_ref, gain_ref, w_ref, out_ref, normed, qkv):
    n = SLOT_TOKENS
    gain = gain_ref[...]
    for i in range(0, n, 32):
        normed[i : i + 32] = norm_rows(x_ref[i : i + 32].astype(jnp.float32), gain).astype(jnp.bfloat16)
    pick = (lax.broadcasted_iota(jnp.int32, (8, 128), 1) == 0).astype(jnp.bfloat16)
    first = lax.dot_general(
        pick, x_ref[:, 0:128], (((1,), (1,)), ((), ())), preferred_element_type=jnp.float32
    )
    empty = jnp.where(first[0:1] > EMPTY_ABOVE, masked_score, 0.0)
    for j in range(3 * HW // W_STEP):
        at = slice(j * W_STEP, j * W_STEP + W_STEP)
        part = jnp.dot(normed[...], w_ref[:, at], preferred_element_type=jnp.float32)
        qkv[:, at] = part.astype(jnp.bfloat16)
    low = lax.broadcasted_iota(jnp.int32, (n, 128), 1) < HD
    for pair in range(HEADS // 2):
        at = pair * 128
        q = qkv[:, at : at + 128] * jnp.bfloat16(HD ** (-0.5))
        k = qkv[:, HW + at : HW + at + 128]
        v = qkv[:, 2 * HW + at : 2 * HW + at + 128]
        mixed = []
        for half in range(2):
            mine = low if half == 0 else jnp.logical_not(low)
            qh = jnp.where(mine, q, jnp.zeros_like(q))
            s = lax.dot_general(qh, k, (((1,), (1,)), ((), ())), preferred_element_type=jnp.float32)
            s = s + empty
            raised = jnp.exp(s - jnp.max(s, axis=-1, keepdims=True))
            weights = (raised * (1.0 / jnp.sum(raised, axis=-1, keepdims=True))).astype(jnp.bfloat16)
            mixed.append(jnp.dot(weights, v, preferred_element_type=jnp.float32))
        out_ref[:, at : at + 128] = jnp.where(low, mixed[0], mixed[1]).astype(jnp.bfloat16)


def window_kernel(
    own_ref, north_ref, south_ref, left_ref, right_ref, gain_ref, table_ref, index_ref, hot_ref, w_ref,
    out_ref, undo_ref, xs, xq, kv, qs, bias, scores, weights, wout, edges,
):
    gain = gain_ref[...]
    lat = lax.axis_index("lat")

    polar = (lat == 0) | (lat == lax.axis_size("lat") - 1)
    undo = jnp.transpose(hot_ref[...].astype(jnp.float32))
    undo_ref[...] = jnp.where(polar, undo, 0.0).astype(jnp.bfloat16)

    lane = lax.broadcasted_iota(jnp.int32, (8, 128), 1)
    first = lane < WTOK
    key_row = (lane % WTOK) // WIN
    off_north = (lat == 0) & (key_row < HALF)
    off_south = (lat == lax.axis_size("lat") - 1) & (key_row >= HALF)
    tables = []
    for h in range(HEADS):
        parts = [table_ref[h : h + 1, c : c + 128] for c in (0, BIAS_ROWS - 128)]
        tables.append([jnp.broadcast_to(part, (8, 128)) for part in parts])
    for a in range(2):
        off = off_north if a == 0 else off_south
        for i in range(0, QROWS, 8):
            at = (QROWS if a == 0 else 0) + i
            idx = index_ref[at : at + 8, :]
            idx = jnp.concatenate([idx, idx], axis=1)
            high = idx >= 128
            inner = jnp.where(high, idx - (BIAS_ROWS - 128), idx)
            for h4 in range(4):
                found = []
                for h in (h4, h4 + 4):
                    lo = jnp.take_along_axis(tables[h][0], inner, axis=1)
                    hi = jnp.take_along_axis(tables[h][1], inner, axis=1)
                    found.append(jnp.where(high, hi, lo))
                value = jnp.where(first, found[0], found[1])
                to = a * 128 + h4 * QROWS + i
                bias[to : to + 8, :] = jnp.where(off, masked_score, value)

    for side, ref in enumerate((left_ref, right_ref)):
        at = HALF * RW + side * RIM_SIDE
        for to, x in (
            (0, north_ref[at : at + RIM_SIDE]),
            (RIM_SIDE, ref[...]),
            (3 * RIM_SIDE, south_ref[at : at + RIM_SIDE]),
        ):
            edges[side, to : to + x.shape[0]] = norm_rows(x.astype(jnp.float32), gain)
    lower = lax.broadcasted_iota(jnp.int32, (8, D), 0) < HALF
    rows = [(north_ref, i) for i in range(HALF)] + [(own_ref, i) for i in range(RH)]
    rows += [(south_ref, i) for i in range(HALF)]
    for r in range(0, RH + WIN, 2):
        blocks = [[], []]
        for k in range(2):
            ref, i = rows[r + k]
            x = ref[i] if ref is own_ref else ref[i * RW : i * RW + RW]
            normed = norm_rows(x.astype(jnp.float32), gain)
            turned = [pltpu.roll(normed[j * 8 : j * 8 + 8], HALF, 0) for j in range(4)]
            lo = edges[0, r * 4 : r * 4 + 8]
            hi = edges[1, r * 4 : r * 4 + 8]
            if k == 0:
                hi = pltpu.roll(hi, HALF, 0)
            else:
                lo = pltpu.roll(lo, HALF, 0)
            seq = [lo] + turned + [hi]
            blocks[k] = [jnp.where(lower, seq[b], seq[b + 1]) for b in range(WIN_B)]
        a, wr = r // WIN, r % WIN
        for b in range(WIN_B):
            both = jnp.concatenate([blocks[0][b], blocks[1][b]], 0).astype(jnp.bfloat16)
            to = (a * WIN_B + b) * WTOK + wr * WIN
            xs[to : to + 16] = both
            if (wr >= HALF) == (a == 0):
                to = (a * WIN_B + b) * QROWS + (wr % HALF) * WIN
                xq[to : to + 16] = both

    for j in range(3 * HW // W_STEP):
        at = slice(j * W_STEP, j * W_STEP + W_STEP)
        if j * W_STEP < HW:
            qs[:, at] = jnp.dot(xq[...], w_ref[:, at], preferred_element_type=jnp.float32).astype(jnp.bfloat16)
        else:
            to = slice(j * W_STEP - HW, j * W_STEP - HW + W_STEP)
            kv[:, to] = jnp.dot(xs[...], w_ref[:, at], preferred_element_type=jnp.float32).astype(jnp.bfloat16)

    head = lax.broadcasted_iota(jnp.int32, (QROWS, HW), 1) // HD % 4
    blank = jnp.zeros((WTOK, HW // 2), jnp.bfloat16)

    def two_groups(x):
        top = jnp.concatenate([x[:, : HW // 2], blank], 1)
        low = jnp.concatenate([blank, x[:, HW // 2 :]], 1)
        return jnp.concatenate([top, low], 0)

    for n in range(N_WIN):
        q = qs[n * QROWS : n * QROWS + QROWS] * jnp.bfloat16(HD ** (-0.5))
        spread = jnp.concatenate([jnp.where(head == h, q, jnp.zeros_like(q)) for h in range(4)], 0)
        k = two_groups(kv[n * WTOK : n * WTOK + WTOK, 0:HW])
        s = lax.dot_general(spread, k, (((1,), (1,)), ((), ())), preferred_element_type=jnp.float32)
        a = n // WIN_B
        scores[n * 128 : n * 128 + 128] = s + bias[a * 128 : a * 128 + 128]
    left = lax.broadcasted_iota(jnp.int32, (128, 128), 1) < WTOK
    for n in range(N_WIN):
        s = scores[n * 128 : n * 128 + 128]
        top0 = jnp.max(jnp.where(left, s, -jnp.inf), axis=-1, keepdims=True)
        top1 = jnp.max(jnp.where(left, -jnp.inf, s), axis=-1, keepdims=True)
        raised = jnp.exp(s - jnp.where(left, top0, top1))
        sum0 = jnp.sum(jnp.where(left, raised, 0.0), axis=-1, keepdims=True)
        sum1 = jnp.sum(jnp.where(left, 0.0, raised), axis=-1, keepdims=True)
        share = jnp.where(left, 1.0 / sum0, 1.0 / sum1)
        weights[n * 128 : n * 128 + 128] = (raised * share).astype(jnp.bfloat16)
    for n in range(N_WIN):
        v = two_groups(kv[n * WTOK : n * WTOK + WTOK, HW : 2 * HW])
        o = jnp.dot(weights[n * 128 : n * 128 + 128], v, preferred_element_type=jnp.float32)
        total = o[0:QROWS]
        for h in range(1, 4):
            total = jnp.where(head == h, o[h * QROWS : h * QROWS + QROWS], total)
        wout[n] = total
    lower = lax.broadcasted_iota(jnp.int32, (8, HW), 0) < HALF
    for r in range(RH):
        a, wr = r // HALF, r % HALF
        turned = [
            pltpu.roll(wout[a * WIN_B + b, wr * WIN : wr * WIN + WIN], HALF, 0) for b in range(WIN_B)
        ]
        for j in range(4):
            to = r * RW + j * 8
            out_ref[to : to + 8] = jnp.where(lower, turned[j], turned[j + 1])


def join_kernel(win_ref, back_ref, undo_ref, out_ref):
    north = lax.axis_index("lat") == 0
    cap = jnp.dot(undo_ref[...], back_ref[...], preferred_element_type=jnp.float32)
    top = win_ref[0:CAP_TOKENS] + jnp.where(north, cap, 0.0)
    low = win_ref[CAP_TOKENS:] + jnp.where(north, 0.0, cap)
    out_ref[0:CAP_TOKENS] = top.astype(jnp.bfloat16)
    out_ref[CAP_TOKENS:] = low.astype(jnp.bfloat16)


def sds(shape, dtype):
    return jax.ShapeDtypeStruct(shape, dtype)


def call(kernel, outs, ins, out_specs, scratch, vmem, flops, nbytes, trans=0, aliases=None):
    return pl.pallas_call(
        kernel,
        out_shape=outs,
        in_specs=ins,
        out_specs=out_specs,
        scratch_shapes=scratch,
        compiler_params=pltpu.CompilerParams(vmem_limit_bytes=vmem),
        input_output_aliases=aliases or {},
        cost_estimate=pl.CostEstimate(flops=flops, bytes_accessed=nbytes, transcendentals=trans),
    )


def exchange(block):
    return lax.all_to_all(block, "lon", split_axis=0, concat_axis=0, tiled=True)


def layer(tokens, ln_gain, w_qkv, bias_table, bias_index, cap_group):
    lat_count = lax.axis_size("lat")
    lon_count = lax.axis_size("lon")
    bf16, f32 = jnp.bfloat16, jnp.float32
    gain = ln_gain.reshape(1, D)
    groups = cap_group.transpose(0, 2, 3, 1)

    side = sds((RH * HALF, D), bf16)
    packed, hot, head, tail = call(
        pack_kernel,
        (sds((SLOT_TOKENS, D), bf16), sds((SLOT_TOKENS, CAP_TOKENS), bf16), side, side),
        [aspec(), hspec()], (hspec(),) + (vspec(),) * 3,
        [
            SMEM((2, CAP, 1, TILE_COLS), jnp.int32),
            VMEM((CAP, RW, D), bf16),
            VMEM((2, RH, 8, D), bf16),
            VMEM((SLOT_TOKENS, D), bf16),
            pltpu.SemaphoreType.DMA,
            pltpu.SemaphoreType.DMA,
            pltpu.SemaphoreType.DMA((2,)),
            pltpu.SemaphoreType.DMA((SLOT_TOKENS // PACK_STEP,)),
        ],
        PACK_VMEM, 2 * SLOT_TOKENS * CAP_TOKENS * D, 1 << 20,
    )(groups, tokens)
    arrived = exchange(packed.reshape(lon_count, MOST * TW, D)).reshape(SLOT_TOKENS, D)

    down = [(i, i + 1) for i in range(lat_count - 1)]
    up = [(i + 1, i) for i in range(lat_count - 1)]
    east = [(i, (i + 1) % lon_count) for i in range(lon_count)]
    west = [((i + 1) % lon_count, i) for i in range(lon_count)]
    left = lax.ppermute(tail, "lon", east)
    right = lax.ppermute(head, "lon", west)
    rim = sds((RIM, D), bf16)
    to_north, to_south, gain = call(
        row_kernel, (rim, rim, sds((1, D), f32)), [vspec()] * 2, (vspec(),) * 3, [],
        SOME_VMEM, 1 << 10, 1 << 20,
    )(tokens, gain)
    to_north, to_south = call(
        rim_kernel, (rim, rim), [vspec()] * 4, (vspec(), vspec()), [],
        SOME_VMEM, 1 << 10, 1 << 18, aliases={2: 0, 3: 1},
    )(left, right, to_north, to_south)
    north = lax.ppermute(to_south, "lat", down)
    south = lax.ppermute(to_north, "lat", up)

    cap_result = call(
        cap_kernel, sds((SLOT_TOKENS, HW), bf16),
        [vspec()] * 3, vspec(),
        [VMEM((SLOT_TOKENS, D), bf16), VMEM((SLOT_TOKENS, 3 * HW), bf16)],
        SOME_VMEM, 1100 << 20, 4 << 20, 1 << 19,
    )(arrived, gain, w_qkv)
    returned = exchange(cap_result.reshape(lon_count, MOST * TW, HW)).reshape(SLOT_TOKENS, HW)

    win_out, undo = call(
        window_kernel,
        (sds((RH * RW, HW), f32), sds((CAP_TOKENS, SLOT_TOKENS), bf16)),
        [vspec()] * 10, (vspec(), vspec()),
        [
            VMEM((N_WIN * WTOK, D), bf16),
            VMEM((N_WIN * QROWS, D), bf16),
            VMEM((N_WIN * WTOK, 2 * HW), bf16),
            VMEM((N_WIN * QROWS, HW), bf16),
            VMEM((2 * 128, 128), f32),
            VMEM((N_WIN * 128, 128), f32),
            VMEM((N_WIN * 128, 128), bf16),
            VMEM((N_WIN, QROWS, HW), f32),
            VMEM((2, 64, D), f32),
        ],
        SOME_VMEM, 2300 << 20, 6 << 20, 1 << 18,
    )(tokens, north, south, left, right, gain, bias_table, bias_index, hot, w_qkv)
    mixed = call(
        join_kernel, sds((RH * RW, HW), bf16),
        [vspec()] * 3, vspec(), [],
        8 << 20, 2 * CAP_TOKENS * SLOT_TOKENS * HW, 1 << 20,
    )(win_out, returned, undo)
    return mixed.reshape(RH, RW, HW)


def solution(mesh):
    placed = (P("lat", "lon", None), P(), P(), P(), P(), P(None, "lon", None, None))
    return jax.shard_map(layer, mesh=mesh, in_specs=placed, out_specs=P("lat", "lon", None), check_vma=False)
```

```python
import jax
import jax.numpy as jnp
from jax import lax
from jax.experimental import pallas as pl
from jax.experimental.pallas import tpu as pltpu
from jax.sharding import PartitionSpec as P


D = 1024
HEADS = 8
HD = 64
WIN = 8
TW = 4
CAP = 4
RH = 8
RW = 32
HW = 512
HALF = 4
BIAS_ROWS = 225
TILES_DEV = 32
TILE_COLS = RW // TW
GROUPS = 32
MOST = 2
SLOT_TOKENS = GROUPS * MOST * TW
CAP_TOKENS = CAP * RW
N_WIN = 10
WIN_B = 5
WTOK = WIN * WIN
QROWS = HALF * WIN

epsilon = 1e-05
masked_score = -1e30
EMPTY = 128.0
EMPTY_ABOVE = 64.0

ALL_VMEM = 67043328
PACK_VMEM = ALL_VMEM - 409600
SOME_VMEM = 24 << 20

VMEM = pltpu.VMEM
SMEM = pltpu.SMEM


def vspec():
    return pl.BlockSpec(memory_space=VMEM)


def aspec():
    return pl.BlockSpec(memory_space=pl.ANY)


def hspec():
    return pl.BlockSpec(memory_space=pltpu.HBM)


def norm_rows(values, gain):
    center = jnp.mean(values, axis=-1, keepdims=True)
    shifted = values - center
    spread = jnp.mean(jnp.square(shifted), axis=-1, keepdims=True)
    return shifted * lax.rsqrt(spread + epsilon) * gain


def slot_rows(group_ref, pole, lane):
    tile = lane // TW
    names = [group_ref[pole, t // TILE_COLS, 0, t % TILE_COLS] for t in range(TILES_DEV)]
    group = jnp.zeros_like(lane)
    for t in range(TILES_DEV):
        group = jnp.where(tile == t, names[t], group)
    rank = jnp.zeros_like(lane)
    for t in range(TILES_DEV):
        same = (group == names[t]) & (tile > t)
        rank = rank + same.astype(jnp.int32)
    return (group * MOST + rank) * TW + lane % TW


PACK_STEP = 64


def pack_kernel(
    names_ref, tokens_ref, send_ref, hot_out, head_out, tail_out,
    group_ref, rows, edge, out, hot_ref, head_ref, tail_ref, name_sem, sem, edge_sem, out_sem, side_sem,
):
    north = lax.axis_index("lat") == 0
    pole = jnp.where(north, 0, 1)
    start = jnp.where(north, 0, RH - CAP)
    names = pltpu.make_async_copy(names_ref, group_ref, name_sem)
    names.start()
    copy = pltpu.make_async_copy(tokens_ref.at[pl.ds(start, CAP)], rows, sem)
    copy.start()
    edges = [
        pltpu.make_async_copy(tokens_ref.at[:, pl.ds(k * (RW - 8), 8)], edge.at[k], edge_sem.at[k])
        for k in range(2)
    ]
    for each in edges:
        each.start()
    names.wait()
    lane = lax.broadcasted_iota(jnp.int32, (8, CAP_TOKENS), 1)
    slot = slot_rows(group_ref, pole, lane)[0:1]
    copy.wait()
    x = rows[...].reshape(CAP_TOKENS, D)
    sends = []
    for n in range(SLOT_TOKENS // PACK_STEP):
        at = pl.ds(n * PACK_STEP, PACK_STEP)
        hit = lax.broadcasted_iota(jnp.int32, (PACK_STEP, CAP_TOKENS), 0) + n * PACK_STEP == slot
        hot = hit.astype(jnp.float32)
        filled = jnp.max(hot, axis=1, keepdims=True) > 0.5
        hot = hot.astype(jnp.bfloat16)
        hot_ref[at, :] = hot
        moved = jnp.dot(hot, x, preferred_element_type=jnp.float32)
        out[at, :] = jnp.where(filled, moved, EMPTY).astype(jnp.bfloat16)
        sends.append(pltpu.make_async_copy(out.at[at], send_ref.at[at], out_sem.at[n]))
        sends[n].start()
    sends.append(pltpu.make_async_copy(hot_ref, hot_out, side_sem.at[0]))
    sends[-1].start()
    for each in edges:
        each.wait()
    lower = lax.broadcasted_iota(jnp.int32, (8, D), 0) < HALF
    for r in range(0, RH, 4):
        heads, tails = [], []
        for i in (r, r + 2):
            first = [edge[0, i + k].astype(jnp.float32) for k in range(2)]
            last = [edge[1, i + k].astype(jnp.float32) for k in range(2)]
            heads.append(jnp.where(lower, first[0], pltpu.roll(first[1], HALF, 0)))
            tails.append(jnp.where(lower, pltpu.roll(last[0], HALF, 0), last[1]))
        head_ref[r * 4 : r * 4 + 16] = jnp.concatenate(heads, 0).astype(jnp.bfloat16)
        tail_ref[r * 4 : r * 4 + 16] = jnp.concatenate(tails, 0).astype(jnp.bfloat16)
    for n, (part, to) in enumerate(((head_ref, head_out), (tail_ref, tail_out))):
        sends.append(pltpu.make_async_copy(part, to, side_sem.at[n + 1]))
        sends[-1].start()
    for send in sends:
        send.wait()


SIDE = HALF * HALF


def corner_kernel(left_ref, right_ref, gain_in, up_ref, down_ref, gain_ref):
    gain_ref[...] = gain_in[...]
    for out, first in ((up_ref, 0), (down_ref, (RH - HALF) * HALF)):
        for k, side in enumerate((left_ref, right_ref)):
            out[k * SIDE : k * SIDE + SIDE] = side[first : first + SIDE]


W_STEP = 256


def cap_kernel(x_ref, gain_ref, w_ref, out_ref, normed, qkv):
    n = SLOT_TOKENS
    gain = gain_ref[...]
    for i in range(0, n, 32):
        normed[i : i + 32] = norm_rows(x_ref[i : i + 32].astype(jnp.float32), gain).astype(jnp.bfloat16)
    pick = (lax.broadcasted_iota(jnp.int32, (8, 128), 1) == 0).astype(jnp.bfloat16)
    first = lax.dot_general(
        pick, x_ref[:, 0:128], (((1,), (1,)), ((), ())), preferred_element_type=jnp.float32
    )
    empty = jnp.where(first[0:1] > EMPTY_ABOVE, masked_score, 0.0)
    for j in range(3 * HW // W_STEP):
        at = slice(j * W_STEP, j * W_STEP + W_STEP)
        part = jnp.dot(normed[...], w_ref[:, at], preferred_element_type=jnp.float32)
        qkv[:, at] = part.astype(jnp.bfloat16)
    low = lax.broadcasted_iota(jnp.int32, (n, 128), 1) < HD
    for pair in range(HEADS // 2):
        at = pair * 128
        q = qkv[:, at : at + 128] * jnp.bfloat16(HD ** (-0.5))
        k = qkv[:, HW + at : HW + at + 128]
        v = qkv[:, 2 * HW + at : 2 * HW + at + 128]
        mixed = []
        for half in range(2):
            mine = low if half == 0 else jnp.logical_not(low)
            qh = jnp.where(mine, q, jnp.zeros_like(q))
            s = lax.dot_general(qh, k, (((1,), (1,)), ((), ())), preferred_element_type=jnp.float32)
            s = s + empty
            raised = jnp.exp(s - jnp.max(s, axis=-1, keepdims=True))
            weights = (raised * (1.0 / jnp.sum(raised, axis=-1, keepdims=True))).astype(jnp.bfloat16)
            mixed.append(jnp.dot(weights, v, preferred_element_type=jnp.float32))
        out_ref[:, at : at + 128] = jnp.where(low, mixed[0], mixed[1]).astype(jnp.bfloat16)


def window_kernel(
    own_ref, north_ref, south_ref, north_side, south_side, left_ref, right_ref, gain_ref, table_ref, index_ref, hot_ref, w_ref,
    out_ref, undo_ref, xs, xq, kv, qs, bias, scores, weights, wout, edges,
):
    gain = gain_ref[...]
    lat = lax.axis_index("lat")

    polar = (lat == 0) | (lat == lax.axis_size("lat") - 1)
    undo = jnp.transpose(hot_ref[...].astype(jnp.float32))
    undo_ref[...] = jnp.where(polar, undo, 0.0).astype(jnp.bfloat16)

    lane = lax.broadcasted_iota(jnp.int32, (8, 128), 1)
    first = lane < WTOK
    key_row = (lane % WTOK) // WIN
    off_north = (lat == 0) & (key_row < HALF)
    off_south = (lat == lax.axis_size("lat") - 1) & (key_row >= HALF)
    tables = []
    for h in range(HEADS):
        parts = [table_ref[h : h + 1, c : c + 128] for c in (0, BIAS_ROWS - 128)]
        tables.append([jnp.broadcast_to(part, (8, 128)) for part in parts])
    for a in range(2):
        off = off_north if a == 0 else off_south
        for i in range(0, QROWS, 8):
            at = (QROWS if a == 0 else 0) + i
            idx = index_ref[at : at + 8, :]
            idx = jnp.concatenate([idx, idx], axis=1)
            high = idx >= 128
            inner = jnp.where(high, idx - (BIAS_ROWS - 128), idx)
            for h4 in range(4):
                found = []
                for h in (h4, h4 + 4):
                    lo = jnp.take_along_axis(tables[h][0], inner, axis=1)
                    hi = jnp.take_along_axis(tables[h][1], inner, axis=1)
                    found.append(jnp.where(high, hi, lo))
                value = jnp.where(first, found[0], found[1])
                to = a * 128 + h4 * QROWS + i
                bias[to : to + 8, :] = jnp.where(off, masked_score, value)

    for side, ref in enumerate((left_ref, right_ref)):
        at = side * SIDE
        for to, x in (
            (0, north_side[at : at + SIDE]),
            (SIDE, ref[...]),
            (3 * SIDE, south_side[at : at + SIDE]),
        ):
            edges[side, to : to + x.shape[0]] = norm_rows(x.astype(jnp.float32), gain)
    lower = lax.broadcasted_iota(jnp.int32, (8, D), 0) < HALF
    rows = [(north_ref, i) for i in range(HALF)] + [(own_ref, i) for i in range(RH)]
    rows += [(south_ref, i) for i in range(HALF)]
    for r in range(0, RH + WIN, 2):
        blocks = [[], []]
        for k in range(2):
            ref, i = rows[r + k]
            normed = norm_rows(ref[i].astype(jnp.float32), gain)
            turned = [pltpu.roll(normed[j * 8 : j * 8 + 8], HALF, 0) for j in range(4)]
            lo = edges[0, r * 4 : r * 4 + 8]
            hi = edges[1, r * 4 : r * 4 + 8]
            if k == 0:
                hi = pltpu.roll(hi, HALF, 0)
            else:
                lo = pltpu.roll(lo, HALF, 0)
            seq = [lo] + turned + [hi]
            blocks[k] = [jnp.where(lower, seq[b], seq[b + 1]) for b in range(WIN_B)]
        a, wr = r // WIN, r % WIN
        for b in range(WIN_B):
            both = jnp.concatenate([blocks[0][b], blocks[1][b]], 0).astype(jnp.bfloat16)
            to = (a * WIN_B + b) * WTOK + wr * WIN
            xs[to : to + 16] = both
            if (wr >= HALF) == (a == 0):
                to = (a * WIN_B + b) * QROWS + (wr % HALF) * WIN
                xq[to : to + 16] = both

    for j in range(3 * HW // W_STEP):
        at = slice(j * W_STEP, j * W_STEP + W_STEP)
        if j * W_STEP < HW:
            qs[:, at] = jnp.dot(xq[...], w_ref[:, at], preferred_element_type=jnp.float32).astype(jnp.bfloat16)
        else:
            to = slice(j * W_STEP - HW, j * W_STEP - HW + W_STEP)
            kv[:, to] = jnp.dot(xs[...], w_ref[:, at], preferred_element_type=jnp.float32).astype(jnp.bfloat16)

    head = lax.broadcasted_iota(jnp.int32, (QROWS, HW), 1) // HD % 4
    blank = jnp.zeros((WTOK, HW // 2), jnp.bfloat16)

    def two_groups(x):
        top = jnp.concatenate([x[:, : HW // 2], blank], 1)
        low = jnp.concatenate([blank, x[:, HW // 2 :]], 1)
        return jnp.concatenate([top, low], 0)

    for n in range(N_WIN):
        q = qs[n * QROWS : n * QROWS + QROWS] * jnp.bfloat16(HD ** (-0.5))
        spread = jnp.concatenate([jnp.where(head == h, q, jnp.zeros_like(q)) for h in range(4)], 0)
        k = two_groups(kv[n * WTOK : n * WTOK + WTOK, 0:HW])
        s = lax.dot_general(spread, k, (((1,), (1,)), ((), ())), preferred_element_type=jnp.float32)
        a = n // WIN_B
        scores[n * 128 : n * 128 + 128] = s + bias[a * 128 : a * 128 + 128]
    left = lax.broadcasted_iota(jnp.int32, (128, 128), 1) < WTOK
    for n in range(N_WIN):
        s = scores[n * 128 : n * 128 + 128]
        top0 = jnp.max(jnp.where(left, s, -jnp.inf), axis=-1, keepdims=True)
        top1 = jnp.max(jnp.where(left, -jnp.inf, s), axis=-1, keepdims=True)
        raised = jnp.exp(s - jnp.where(left, top0, top1))
        sum0 = jnp.sum(jnp.where(left, raised, 0.0), axis=-1, keepdims=True)
        sum1 = jnp.sum(jnp.where(left, 0.0, raised), axis=-1, keepdims=True)
        share = jnp.where(left, 1.0 / sum0, 1.0 / sum1)
        weights[n * 128 : n * 128 + 128] = (raised * share).astype(jnp.bfloat16)
    for n in range(N_WIN):
        v = two_groups(kv[n * WTOK : n * WTOK + WTOK, HW : 2 * HW])
        o = jnp.dot(weights[n * 128 : n * 128 + 128], v, preferred_element_type=jnp.float32)
        total = o[0:QROWS]
        for h in range(1, 4):
            total = jnp.where(head == h, o[h * QROWS : h * QROWS + QROWS], total)
        wout[n] = total
    lower = lax.broadcasted_iota(jnp.int32, (8, HW), 0) < HALF
    for r in range(RH):
        a, wr = r // HALF, r % HALF
        turned = [
            pltpu.roll(wout[a * WIN_B + b, wr * WIN : wr * WIN + WIN], HALF, 0) for b in range(WIN_B)
        ]
        for j in range(4):
            to = r * RW + j * 8
            out_ref[to : to + 8] = jnp.where(lower, turned[j], turned[j + 1])


def join_kernel(win_ref, back_ref, undo_ref, out_ref):
    north = lax.axis_index("lat") == 0
    cap = jnp.dot(undo_ref[...], back_ref[...], preferred_element_type=jnp.float32)
    top = win_ref[0:CAP_TOKENS] + jnp.where(north, cap, 0.0)
    low = win_ref[CAP_TOKENS:] + jnp.where(north, 0.0, cap)
    out_ref[0:CAP_TOKENS] = top.astype(jnp.bfloat16)
    out_ref[CAP_TOKENS:] = low.astype(jnp.bfloat16)


def sds(shape, dtype):
    return jax.ShapeDtypeStruct(shape, dtype)


def call(kernel, outs, ins, out_specs, scratch, vmem, flops, nbytes, trans=0, aliases=None):
    return pl.pallas_call(
        kernel,
        out_shape=outs,
        in_specs=ins,
        out_specs=out_specs,
        scratch_shapes=scratch,
        compiler_params=pltpu.CompilerParams(vmem_limit_bytes=vmem),
        input_output_aliases=aliases or {},
        cost_estimate=pl.CostEstimate(flops=flops, bytes_accessed=nbytes, transcendentals=trans),
    )


def exchange(block):
    return lax.all_to_all(block, "lon", split_axis=0, concat_axis=0, tiled=True)


def layer(tokens, ln_gain, w_qkv, bias_table, bias_index, cap_group):
    lat_count = lax.axis_size("lat")
    lon_count = lax.axis_size("lon")
    bf16, f32 = jnp.bfloat16, jnp.float32
    gain = ln_gain.reshape(1, D)
    groups = cap_group.transpose(0, 2, 3, 1)

    side = sds((RH * HALF, D), bf16)
    packed, hot, head, tail = call(
        pack_kernel,
        (sds((SLOT_TOKENS, D), bf16), sds((SLOT_TOKENS, CAP_TOKENS), bf16), side, side),
        [aspec(), hspec()], (hspec(),) * 4,
        [
            SMEM((2, CAP, 1, TILE_COLS), jnp.int32),
            VMEM((CAP, RW, D), bf16),
            VMEM((2, RH, 8, D), bf16),
            VMEM((SLOT_TOKENS, D), bf16),
            VMEM((SLOT_TOKENS, CAP_TOKENS), bf16),
            VMEM((RH * HALF, D), bf16),
            VMEM((RH * HALF, D), bf16),
            pltpu.SemaphoreType.DMA,
            pltpu.SemaphoreType.DMA,
            pltpu.SemaphoreType.DMA((2,)),
            pltpu.SemaphoreType.DMA((SLOT_TOKENS // PACK_STEP,)),
            pltpu.SemaphoreType.DMA((3,)),
        ],
        PACK_VMEM, 2 * SLOT_TOKENS * CAP_TOKENS * D, 1 << 20,
    )(groups, tokens)
    arrived = exchange(packed.reshape(lon_count, MOST * TW, D)).reshape(SLOT_TOKENS, D)

    down = [(i, i + 1) for i in range(lat_count - 1)]
    up = [(i + 1, i) for i in range(lat_count - 1)]
    east = [(i, (i + 1) % lon_count) for i in range(lon_count)]
    west = [((i + 1) % lon_count, i) for i in range(lon_count)]
    tied, _ = lax.optimization_barrier((tokens, packed))
    north = lax.ppermute(tied[RH - HALF :], "lat", down)
    south = lax.ppermute(tied[:HALF], "lat", up)
    left = lax.ppermute(tail, "lon", east)
    right = lax.ppermute(head, "lon", west)
    pair = sds((2 * SIDE, D), bf16)
    to_north, to_south, gain = call(
        corner_kernel, (pair, pair, sds((1, D), f32)), [vspec()] * 3, (vspec(),) * 3, [],
        SOME_VMEM, 1 << 10, 1 << 19,
    )(left, right, gain)
    north_side = lax.ppermute(to_south, "lat", down)
    south_side = lax.ppermute(to_north, "lat", up)

    cap_result = call(
        cap_kernel, sds((SLOT_TOKENS, HW), bf16),
        [vspec()] * 3, vspec(),
        [VMEM((SLOT_TOKENS, D), bf16), VMEM((SLOT_TOKENS, 3 * HW), bf16)],
        SOME_VMEM, 1100 << 20, 4 << 20, 1 << 19,
    )(arrived, gain, w_qkv)
    returned = exchange(cap_result.reshape(lon_count, MOST * TW, HW)).reshape(SLOT_TOKENS, HW)

    win_out, undo = call(
        window_kernel,
        (sds((RH * RW, HW), f32), sds((CAP_TOKENS, SLOT_TOKENS), bf16)),
        [vspec()] * 12, (vspec(), vspec()),
        [
            VMEM((N_WIN * WTOK, D), bf16),
            VMEM((N_WIN * QROWS, D), bf16),
            VMEM((N_WIN * WTOK, 2 * HW), bf16),
            VMEM((N_WIN * QROWS, HW), bf16),
            VMEM((2 * 128, 128), f32),
            VMEM((N_WIN * 128, 128), f32),
            VMEM((N_WIN * 128, 128), bf16),
            VMEM((N_WIN, QROWS, HW), f32),
            VMEM((2, 64, D), f32),
        ],
        SOME_VMEM, 2300 << 20, 6 << 20, 1 << 18,
    )(tokens, north, south, north_side, south_side, left, right, gain, bias_table, bias_index, hot, w_qkv)
    mixed = call(
        join_kernel, sds((RH * RW, HW), bf16),
        [vspec()] * 3, vspec(), [],
        8 << 20, 2 * CAP_TOKENS * SLOT_TOKENS * HW, 1 << 20,
    )(win_out, returned, undo)
    return mixed.reshape(RH, RW, HW)


def solution(mesh):
    placed = (P("lat", "lon", None), P(), P(), P(), P(), P(None, "lon", None, None))
    return jax.shard_map(layer, mesh=mesh, in_specs=placed, out_specs=P("lat", "lon", None), check_vma=False)
```

```python
import jax
import jax.numpy as jnp
from jax import lax
from jax.experimental import pallas as pl
from jax.experimental.pallas import tpu as pltpu
from jax.sharding import PartitionSpec as P


D = 1024
HEADS = 8
HD = 64
WIN = 8
TW = 4
CAP = 4
RH = 8
RW = 32
HW = 512
HALF = 4
BIAS_ROWS = 225
TILES_DEV = 32
TILE_COLS = RW // TW
GROUPS = 32
MOST = 2
SLOT_TOKENS = GROUPS * MOST * TW
CAP_TOKENS = CAP * RW
N_WIN = 10
WIN_B = 5
WTOK = WIN * WIN
QROWS = HALF * WIN

epsilon = 1e-05
masked_score = -1e30
EMPTY = 128.0
EMPTY_ABOVE = 64.0

ALL_VMEM = 67043328
PACK_VMEM = ALL_VMEM - 409600
SOME_VMEM = 24 << 20

VMEM = pltpu.VMEM
SMEM = pltpu.SMEM


def vspec():
    return pl.BlockSpec(memory_space=VMEM)


def aspec():
    return pl.BlockSpec(memory_space=pl.ANY)


def hspec():
    return pl.BlockSpec(memory_space=pltpu.HBM)


def norm_rows(values, gain):
    center = jnp.mean(values, axis=-1, keepdims=True)
    shifted = values - center
    spread = jnp.mean(jnp.square(shifted), axis=-1, keepdims=True)
    return shifted * lax.rsqrt(spread + epsilon) * gain


def slot_rows(group_ref, pole, lane):
    tile = lane // TW
    names = [group_ref[pole, t // TILE_COLS, 0, t % TILE_COLS] for t in range(TILES_DEV)]
    group = jnp.zeros_like(lane)
    for t in range(TILES_DEV):
        group = jnp.where(tile == t, names[t], group)
    rank = jnp.zeros_like(lane)
    for t in range(TILES_DEV):
        same = (group == names[t]) & (tile > t)
        rank = rank + same.astype(jnp.int32)
    return (group * MOST + rank) * TW + lane % TW


PACK_STEP = 64


def pack_kernel(names_ref, tokens_ref, send_ref, hot_ref, group_ref, rows, out, hot, name_sem, sem, out_sem):
    north = lax.axis_index("lat") == 0
    pole = jnp.where(north, 0, 1)
    start = jnp.where(north, 0, RH - CAP)
    names = pltpu.make_async_copy(names_ref, group_ref, name_sem)
    names.start()
    copy = pltpu.make_async_copy(tokens_ref.at[pl.ds(start, CAP)], rows, sem)
    copy.start()
    names.wait()
    lane = lax.broadcasted_iota(jnp.int32, (8, CAP_TOKENS), 1)
    slot = slot_rows(group_ref, pole, lane)[0:1]
    copy.wait()
    x = rows[...].reshape(CAP_TOKENS, D)
    sends = []
    for n in range(SLOT_TOKENS // PACK_STEP):
        at = pl.ds(n * PACK_STEP, PACK_STEP)
        hit = lax.broadcasted_iota(jnp.int32, (PACK_STEP, CAP_TOKENS), 0) + n * PACK_STEP == slot
        here = hit.astype(jnp.float32)
        filled = jnp.max(here, axis=1, keepdims=True) > 0.5
        here = here.astype(jnp.bfloat16)
        hot[at, :] = here
        moved = jnp.dot(here, x, preferred_element_type=jnp.float32)
        out[at, :] = jnp.where(filled, moved, EMPTY).astype(jnp.bfloat16)
        sends.append(pltpu.make_async_copy(out.at[at], send_ref.at[at], out_sem.at[n]))
        sends[n].start()
    sends.append(pltpu.make_async_copy(hot, hot_ref, out_sem.at[len(sends)]))
    sends[-1].start()
    for send in sends:
        send.wait()


def edge_kernel(own_ref, north_ref, south_ref, head_ref, tail_ref):
    lower = lax.broadcasted_iota(jnp.int32, (8, D), 0) < HALF
    pairs = [(north_ref, 0), (north_ref, 2)]
    pairs += [(own_ref, i) for i in range(0, RH, 2)]
    pairs += [(south_ref, 0), (south_ref, 2)]
    for n in range(0, len(pairs), 2):
        heads, tails = [], []
        for ref, i in pairs[n : n + 2]:
            first = [ref[i + k, 0:8].astype(jnp.float32) for k in range(2)]
            last = [ref[i + k, 24:32].astype(jnp.float32) for k in range(2)]
            heads.append(jnp.where(lower, first[0], pltpu.roll(first[1], HALF, 0)))
            tails.append(jnp.where(lower, pltpu.roll(last[0], HALF, 0), last[1]))
        head_ref[n * 8 : n * 8 + 16] = jnp.concatenate(heads, 0).astype(jnp.bfloat16)
        tail_ref[n * 8 : n * 8 + 16] = jnp.concatenate(tails, 0).astype(jnp.bfloat16)


def bias_kernel(table_ref, index_ref, gain_in, bias, gain_ref):
    gain_ref[...] = gain_in[...]
    lat = lax.axis_index("lat")
    lane = lax.broadcasted_iota(jnp.int32, (8, 128), 1)
    first = lane < WTOK
    key_row = (lane % WTOK) // WIN
    off_north = (lat == 0) & (key_row < HALF)
    off_south = (lat == lax.axis_size("lat") - 1) & (key_row >= HALF)
    tables = []
    for h in range(HEADS):
        parts = [table_ref[h : h + 1, c : c + 128] for c in (0, BIAS_ROWS - 128)]
        tables.append([jnp.broadcast_to(part, (8, 128)) for part in parts])
    for a in range(2):
        off = off_north if a == 0 else off_south
        for i in range(0, QROWS, 8):
            at = (QROWS if a == 0 else 0) + i
            idx = index_ref[at : at + 8, :]
            idx = jnp.concatenate([idx, idx], axis=1)
            high = idx >= 128
            inner = jnp.where(high, idx - (BIAS_ROWS - 128), idx)
            for h4 in range(4):
                found = []
                for h in (h4, h4 + 4):
                    lo = jnp.take_along_axis(tables[h][0], inner, axis=1)
                    hi = jnp.take_along_axis(tables[h][1], inner, axis=1)
                    found.append(jnp.where(high, hi, lo))
                value = jnp.where(first, found[0], found[1])
                to = a * 128 + h4 * QROWS + i
                bias[to : to + 8, :] = jnp.where(off, masked_score, value)


W_STEP = 256


def cap_kernel(x_ref, gain_ref, w_ref, out_ref, normed, qkv):
    n = SLOT_TOKENS
    gain = gain_ref[...]
    for i in range(0, n, 32):
        normed[i : i + 32] = norm_rows(x_ref[i : i + 32].astype(jnp.float32), gain).astype(jnp.bfloat16)
    pick = (lax.broadcasted_iota(jnp.int32, (8, 128), 1) == 0).astype(jnp.bfloat16)
    first = lax.dot_general(
        pick, x_ref[:, 0:128], (((1,), (1,)), ((), ())), preferred_element_type=jnp.float32
    )
    empty = jnp.where(first[0:1] > EMPTY_ABOVE, masked_score, 0.0)
    for j in range(3 * HW // W_STEP):
        at = slice(j * W_STEP, j * W_STEP + W_STEP)
        part = jnp.dot(normed[...], w_ref[:, at], preferred_element_type=jnp.float32)
        qkv[:, at] = part.astype(jnp.bfloat16)
    low = lax.broadcasted_iota(jnp.int32, (n, 128), 1) < HD
    for pair in range(HEADS // 2):
        at = pair * 128
        q = qkv[:, at : at + 128] * jnp.bfloat16(HD ** (-0.5))
        k = qkv[:, HW + at : HW + at + 128]
        v = qkv[:, 2 * HW + at : 2 * HW + at + 128]
        mixed = []
        for half in range(2):
            mine = low if half == 0 else jnp.logical_not(low)
            qh = jnp.where(mine, q, jnp.zeros_like(q))
            s = lax.dot_general(qh, k, (((1,), (1,)), ((), ())), preferred_element_type=jnp.float32)
            s = s + empty
            raised = jnp.exp(s - jnp.max(s, axis=-1, keepdims=True))
            weights = (raised * (1.0 / jnp.sum(raised, axis=-1, keepdims=True))).astype(jnp.bfloat16)
            mixed.append(jnp.dot(weights, v, preferred_element_type=jnp.float32))
        out_ref[:, at : at + 128] = jnp.where(low, mixed[0], mixed[1]).astype(jnp.bfloat16)


def window_kernel(
    own_ref, north_ref, south_ref, left_ref, right_ref, gain_ref, bias, hot_ref, w_ref,
    out_ref, undo_ref, xs, xq, kv, qs, scores, weights, wout, edges,
):
    gain = gain_ref[...]
    lat = lax.axis_index("lat")

    polar = (lat == 0) | (lat == lax.axis_size("lat") - 1)
    undo = jnp.transpose(hot_ref[...].astype(jnp.float32))
    undo_ref[...] = jnp.where(polar, undo, 0.0).astype(jnp.bfloat16)

    for side, ref in enumerate((left_ref, right_ref)):
        for i in range(0, 64, 32):
            edges[side, i : i + 32] = norm_rows(ref[i : i + 32].astype(jnp.float32), gain)
    lower = lax.broadcasted_iota(jnp.int32, (8, D), 0) < HALF
    rows = [(north_ref, i) for i in range(HALF)] + [(own_ref, i) for i in range(RH)]
    rows += [(south_ref, i) for i in range(HALF)]
    for r in range(0, RH + WIN, 2):
        blocks = [[], []]
        for k in range(2):
            ref, i = rows[r + k]
            normed = norm_rows(ref[i].astype(jnp.float32), gain)
            turned = [pltpu.roll(normed[j * 8 : j * 8 + 8], HALF, 0) for j in range(4)]
            lo = edges[0, r * 4 : r * 4 + 8]
            hi = edges[1, r * 4 : r * 4 + 8]
            if k == 0:
                hi = pltpu.roll(hi, HALF, 0)
            else:
                lo = pltpu.roll(lo, HALF, 0)
            seq = [lo] + turned + [hi]
            blocks[k] = [jnp.where(lower, seq[b], seq[b + 1]) for b in range(WIN_B)]
        a, wr = r // WIN, r % WIN
        for b in range(WIN_B):
            both = jnp.concatenate([blocks[0][b], blocks[1][b]], 0).astype(jnp.bfloat16)
            to = (a * WIN_B + b) * WTOK + wr * WIN
            xs[to : to + 16] = both
            if (wr >= HALF) == (a == 0):
                to = (a * WIN_B + b) * QROWS + (wr % HALF) * WIN
                xq[to : to + 16] = both

    for j in range(3 * HW // W_STEP):
        at = slice(j * W_STEP, j * W_STEP + W_STEP)
        if j * W_STEP < HW:
            qs[:, at] = jnp.dot(xq[...], w_ref[:, at], preferred_element_type=jnp.float32).astype(jnp.bfloat16)
        else:
            to = slice(j * W_STEP - HW, j * W_STEP - HW + W_STEP)
            kv[:, to] = jnp.dot(xs[...], w_ref[:, at], preferred_element_type=jnp.float32).astype(jnp.bfloat16)

    head = lax.broadcasted_iota(jnp.int32, (QROWS, HW), 1) // HD % 4
    blank = jnp.zeros((WTOK, HW // 2), jnp.bfloat16)

    def two_groups(x):
        top = jnp.concatenate([x[:, : HW // 2], blank], 1)
        low = jnp.concatenate([blank, x[:, HW // 2 :]], 1)
        return jnp.concatenate([top, low], 0)

    for n in range(N_WIN):
        q = qs[n * QROWS : n * QROWS + QROWS] * jnp.bfloat16(HD ** (-0.5))
        spread = jnp.concatenate([jnp.where(head == h, q, jnp.zeros_like(q)) for h in range(4)], 0)
        k = two_groups(kv[n * WTOK : n * WTOK + WTOK, 0:HW])
        s = lax.dot_general(spread, k, (((1,), (1,)), ((), ())), preferred_element_type=jnp.float32)
        a = n // WIN_B
        scores[n * 128 : n * 128 + 128] = s + bias[a * 128 : a * 128 + 128]
    left = lax.broadcasted_iota(jnp.int32, (128, 128), 1) < WTOK
    for n in range(N_WIN):
        s = scores[n * 128 : n * 128 + 128]
        top0 = jnp.max(jnp.where(left, s, -jnp.inf), axis=-1, keepdims=True)
        top1 = jnp.max(jnp.where(left, -jnp.inf, s), axis=-1, keepdims=True)
        raised = jnp.exp(s - jnp.where(left, top0, top1))
        sum0 = jnp.sum(jnp.where(left, raised, 0.0), axis=-1, keepdims=True)
        sum1 = jnp.sum(jnp.where(left, 0.0, raised), axis=-1, keepdims=True)
        share = jnp.where(left, 1.0 / sum0, 1.0 / sum1)
        weights[n * 128 : n * 128 + 128] = (raised * share).astype(jnp.bfloat16)
    for n in range(N_WIN):
        v = two_groups(kv[n * WTOK : n * WTOK + WTOK, HW : 2 * HW])
        o = jnp.dot(weights[n * 128 : n * 128 + 128], v, preferred_element_type=jnp.float32)
        total = o[0:QROWS]
        for h in range(1, 4):
            total = jnp.where(head == h, o[h * QROWS : h * QROWS + QROWS], total)
        wout[n] = total
    lower = lax.broadcasted_iota(jnp.int32, (8, HW), 0) < HALF
    for r in range(RH):
        a, wr = r // HALF, r % HALF
        turned = [
            pltpu.roll(wout[a * WIN_B + b, wr * WIN : wr * WIN + WIN], HALF, 0) for b in range(WIN_B)
        ]
        for j in range(4):
            to = r * RW + j * 8
            out_ref[to : to + 8] = jnp.where(lower, turned[j], turned[j + 1])


def join_kernel(win_ref, back_ref, undo_ref, out_ref):
    north = lax.axis_index("lat") == 0
    cap = jnp.dot(undo_ref[...], back_ref[...], preferred_element_type=jnp.float32)
    top = win_ref[0:CAP_TOKENS] + jnp.where(north, cap, 0.0)
    low = win_ref[CAP_TOKENS:] + jnp.where(north, 0.0, cap)
    out_ref[0:CAP_TOKENS] = top.astype(jnp.bfloat16)
    out_ref[CAP_TOKENS:] = low.astype(jnp.bfloat16)


def sds(shape, dtype):
    return jax.ShapeDtypeStruct(shape, dtype)


def call(kernel, outs, ins, out_specs, scratch, vmem, flops, nbytes, trans=0, aliases=None):
    return pl.pallas_call(
        kernel,
        out_shape=outs,
        in_specs=ins,
        out_specs=out_specs,
        scratch_shapes=scratch,
        compiler_params=pltpu.CompilerParams(vmem_limit_bytes=vmem),
        input_output_aliases=aliases or {},
        cost_estimate=pl.CostEstimate(flops=flops, bytes_accessed=nbytes, transcendentals=trans),
    )


def exchange(block):
    return lax.all_to_all(block, "lon", split_axis=0, concat_axis=0, tiled=True)


def layer(tokens, ln_gain, w_qkv, bias_table, bias_index, cap_group):
    lat_count = lax.axis_size("lat")
    lon_count = lax.axis_size("lon")
    bf16, f32 = jnp.bfloat16, jnp.float32
    gain = ln_gain.reshape(1, D)
    groups = cap_group.transpose(0, 2, 3, 1)

    packed, hot = call(
        pack_kernel, (sds((SLOT_TOKENS, D), bf16), sds((SLOT_TOKENS, CAP_TOKENS), bf16)),
        [aspec(), hspec()], (hspec(), hspec()),
        [
            SMEM((2, CAP, 1, TILE_COLS), jnp.int32),
            VMEM((CAP, RW, D), bf16),
            VMEM((SLOT_TOKENS, D), bf16),
            VMEM((SLOT_TOKENS, CAP_TOKENS), bf16),
            pltpu.SemaphoreType.DMA,
            pltpu.SemaphoreType.DMA,
            pltpu.SemaphoreType.DMA((SLOT_TOKENS // PACK_STEP + 1,)),
        ],
        PACK_VMEM, 2 * SLOT_TOKENS * CAP_TOKENS * D, 1 << 20,
    )(groups, tokens)
    arrived = exchange(packed.reshape(lon_count, MOST * TW, D)).reshape(SLOT_TOKENS, D)

    down = [(i, i + 1) for i in range(lat_count - 1)]
    up = [(i + 1, i) for i in range(lat_count - 1)]
    east = [(i, (i + 1) % lon_count) for i in range(lon_count)]
    west = [((i + 1) % lon_count, i) for i in range(lon_count)]
    tied, _ = lax.optimization_barrier((tokens, packed))
    north = lax.ppermute(tied[RH - HALF :], "lat", down)
    south = lax.ppermute(tied[:HALF], "lat", up)
    bias, gain = call(
        bias_kernel, (sds((2 * 128, 128), f32), sds((1, D), f32)), [vspec()] * 3, (vspec(), vspec()), [],
        SOME_VMEM, 1 << 18, 1 << 18,
    )(bias_table, bias_index, gain)
    side = sds(((RH + WIN) * HALF, D), bf16)
    head, tail = call(
        edge_kernel, (side, side), [vspec()] * 3, (vspec(), vspec()), [],
        SOME_VMEM, 4 << 30, 3 << 19,
    )(tokens, north, south)
    left = lax.ppermute(tail, "lon", east)
    right = lax.ppermute(head, "lon", west)

    cap_result = call(
        cap_kernel, sds((SLOT_TOKENS, HW), bf16),
        [vspec()] * 3, vspec(),
        [VMEM((SLOT_TOKENS, D), bf16), VMEM((SLOT_TOKENS, 3 * HW), bf16)],
        SOME_VMEM, 1100 << 20, 4 << 20, 1 << 19,
    )(arrived, gain, w_qkv)
    returned = exchange(cap_result.reshape(lon_count, MOST * TW, HW)).reshape(SLOT_TOKENS, HW)

    win_out, undo = call(
        window_kernel,
        (sds((RH * RW, HW), f32), sds((CAP_TOKENS, SLOT_TOKENS), bf16)),
        [vspec()] * 9, (vspec(), vspec()),
        [
            VMEM((N_WIN * WTOK, D), bf16),
            VMEM((N_WIN * QROWS, D), bf16),
            VMEM((N_WIN * WTOK, 2 * HW), bf16),
            VMEM((N_WIN * QROWS, HW), bf16),
            VMEM((N_WIN * 128, 128), f32),
            VMEM((N_WIN * 128, 128), bf16),
            VMEM((N_WIN, QROWS, HW), f32),
            VMEM((2, 64, D), f32),
        ],
        SOME_VMEM, 2300 << 20, 6 << 20, 1 << 18,
    )(tokens, north, south, left, right, gain, bias, hot, w_qkv)
    mixed = call(
        join_kernel, sds((RH * RW, HW), bf16),
        [vspec()] * 3, vspec(), [],
        8 << 20, 2 * CAP_TOKENS * SLOT_TOKENS * HW, 1 << 20,
    )(win_out, returned, undo)
    return mixed.reshape(RH, RW, HW)


def solution(mesh):
    placed = (P("lat", "lon", None), P(), P(), P(), P(), P(None, "lon", None, None))
    return jax.shard_map(layer, mesh=mesh, in_specs=placed, out_specs=P("lat", "lon", None), check_vma=False)
```

```python
import jax
import jax.numpy as jnp
from jax import lax
from jax.experimental import pallas as pl
from jax.experimental.pallas import tpu as pltpu
from jax.sharding import PartitionSpec as P


D = 1024
HEADS = 8
HD = 64
WIN = 8
TW = 4
CAP = 4
RH = 8
RW = 32
HW = 512
HALF = 4
BIAS_ROWS = 225
TILES_DEV = 32
TILE_COLS = RW // TW
GROUPS = 32
MOST = 2
SLOT_TOKENS = GROUPS * MOST * TW
CAP_TOKENS = CAP * RW
WTOK = WIN * WIN
QROWS = HALF * WIN

epsilon = 1e-05
masked_score = -1e30
EMPTY = 128.0
EMPTY_ABOVE = 64.0

ALL_VMEM = 67043328
PACK_VMEM = ALL_VMEM - 409600
SOME_VMEM = 24 << 20

VMEM = pltpu.VMEM
SMEM = pltpu.SMEM


def vspec():
    return pl.BlockSpec(memory_space=VMEM)


def aspec():
    return pl.BlockSpec(memory_space=pl.ANY)


def hspec():
    return pl.BlockSpec(memory_space=pltpu.HBM)


def norm_rows(values, gain):
    center = jnp.mean(values, axis=-1, keepdims=True)
    shifted = values - center
    spread = jnp.mean(jnp.square(shifted), axis=-1, keepdims=True)
    return shifted * lax.rsqrt(spread + epsilon) * gain


def slot_rows(group_ref, pole, lane):
    tile = lane // TW
    names = [group_ref[pole, t // TILE_COLS, 0, t % TILE_COLS] for t in range(TILES_DEV)]
    group = jnp.zeros_like(lane)
    for t in range(TILES_DEV):
        group = jnp.where(tile == t, names[t], group)
    rank = jnp.zeros_like(lane)
    for t in range(TILES_DEV):
        same = (group == names[t]) & (tile > t)
        rank = rank + same.astype(jnp.int32)
    return (group * MOST + rank) * TW + lane % TW


PACK_STEP = 64


def pack_kernel(names_ref, tokens_ref, send_ref, hot_ref, group_ref, rows, out, hot, name_sem, sem, out_sem):
    north = lax.axis_index("lat") == 0
    pole = jnp.where(north, 0, 1)
    start = jnp.where(north, 0, RH - CAP)
    names = pltpu.make_async_copy(names_ref, group_ref, name_sem)
    names.start()
    copy = pltpu.make_async_copy(tokens_ref.at[pl.ds(start, CAP)], rows, sem)
    copy.start()
    names.wait()
    lane = lax.broadcasted_iota(jnp.int32, (8, CAP_TOKENS), 1)
    slot = slot_rows(group_ref, pole, lane)[0:1]
    copy.wait()
    x = rows[...].reshape(CAP_TOKENS, D)
    sends = []
    for n in range(SLOT_TOKENS // PACK_STEP):
        at = pl.ds(n * PACK_STEP, PACK_STEP)
        hit = lax.broadcasted_iota(jnp.int32, (PACK_STEP, CAP_TOKENS), 0) + n * PACK_STEP == slot
        here = hit.astype(jnp.float32)
        filled = jnp.max(here, axis=1, keepdims=True) > 0.5
        here = here.astype(jnp.bfloat16)
        hot[at, :] = here
        moved = jnp.dot(here, x, preferred_element_type=jnp.float32)
        out[at, :] = jnp.where(filled, moved, EMPTY).astype(jnp.bfloat16)
        sends.append(pltpu.make_async_copy(out.at[at], send_ref.at[at], out_sem.at[n]))
        sends[n].start()
    sends.append(pltpu.make_async_copy(hot, hot_ref, out_sem.at[len(sends)]))
    sends[-1].start()
    for send in sends:
        send.wait()


def edge_kernel(own_ref, north_ref, south_ref, head_ref, tail_ref):
    lower = lax.broadcasted_iota(jnp.int32, (8, D), 0) < HALF
    pairs = [(north_ref, 0), (north_ref, 2)]
    pairs += [(own_ref, i) for i in range(0, RH, 2)]
    pairs += [(south_ref, 0), (south_ref, 2)]
    for n in range(0, len(pairs), 2):
        heads, tails = [], []
        for ref, i in pairs[n : n + 2]:
            first = [ref[i + k, 0:8].astype(jnp.float32) for k in range(2)]
            last = [ref[i + k, 24:32].astype(jnp.float32) for k in range(2)]
            heads.append(jnp.where(lower, first[0], pltpu.roll(first[1], HALF, 0)))
            tails.append(jnp.where(lower, pltpu.roll(last[0], HALF, 0), last[1]))
        head_ref[n * 8 : n * 8 + 16] = jnp.concatenate(heads, 0).astype(jnp.bfloat16)
        tail_ref[n * 8 : n * 8 + 16] = jnp.concatenate(tails, 0).astype(jnp.bfloat16)


def bias_kernel(table_ref, index_ref, gain_in, bias, gain_ref):
    gain_ref[...] = gain_in[...]
    lat = lax.axis_index("lat")
    lane = lax.broadcasted_iota(jnp.int32, (8, 128), 1)
    first = lane < WTOK
    key_row = (lane % WTOK) // WIN
    off_north = (lat == 0) & (key_row < HALF)
    off_south = (lat == lax.axis_size("lat") - 1) & (key_row >= HALF)
    tables = []
    for h in range(HEADS):
        parts = [table_ref[h : h + 1, c : c + 128] for c in (0, BIAS_ROWS - 128)]
        tables.append([jnp.broadcast_to(part, (8, 128)) for part in parts])
    for a in range(2):
        off = off_north if a == 0 else off_south
        for i in range(0, QROWS, 8):
            at = (QROWS if a == 0 else 0) + i
            idx = index_ref[at : at + 8, :]
            idx = jnp.concatenate([idx, idx], axis=1)
            high = idx >= 128
            inner = jnp.where(high, idx - (BIAS_ROWS - 128), idx)
            for h4 in range(4):
                found = []
                for h in (h4, h4 + 4):
                    lo = jnp.take_along_axis(tables[h][0], inner, axis=1)
                    hi = jnp.take_along_axis(tables[h][1], inner, axis=1)
                    found.append(jnp.where(high, hi, lo))
                value = jnp.where(first, found[0], found[1])
                to = a * 128 + h4 * QROWS + i
                bias[to : to + 8, :] = jnp.where(off, masked_score, value)


W_STEP = 256


def cap_kernel(x_ref, gain_ref, w_ref, out_ref, normed, qkv):
    n = SLOT_TOKENS
    gain = gain_ref[...]
    for i in range(0, SLOT_TOKENS, 32):
        normed[i : i + 32] = norm_rows(x_ref[i : i + 32].astype(jnp.float32), gain).astype(jnp.bfloat16)
    pick = (lax.broadcasted_iota(jnp.int32, (8, 128), 1) == 0).astype(jnp.bfloat16)
    first = lax.dot_general(
        pick, x_ref[:, 0:128], (((1,), (1,)), ((), ())), preferred_element_type=jnp.float32
    )
    empty = jnp.where(first[0:1] > EMPTY_ABOVE, masked_score, 0.0)
    for j in range(3 * HW // W_STEP):
        at = slice(j * W_STEP, j * W_STEP + W_STEP)
        part = jnp.dot(normed[...], w_ref[:, at], preferred_element_type=jnp.float32)
        qkv[:, at] = part.astype(jnp.bfloat16)
    low = lax.broadcasted_iota(jnp.int32, (n, 128), 1) < HD
    for pair in range(HEADS // 2):
        at = pair * 128
        q = qkv[:, at : at + 128] * jnp.bfloat16(HD ** (-0.5))
        k = qkv[:, HW + at : HW + at + 128]
        v = qkv[:, 2 * HW + at : 2 * HW + at + 128]
        mixed = []
        for half in range(2):
            mine = low if half == 0 else jnp.logical_not(low)
            qh = jnp.where(mine, q, jnp.zeros_like(q))
            s = lax.dot_general(qh, k, (((1,), (1,)), ((), ())), preferred_element_type=jnp.float32)
            s = s + empty
            raised = jnp.exp(s - jnp.max(s, axis=-1, keepdims=True))
            vh = jnp.where(mine, v, jnp.ones_like(v))
            both = jnp.dot(raised.astype(jnp.bfloat16), vh, preferred_element_type=jnp.float32)
            total = both[:, 127:128] if half == 0 else both[:, 0:1]
            mixed.append(both * (1.0 / total))
        out_ref[:, at : at + 128] = jnp.where(low, mixed[0], mixed[1]).astype(jnp.bfloat16)


def project(xs, xq, w_ref, qs, kv):
    for j in range(3 * HW // W_STEP):
        at = slice(j * W_STEP, j * W_STEP + W_STEP)
        if j * W_STEP < HW:
            qs[:, at] = jnp.dot(xq[...], w_ref[:, at], preferred_element_type=jnp.float32).astype(jnp.bfloat16)
        else:
            to = slice(j * W_STEP - HW, j * W_STEP - HW + W_STEP)
            kv[:, to] = jnp.dot(xs[...], w_ref[:, at], preferred_element_type=jnp.float32).astype(jnp.bfloat16)


def attend(qs, kv, bias, scores, weights, wout):
    count = qs.shape[0] // QROWS
    head = lax.broadcasted_iota(jnp.int32, (QROWS, HW), 1) // HD % 4
    blank = jnp.zeros((WTOK, HW // 2), jnp.bfloat16)

    def two_groups(x):
        top = jnp.concatenate([x[:, : HW // 2], blank], 1)
        low = jnp.concatenate([blank, x[:, HW // 2 :]], 1)
        return jnp.concatenate([top, low], 0)

    for n in range(count):
        q = qs[n * QROWS : n * QROWS + QROWS] * jnp.bfloat16(HD ** (-0.5))
        spread = jnp.concatenate([jnp.where(head == h, q, jnp.zeros_like(q)) for h in range(4)], 0)
        k = two_groups(kv[n * WTOK : n * WTOK + WTOK, 0:HW])
        s = lax.dot_general(spread, k, (((1,), (1,)), ((), ())), preferred_element_type=jnp.float32)
        a = n // (count // 2)
        scores[n * 128 : n * 128 + 128] = s + bias[a * 128 : a * 128 + 128]
    left = lax.broadcasted_iota(jnp.int32, (128, 128), 1) < WTOK
    for n in range(count):
        s = scores[n * 128 : n * 128 + 128]
        top0 = jnp.max(jnp.where(left, s, -jnp.inf), axis=-1, keepdims=True)
        top1 = jnp.max(jnp.where(left, -jnp.inf, s), axis=-1, keepdims=True)
        raised = jnp.exp(s - jnp.where(left, top0, top1))
        sum0 = jnp.sum(jnp.where(left, raised, 0.0), axis=-1, keepdims=True)
        sum1 = jnp.sum(jnp.where(left, 0.0, raised), axis=-1, keepdims=True)
        share = jnp.where(left, 1.0 / sum0, 1.0 / sum1)
        weights[n * 128 : n * 128 + 128] = (raised * share).astype(jnp.bfloat16)
    for n in range(count):
        v = two_groups(kv[n * WTOK : n * WTOK + WTOK, HW : 2 * HW])
        o = jnp.dot(weights[n * 128 : n * 128 + 128], v, preferred_element_type=jnp.float32)
        total = o[0:QROWS]
        for h in range(1, 4):
            total = jnp.where(head == h, o[h * QROWS : h * QROWS + QROWS], total)
        wout[n] = total


def place(blocks, per_row, r, n, xs, xq):
    a, wr = r // WIN, r % WIN
    both = jnp.concatenate(blocks, 0).astype(jnp.bfloat16)
    to = (a * per_row + n) * WTOK + wr * WIN
    xs[to : to + 16] = both
    if (wr >= HALF) == (a == 0):
        to = (a * per_row + n) * QROWS + (wr % HALF) * WIN
        xq[to : to + 16] = both


INNER = 3
OUTER = 2


def inner_kernel(
    own_ref, north_ref, south_ref, gain_ref, bias, w_ref, wout, rims_ref, xs, xq, kv, qs, scores, weights,
):
    gain = gain_ref[...]
    lower = lax.broadcasted_iota(jnp.int32, (8, D), 0) < HALF
    rows = [(north_ref, i) for i in range(HALF)] + [(own_ref, i) for i in range(RH)]
    rows += [(south_ref, i) for i in range(HALF)]
    for r in range(0, RH + WIN, 2):
        turned = []
        for ref, i in rows[r : r + 2]:
            normed = norm_rows(ref[i].astype(jnp.float32), gain)
            turned.append([pltpu.roll(normed[j * 8 : j * 8 + 8], HALF, 0) for j in range(4)])
        for n in range(INNER):
            place([jnp.where(lower, row[n], row[n + 1]) for row in turned], INNER, r, n, xs, xq)
        for side in range(2):
            both = jnp.concatenate([row[3 * side] for row in turned], 0)
            rims_ref[side, r * 8 : r * 8 + 16] = both.astype(jnp.bfloat16)
    project(xs, xq, w_ref, qs, kv)
    attend(qs, kv, bias, scores, weights, wout)


def outer_kernel(
    left_ref, right_ref, rims_ref, inner_ref, gain_ref, bias, hot_ref, w_ref,
    out_ref, cap_ref, undo_ref, xs, xq, kv, qs, scores, weights, wout, edges, full,
):
    gain = gain_ref[...]
    lat = lax.axis_index("lat")

    polar = (lat == 0) | (lat == lax.axis_size("lat") - 1)
    undo = jnp.transpose(hot_ref[...].astype(jnp.float32))
    undo_ref[...] = jnp.where(polar, undo, 0.0).astype(jnp.bfloat16)

    for side, ref in enumerate((left_ref, right_ref)):
        for i in range(0, 64, 32):
            edges[side, i : i + 32] = norm_rows(ref[i : i + 32].astype(jnp.float32), gain)
    lower = lax.broadcasted_iota(jnp.int32, (8, D), 0) < HALF
    for r in range(0, RH + WIN, 2):
        lo = edges[0, r * 4 : r * 4 + 8]
        hi = edges[1, r * 4 : r * 4 + 8]
        lows, highs = [lo, pltpu.roll(lo, HALF, 0)], [pltpu.roll(hi, HALF, 0), hi]
        heads = rims_ref[0, r * 8 : r * 8 + 16].astype(jnp.float32)
        tails = rims_ref[1, r * 8 : r * 8 + 16].astype(jnp.float32)
        place([jnp.where(lower, lows[k], heads[k * 8 : k * 8 + 8]) for k in range(2)], OUTER, r, 0, xs, xq)
        place([jnp.where(lower, tails[k * 8 : k * 8 + 8], highs[k]) for k in range(2)], OUTER, r, 1, xs, xq)
    project(xs, xq, w_ref, qs, kv)
    attend(qs, kv, bias, scores, weights, wout)

    lower = lax.broadcasted_iota(jnp.int32, (8, HW), 0) < HALF
    for r in range(RH):
        a, wr = r // HALF, r % HALF
        at = slice(wr * WIN, wr * WIN + WIN)
        parts = [wout[a * OUTER, at]]
        parts += [inner_ref[a * INNER + n, at] for n in range(INNER)]
        parts += [wout[a * OUTER + 1, at]]
        turned = [pltpu.roll(part, HALF, 0) for part in parts]
        for j in range(4):
            to = r * RW + j * 8
            full[to : to + 8] = jnp.where(lower, turned[j], turned[j + 1])
    out_ref[...] = full[...].astype(jnp.bfloat16)
    cap_ref[...] = jnp.where(lat == 0, full[0:CAP_TOKENS], full[CAP_TOKENS:])


def join_kernel(win_ref, back_ref, undo_ref, out_in, out_ref, mixed, sem):
    cap = jnp.dot(undo_ref[...], back_ref[...], preferred_element_type=jnp.float32)
    mixed[...] = (win_ref[...] + cap).astype(jnp.bfloat16)
    start = jnp.where(lax.axis_index("lat") == 0, 0, CAP_TOKENS)
    copy = pltpu.make_async_copy(mixed, out_ref.at[pl.ds(pl.multiple_of(start, CAP_TOKENS), CAP_TOKENS)], sem)
    copy.start()
    copy.wait()


def sds(shape, dtype):
    return jax.ShapeDtypeStruct(shape, dtype)


def call(kernel, outs, ins, out_specs, scratch, vmem, flops, nbytes, trans=0, aliases=None):
    return pl.pallas_call(
        kernel,
        out_shape=outs,
        in_specs=ins,
        out_specs=out_specs,
        scratch_shapes=scratch,
        compiler_params=pltpu.CompilerParams(vmem_limit_bytes=vmem),
        input_output_aliases=aliases or {},
        cost_estimate=pl.CostEstimate(flops=flops, bytes_accessed=nbytes, transcendentals=trans),
    )


def exchange(block):
    return lax.all_to_all(block, "lon", split_axis=0, concat_axis=0, tiled=True)


def layer(tokens, ln_gain, w_qkv, bias_table, bias_index, cap_group):
    lat_count = lax.axis_size("lat")
    lon_count = lax.axis_size("lon")
    bf16, f32 = jnp.bfloat16, jnp.float32
    gain = ln_gain.reshape(1, D)
    groups = cap_group.transpose(0, 2, 3, 1)

    packed, hot = call(
        pack_kernel, (sds((SLOT_TOKENS, D), bf16), sds((SLOT_TOKENS, CAP_TOKENS), bf16)),
        [aspec(), hspec()], (hspec(), hspec()),
        [
            SMEM((2, CAP, 1, TILE_COLS), jnp.int32),
            VMEM((CAP, RW, D), bf16),
            VMEM((SLOT_TOKENS, D), bf16),
            VMEM((SLOT_TOKENS, CAP_TOKENS), bf16),
            pltpu.SemaphoreType.DMA,
            pltpu.SemaphoreType.DMA,
            pltpu.SemaphoreType.DMA((SLOT_TOKENS // PACK_STEP + 1,)),
        ],
        PACK_VMEM, 2 * SLOT_TOKENS * CAP_TOKENS * D, 1 << 20,
    )(groups, tokens)
    arrived = exchange(packed.reshape(lon_count, MOST * TW, D)).reshape(SLOT_TOKENS, D)

    down = [(i, i + 1) for i in range(lat_count - 1)]
    up = [(i + 1, i) for i in range(lat_count - 1)]
    east = [(i, (i + 1) % lon_count) for i in range(lon_count)]
    west = [((i + 1) % lon_count, i) for i in range(lon_count)]
    tied, _ = lax.optimization_barrier((tokens, packed))
    north = lax.ppermute(tied[RH - HALF :], "lat", down)
    south = lax.ppermute(tied[:HALF], "lat", up)
    bias, gain = call(
        bias_kernel, (sds((2 * 128, 128), f32), sds((1, D), f32)), [vspec()] * 3, (vspec(), vspec()), [],
        SOME_VMEM, 1 << 18, 1 << 18,
    )(bias_table, bias_index, gain)
    side = sds(((RH + WIN) * HALF, D), bf16)
    head, tail = call(
        edge_kernel, (side, side), [vspec()] * 3, (vspec(), vspec()), [],
        SOME_VMEM, 4 << 30, 3 << 19,
    )(tokens, north, south)
    left = lax.ppermute(tail, "lon", east)
    right = lax.ppermute(head, "lon", west)

    cap_result = call(
        cap_kernel, sds((SLOT_TOKENS, HW), bf16),
        [vspec()] * 3, vspec(),
        [VMEM((SLOT_TOKENS, D), bf16), VMEM((SLOT_TOKENS, 3 * HW), bf16)],
        SOME_VMEM, 1100 << 20, 4 << 20, 1 << 19,
    )(arrived, gain, w_qkv)
    returned = exchange(cap_result.reshape(lon_count, MOST * TW, HW)).reshape(SLOT_TOKENS, HW)

    def scratch(count):
        return [
            VMEM((count * WTOK, D), bf16),
            VMEM((count * QROWS, D), bf16),
            VMEM((count * WTOK, 2 * HW), bf16),
            VMEM((count * QROWS, HW), bf16),
            VMEM((count * 128, 128), f32),
            VMEM((count * 128, 128), bf16),
        ]

    inner, rims = call(
        inner_kernel,
        (sds((2 * INNER, QROWS, HW), f32), sds((2, (RH + WIN) * 8, D), bf16)),
        [vspec()] * 6, (vspec(), vspec()), scratch(2 * INNER),
        SOME_VMEM, 1400 << 20, 5 << 20, 1 << 17,
    )(tokens, north, south, gain, bias, w_qkv)
    win_out, cap_rows, undo = call(
        outer_kernel,
        (sds((RH * RW, HW), bf16), sds((CAP_TOKENS, HW), f32), sds((CAP_TOKENS, SLOT_TOKENS), bf16)),
        [vspec()] * 8, (vspec(),) * 3,
        scratch(2 * OUTER)
        + [VMEM((2 * OUTER, QROWS, HW), f32), VMEM((2, 64, D), f32), VMEM((RH * RW, HW), f32)],
        SOME_VMEM, 900 << 20, 5 << 20, 1 << 17,
    )(left, right, rims, inner, gain, bias, hot, w_qkv)
    mixed = call(
        join_kernel, sds((RH * RW, HW), bf16),
        [vspec()] * 3 + [aspec()], aspec(),
        [VMEM((CAP_TOKENS, HW), bf16), pltpu.SemaphoreType.DMA],
        8 << 20, 2 * CAP_TOKENS * SLOT_TOKENS * HW, 1 << 19, aliases={3: 0},
    )(cap_rows, returned, undo, win_out)
    return mixed.reshape(RH, RW, HW)


def solution(mesh):
    placed = (P("lat", "lon", None), P(), P(), P(), P(), P(None, "lon", None, None))
    return jax.shard_map(layer, mesh=mesh, in_specs=placed, out_specs=P("lat", "lon", None), check_vma=False)
```

```python
import jax
import jax.numpy as jnp
from jax import lax
from jax.experimental import pallas as pl
from jax.experimental.pallas import tpu as pltpu
from jax.sharding import PartitionSpec as P


D = 1024
HEADS = 8
HD = 64
WIN = 8
TW = 4
CAP = 4
RH = 8
RW = 32
HW = 512
HALF = 4
BIAS_ROWS = 225
TILES_DEV = 32
TILE_COLS = RW // TW
GROUPS = 32
MOST = 2
SLOT_TOKENS = GROUPS * MOST * TW
CAP_TOKENS = CAP * RW
WTOK = WIN * WIN
QROWS = HALF * WIN

epsilon = 1e-05
masked_score = -1e30
EMPTY = 128.0
EMPTY_ABOVE = 64.0

ALL_VMEM = 67043328
PACK_VMEM = ALL_VMEM - 409600
SOME_VMEM = 24 << 20

VMEM = pltpu.VMEM
SMEM = pltpu.SMEM


def vspec():
    return pl.BlockSpec(memory_space=VMEM)


def aspec():
    return pl.BlockSpec(memory_space=pl.ANY)


def hspec():
    return pl.BlockSpec(memory_space=pltpu.HBM)


def norm_rows(values, gain):
    center = jnp.mean(values, axis=-1, keepdims=True)
    shifted = values - center
    spread = jnp.mean(jnp.square(shifted), axis=-1, keepdims=True)
    return shifted * lax.rsqrt(spread + epsilon) * gain


def slot_rows(group_ref, pole, lane):
    tile = lane // TW
    names = [group_ref[pole, t // TILE_COLS, 0, t % TILE_COLS] for t in range(TILES_DEV)]
    group = jnp.zeros_like(lane)
    for t in range(TILES_DEV):
        group = jnp.where(tile == t, names[t], group)
    rank = jnp.zeros_like(lane)
    for t in range(TILES_DEV):
        same = (group == names[t]) & (tile > t)
        rank = rank + same.astype(jnp.int32)
    return (group * MOST + rank) * TW + lane % TW


PACK_STEP = 64


def pack_kernel(names_ref, tokens_ref, send_ref, hot_ref, group_ref, rows, out, hot, name_sem, sem, out_sem):
    north = lax.axis_index("lat") == 0
    pole = jnp.where(north, 0, 1)
    start = jnp.where(north, 0, RH - CAP)
    names = pltpu.make_async_copy(names_ref, group_ref, name_sem)
    names.start()
    copy = pltpu.make_async_copy(tokens_ref.at[pl.ds(start, CAP)], rows, sem)
    copy.start()
    names.wait()
    lane = lax.broadcasted_iota(jnp.int32, (8, CAP_TOKENS), 1)
    slot = slot_rows(group_ref, pole, lane)[0:1]
    copy.wait()
    x = rows[...].reshape(CAP_TOKENS, D)
    sends = []
    for n in range(SLOT_TOKENS // PACK_STEP):
        at = pl.ds(n * PACK_STEP, PACK_STEP)
        hit = lax.broadcasted_iota(jnp.int32, (PACK_STEP, CAP_TOKENS), 0) + n * PACK_STEP == slot
        here = hit.astype(jnp.float32)
        filled = jnp.max(here, axis=1, keepdims=True) > 0.5
        here = here.astype(jnp.bfloat16)
        hot[at, :] = here
        moved = jnp.dot(here, x, preferred_element_type=jnp.float32)
        out[at, :] = jnp.where(filled, moved, EMPTY).astype(jnp.bfloat16)
        sends.append(pltpu.make_async_copy(out.at[at], send_ref.at[at], out_sem.at[n]))
        sends[n].start()
    sends.append(pltpu.make_async_copy(hot, hot_ref, out_sem.at[len(sends)]))
    sends[-1].start()
    for send in sends:
        send.wait()


def edge_kernel(own_ref, north_ref, south_ref, head_ref, tail_ref):
    lower = lax.broadcasted_iota(jnp.int32, (8, D), 0) < HALF
    pairs = [(north_ref, 0), (north_ref, 2)]
    pairs += [(own_ref, i) for i in range(0, RH, 2)]
    pairs += [(south_ref, 0), (south_ref, 2)]
    for n in range(0, len(pairs), 2):
        heads, tails = [], []
        for ref, i in pairs[n : n + 2]:
            first = [ref[i + k, 0:8].astype(jnp.float32) for k in range(2)]
            last = [ref[i + k, 24:32].astype(jnp.float32) for k in range(2)]
            heads.append(jnp.where(lower, first[0], pltpu.roll(first[1], HALF, 0)))
            tails.append(jnp.where(lower, pltpu.roll(last[0], HALF, 0), last[1]))
        head_ref[n * 8 : n * 8 + 16] = jnp.concatenate(heads, 0).astype(jnp.bfloat16)
        tail_ref[n * 8 : n * 8 + 16] = jnp.concatenate(tails, 0).astype(jnp.bfloat16)


def bias_kernel(table_ref, index_ref, gain_in, hot_ref, own_ref, bias, gain_ref, undo_ref, normed_ref):
    gain = gain_in[...]
    gain_ref[...] = gain
    for r in range(RH):
        normed_ref[r] = norm_rows(own_ref[r].astype(jnp.float32), gain).astype(jnp.bfloat16)
    lat = lax.axis_index("lat")
    polar = (lat == 0) | (lat == lax.axis_size("lat") - 1)
    undo = jnp.transpose(hot_ref[...].astype(jnp.float32))
    undo_ref[...] = jnp.where(polar, undo, 0.0).astype(jnp.bfloat16)
    lane = lax.broadcasted_iota(jnp.int32, (8, 128), 1)
    first = lane < WTOK
    key_row = (lane % WTOK) // WIN
    off_north = (lat == 0) & (key_row < HALF)
    off_south = (lat == lax.axis_size("lat") - 1) & (key_row >= HALF)
    tables = []
    for h in range(HEADS):
        parts = [table_ref[h : h + 1, c : c + 128] for c in (0, BIAS_ROWS - 128)]
        tables.append([jnp.broadcast_to(part, (8, 128)) for part in parts])
    for a in range(2):
        off = off_north if a == 0 else off_south
        for i in range(0, QROWS, 8):
            at = (QROWS if a == 0 else 0) + i
            idx = index_ref[at : at + 8, :]
            idx = jnp.concatenate([idx, idx], axis=1)
            high = idx >= 128
            inner = jnp.where(high, idx - (BIAS_ROWS - 128), idx)
            for h4 in range(4):
                found = []
                for h in (h4, h4 + 4):
                    lo = jnp.take_along_axis(tables[h][0], inner, axis=1)
                    hi = jnp.take_along_axis(tables[h][1], inner, axis=1)
                    found.append(jnp.where(high, hi, lo))
                value = jnp.where(first, found[0], found[1])
                to = a * 128 + h4 * QROWS + i
                bias[to : to + 8, :] = jnp.where(off, masked_score, value)


W_STEP = 256


def cap_kernel(x_ref, gain_ref, w_ref, out_ref, normed, qkv):
    n = SLOT_TOKENS
    gain = gain_ref[...]
    for i in range(0, SLOT_TOKENS, 32):
        normed[i : i + 32] = norm_rows(x_ref[i : i + 32].astype(jnp.float32), gain).astype(jnp.bfloat16)
    pick = (lax.broadcasted_iota(jnp.int32, (8, 128), 1) == 0).astype(jnp.bfloat16)
    first = lax.dot_general(
        pick, x_ref[:, 0:128], (((1,), (1,)), ((), ())), preferred_element_type=jnp.float32
    )
    empty = jnp.where(first[0:1] > EMPTY_ABOVE, masked_score, 0.0)
    for j in range(3 * HW // W_STEP):
        at = slice(j * W_STEP, j * W_STEP + W_STEP)
        part = jnp.dot(normed[...], w_ref[:, at], preferred_element_type=jnp.float32)
        qkv[:, at] = part.astype(jnp.bfloat16)
    low = lax.broadcasted_iota(jnp.int32, (n, 128), 1) < HD
    for pair in range(HEADS // 2):
        at = pair * 128
        q = qkv[:, at : at + 128] * jnp.bfloat16(HD ** (-0.5))
        k = qkv[:, HW + at : HW + at + 128]
        v = qkv[:, 2 * HW + at : 2 * HW + at + 128]
        mixed = []
        for half in range(2):
            mine = low if half == 0 else jnp.logical_not(low)
            qh = jnp.where(mine, q, jnp.zeros_like(q))
            s = lax.dot_general(qh, k, (((1,), (1,)), ((), ())), preferred_element_type=jnp.float32)
            s = s + empty
            raised = jnp.exp(s - jnp.max(s, axis=-1, keepdims=True))
            both = jnp.dot(raised.astype(jnp.bfloat16), v, preferred_element_type=jnp.float32)
            mixed.append(both * (1.0 / jnp.sum(raised, axis=-1, keepdims=True)))
        out_ref[:, at : at + 128] = jnp.where(low, mixed[0], mixed[1]).astype(jnp.bfloat16)


def project(xs, xq, w_ref, qs, kv):
    for j in range(3 * HW // W_STEP):
        at = slice(j * W_STEP, j * W_STEP + W_STEP)
        if j * W_STEP < HW:
            qs[:, at] = jnp.dot(xq[...], w_ref[:, at], preferred_element_type=jnp.float32).astype(jnp.bfloat16)
        else:
            to = slice(j * W_STEP - HW, j * W_STEP - HW + W_STEP)
            kv[:, to] = jnp.dot(xs[...], w_ref[:, at], preferred_element_type=jnp.float32).astype(jnp.bfloat16)


def attend(qs, kv, bias, scores, weights, wout):
    count = qs.shape[0] // QROWS
    head = lax.broadcasted_iota(jnp.int32, (QROWS, HW), 1) // HD % 4
    blank = jnp.zeros((WTOK, HW // 2), jnp.bfloat16)

    def two_groups(x):
        top = jnp.concatenate([x[:, : HW // 2], blank], 1)
        low = jnp.concatenate([blank, x[:, HW // 2 :]], 1)
        return jnp.concatenate([top, low], 0)

    for n in range(count):
        q = qs[n * QROWS : n * QROWS + QROWS] * jnp.bfloat16(HD ** (-0.5))
        spread = jnp.concatenate([jnp.where(head == h, q, jnp.zeros_like(q)) for h in range(4)], 0)
        k = two_groups(kv[n * WTOK : n * WTOK + WTOK, 0:HW])
        s = lax.dot_general(spread, k, (((1,), (1,)), ((), ())), preferred_element_type=jnp.float32)
        a = n // (count // 2)
        scores[n * 128 : n * 128 + 128] = s + bias[a * 128 : a * 128 + 128]
    left = lax.broadcasted_iota(jnp.int32, (128, 128), 1) < WTOK
    for n in range(count):
        s = scores[n * 128 : n * 128 + 128]
        top0 = jnp.max(jnp.where(left, s, -jnp.inf), axis=-1, keepdims=True)
        top1 = jnp.max(jnp.where(left, -jnp.inf, s), axis=-1, keepdims=True)
        raised = jnp.exp(s - jnp.where(left, top0, top1))
        sum0 = jnp.sum(jnp.where(left, raised, 0.0), axis=-1, keepdims=True)
        sum1 = jnp.sum(jnp.where(left, 0.0, raised), axis=-1, keepdims=True)
        share = jnp.where(left, 1.0 / sum0, 1.0 / sum1)
        weights[n * 128 : n * 128 + 128] = (raised * share).astype(jnp.bfloat16)
    for n in range(count):
        v = two_groups(kv[n * WTOK : n * WTOK + WTOK, HW : 2 * HW])
        o = jnp.dot(weights[n * 128 : n * 128 + 128], v, preferred_element_type=jnp.float32)
        total = o[0:QROWS]
        for h in range(1, 4):
            total = jnp.where(head == h, o[h * QROWS : h * QROWS + QROWS], total)
        wout[n] = total


def place(blocks, per_row, r, n, xs, xq):
    a, wr = r // WIN, r % WIN
    both = jnp.concatenate(blocks, 0).astype(jnp.bfloat16)
    to = (a * per_row + n) * WTOK + wr * WIN
    xs[to : to + 16] = both
    if (wr >= HALF) == (a == 0):
        to = (a * per_row + n) * QROWS + (wr % HALF) * WIN
        xq[to : to + 16] = both


INNER = 3
OUTER = 2


def inner_kernel(
    own_ref, north_ref, south_ref, gain_ref, bias, w_ref, wout, rims_ref, xs, xq, kv, qs, scores, weights,
):
    gain = gain_ref[...]
    lower = lax.broadcasted_iota(jnp.int32, (8, D), 0) < HALF
    rows = [(north_ref, i) for i in range(HALF)] + [(own_ref, i) for i in range(RH)]
    rows += [(south_ref, i) for i in range(HALF)]
    for r in range(0, RH + WIN, 2):
        turned = []
        for ref, i in rows[r : r + 2]:
            normed = ref[i].astype(jnp.float32)
            if ref is not own_ref:
                normed = norm_rows(normed, gain)
            turned.append([pltpu.roll(normed[j * 8 : j * 8 + 8], HALF, 0) for j in range(4)])
        for n in range(INNER):
            place([jnp.where(lower, row[n], row[n + 1]) for row in turned], INNER, r, n, xs, xq)
        for side in range(2):
            both = jnp.concatenate([row[3 * side] for row in turned], 0)
            rims_ref[side, r * 8 : r * 8 + 16] = both.astype(jnp.bfloat16)
    project(xs, xq, w_ref, qs, kv)
    attend(qs, kv, bias, scores, weights, wout)


def outer_kernel(
    left_ref, right_ref, rims_ref, inner_ref, gain_ref, bias, w_ref, out_ref, cap_ref, xs, xq, kv, qs, scores, weights, wout, edges, full,
):
    gain = gain_ref[...]
    lat = lax.axis_index("lat")

    for side, ref in enumerate((left_ref, right_ref)):
        for i in range(0, 64, 32):
            edges[side, i : i + 32] = norm_rows(ref[i : i + 32].astype(jnp.float32), gain)
    lower = lax.broadcasted_iota(jnp.int32, (8, D), 0) < HALF
    for r in range(0, RH + WIN, 2):
        lo = edges[0, r * 4 : r * 4 + 8]
        hi = edges[1, r * 4 : r * 4 + 8]
        lows, highs = [lo, pltpu.roll(lo, HALF, 0)], [pltpu.roll(hi, HALF, 0), hi]
        heads = rims_ref[0, r * 8 : r * 8 + 16].astype(jnp.float32)
        tails = rims_ref[1, r * 8 : r * 8 + 16].astype(jnp.float32)
        place([jnp.where(lower, lows[k], heads[k * 8 : k * 8 + 8]) for k in range(2)], OUTER, r, 0, xs, xq)
        place([jnp.where(lower, tails[k * 8 : k * 8 + 8], highs[k]) for k in range(2)], OUTER, r, 1, xs, xq)
    project(xs, xq, w_ref, qs, kv)
    attend(qs, kv, bias, scores, weights, wout)

    lower = lax.broadcasted_iota(jnp.int32, (8, HW), 0) < HALF
    for r in range(RH):
        a, wr = r // HALF, r % HALF
        at = slice(wr * WIN, wr * WIN + WIN)
        parts = [wout[a * OUTER, at]]
        parts += [inner_ref[a * INNER + n, at] for n in range(INNER)]
        parts += [wout[a * OUTER + 1, at]]
        turned = [pltpu.roll(part, HALF, 0) for part in parts]
        for j in range(4):
            to = r * RW + j * 8
            full[to : to + 8] = jnp.where(lower, turned[j], turned[j + 1])
    out_ref[...] = full[...].astype(jnp.bfloat16)
    cap_ref[...] = jnp.where(lat == 0, full[0:CAP_TOKENS], full[CAP_TOKENS:])


def join_kernel(win_ref, back_ref, undo_ref, out_in, out_ref, mixed, sem):
    cap = jnp.dot(undo_ref[...], back_ref[...], preferred_element_type=jnp.float32)
    mixed[...] = (win_ref[...] + cap).astype(jnp.bfloat16)
    start = jnp.where(lax.axis_index("lat") == 0, 0, CAP_TOKENS)
    copy = pltpu.make_async_copy(mixed, out_ref.at[pl.ds(pl.multiple_of(start, CAP_TOKENS), CAP_TOKENS)], sem)
    copy.start()
    copy.wait()


def sds(shape, dtype):
    return jax.ShapeDtypeStruct(shape, dtype)


def call(kernel, outs, ins, out_specs, scratch, vmem, flops, nbytes, trans=0, aliases=None):
    return pl.pallas_call(
        kernel,
        out_shape=outs,
        in_specs=ins,
        out_specs=out_specs,
        scratch_shapes=scratch,
        compiler_params=pltpu.CompilerParams(vmem_limit_bytes=vmem),
        input_output_aliases=aliases or {},
        cost_estimate=pl.CostEstimate(flops=flops, bytes_accessed=nbytes, transcendentals=trans),
    )


def exchange(block):
    return lax.all_to_all(block, "lon", split_axis=0, concat_axis=0, tiled=True)


def layer(tokens, ln_gain, w_qkv, bias_table, bias_index, cap_group):
    lat_count = lax.axis_size("lat")
    lon_count = lax.axis_size("lon")
    bf16, f32 = jnp.bfloat16, jnp.float32
    gain = ln_gain.reshape(1, D)
    groups = cap_group.transpose(0, 2, 3, 1)

    packed, hot = call(
        pack_kernel, (sds((SLOT_TOKENS, D), bf16), sds((SLOT_TOKENS, CAP_TOKENS), bf16)),
        [aspec(), hspec()], (hspec(), hspec()),
        [
            SMEM((2, CAP, 1, TILE_COLS), jnp.int32),
            VMEM((CAP, RW, D), bf16),
            VMEM((SLOT_TOKENS, D), bf16),
            VMEM((SLOT_TOKENS, CAP_TOKENS), bf16),
            pltpu.SemaphoreType.DMA,
            pltpu.SemaphoreType.DMA,
            pltpu.SemaphoreType.DMA((SLOT_TOKENS // PACK_STEP + 1,)),
        ],
        PACK_VMEM, 2 * SLOT_TOKENS * CAP_TOKENS * D, 1 << 20,
    )(groups, tokens)
    arrived = exchange(packed.reshape(lon_count, MOST * TW, D)).reshape(SLOT_TOKENS, D)

    down = [(i, i + 1) for i in range(lat_count - 1)]
    up = [(i + 1, i) for i in range(lat_count - 1)]
    east = [(i, (i + 1) % lon_count) for i in range(lon_count)]
    west = [((i + 1) % lon_count, i) for i in range(lon_count)]
    tied, _ = lax.optimization_barrier((tokens, packed))
    north = lax.ppermute(tied[RH - HALF :], "lat", down)
    south = lax.ppermute(tied[:HALF], "lat", up)
    bias, gain, undo, normed = call(
        bias_kernel,
        (
            sds((2 * 128, 128), f32), sds((1, D), f32), sds((CAP_TOKENS, SLOT_TOKENS), bf16),
            sds((RH, RW, D), bf16),
        ),
        [vspec()] * 5, (vspec(),) * 4, [],
        SOME_VMEM, 1 << 20, 3 << 19,
    )(bias_table, bias_index, gain, hot, tokens)
    side = sds(((RH + WIN) * HALF, D), bf16)
    head, tail = call(
        edge_kernel, (side, side), [vspec()] * 3, (vspec(), vspec()), [],
        SOME_VMEM, 4 << 30, 3 << 19,
    )(tokens, north, south)
    left = lax.ppermute(tail, "lon", east)
    right = lax.ppermute(head, "lon", west)

    cap_result = call(
        cap_kernel, sds((SLOT_TOKENS, HW), bf16),
        [vspec()] * 3, vspec(),
        [VMEM((SLOT_TOKENS, D), bf16), VMEM((SLOT_TOKENS, 3 * HW), bf16)],
        SOME_VMEM, 1100 << 20, 4 << 20, 1 << 19,
    )(arrived, gain, w_qkv)
    returned = exchange(cap_result.reshape(lon_count, MOST * TW, HW)).reshape(SLOT_TOKENS, HW)

    def scratch(count):
        return [
            VMEM((count * WTOK, D), bf16),
            VMEM((count * QROWS, D), bf16),
            VMEM((count * WTOK, 2 * HW), bf16),
            VMEM((count * QROWS, HW), bf16),
            VMEM((count * 128, 128), f32),
            VMEM((count * 128, 128), bf16),
        ]

    inner, rims = call(
        inner_kernel,
        (sds((2 * INNER, QROWS, HW), f32), sds((2, (RH + WIN) * 8, D), bf16)),
        [vspec()] * 6, (vspec(), vspec()), scratch(2 * INNER),
        SOME_VMEM, 1400 << 20, 5 << 20, 1 << 17,
    )(normed, north, south, gain, bias, w_qkv)
    win_out, cap_rows = call(
        outer_kernel,
        (sds((RH * RW, HW), bf16), sds((CAP_TOKENS, HW), f32)), [vspec()] * 7, (vspec(),) * 2,
        scratch(2 * OUTER)
        + [VMEM((2 * OUTER, QROWS, HW), f32), VMEM((2, 64, D), f32), VMEM((RH * RW, HW), f32)],
        SOME_VMEM, 900 << 20, 5 << 20, 1 << 17,
    )(left, right, rims, inner, gain, bias, w_qkv)
    mixed = call(
        join_kernel, sds((RH * RW, HW), bf16),
        [vspec()] * 3 + [aspec()], aspec(),
        [VMEM((CAP_TOKENS, HW), bf16), pltpu.SemaphoreType.DMA],
        8 << 20, 2 * CAP_TOKENS * SLOT_TOKENS * HW, 1 << 19, aliases={3: 0},
    )(cap_rows, returned, undo, win_out)
    return mixed.reshape(RH, RW, HW)


def solution(mesh):
    placed = (P("lat", "lon", None), P(), P(), P(), P(), P(None, "lon", None, None))
    return jax.shard_map(layer, mesh=mesh, in_specs=placed, out_specs=P("lat", "lon", None), check_vma=False)
```

```python
import jax
import jax.numpy as jnp
from jax import lax
from jax.experimental import pallas as pl
from jax.experimental.pallas import tpu as pltpu
from jax.sharding import PartitionSpec as P


D = 1024
HEADS = 8
HD = 64
WIN = 8
TW = 4
CAP = 4
RH = 8
RW = 32
HW = 512
HALF = 4
BIAS_ROWS = 225
TILES_DEV = 32
TILE_COLS = RW // TW
GROUPS = 32
MOST = 2
SLOT_TOKENS = GROUPS * MOST * TW
CAP_TOKENS = CAP * RW
WTOK = WIN * WIN
QROWS = HALF * WIN

epsilon = 1e-05
masked_score = -1e30
EMPTY = 128.0
EMPTY_ABOVE = 64.0

ALL_VMEM = 67043328
PACK_VMEM = ALL_VMEM - 409600
SOME_VMEM = 24 << 20

VMEM = pltpu.VMEM
SMEM = pltpu.SMEM


def vspec():
    return pl.BlockSpec(memory_space=VMEM)


def aspec():
    return pl.BlockSpec(memory_space=pl.ANY)


def hspec():
    return pl.BlockSpec(memory_space=pltpu.HBM)


def norm_rows(values, gain):
    center = jnp.mean(values, axis=-1, keepdims=True)
    shifted = values - center
    spread = jnp.mean(jnp.square(shifted), axis=-1, keepdims=True)
    return shifted * lax.rsqrt(spread + epsilon) * gain


def slot_rows(group_ref, pole, lane):
    tile = lane // TW
    names = [group_ref[pole, t // TILE_COLS, 0, t % TILE_COLS] for t in range(TILES_DEV)]
    group = jnp.zeros_like(lane)
    for t in range(TILES_DEV):
        group = jnp.where(tile == t, names[t], group)
    rank = jnp.zeros_like(lane)
    for t in range(TILES_DEV):
        same = (group == names[t]) & (tile > t)
        rank = rank + same.astype(jnp.int32)
    return (group * MOST + rank) * TW + lane % TW


PACK_STEP = 64


def pack_kernel(names_ref, tokens_ref, send_ref, hot_ref, group_ref, rows, out, hot, name_sem, sem, out_sem):
    north = lax.axis_index("lat") == 0
    pole = jnp.where(north, 0, 1)
    start = jnp.where(north, 0, RH - CAP)
    names = pltpu.make_async_copy(names_ref, group_ref, name_sem)
    names.start()
    copy = pltpu.make_async_copy(tokens_ref.at[pl.ds(start, CAP)], rows, sem)
    copy.start()
    names.wait()
    lane = lax.broadcasted_iota(jnp.int32, (8, CAP_TOKENS), 1)
    slot = slot_rows(group_ref, pole, lane)[0:1]
    copy.wait()
    x = rows[...].reshape(CAP_TOKENS, D)
    sends = []
    for n in range(SLOT_TOKENS // PACK_STEP):
        at = pl.ds(n * PACK_STEP, PACK_STEP)
        hit = lax.broadcasted_iota(jnp.int32, (PACK_STEP, CAP_TOKENS), 0) + n * PACK_STEP == slot
        here = hit.astype(jnp.float32)
        filled = jnp.max(here, axis=1, keepdims=True) > 0.5
        here = here.astype(jnp.bfloat16)
        hot[at, :] = here
        moved = jnp.dot(here, x, preferred_element_type=jnp.float32)
        out[at, :] = jnp.where(filled, moved, EMPTY).astype(jnp.bfloat16)
        sends.append(pltpu.make_async_copy(out.at[at], send_ref.at[at], out_sem.at[n]))
        sends[n].start()
    sends.append(pltpu.make_async_copy(hot, hot_ref, out_sem.at[len(sends)]))
    sends[-1].start()
    for send in sends:
        send.wait()


def edge_kernel(own_ref, north_ref, south_ref, head_ref, tail_ref):
    lower = lax.broadcasted_iota(jnp.int32, (8, D), 0) < HALF
    pairs = [(north_ref, 0), (north_ref, 2)]
    pairs += [(own_ref, i) for i in range(0, RH, 2)]
    pairs += [(south_ref, 0), (south_ref, 2)]
    for n in range(0, len(pairs), 2):
        heads, tails = [], []
        for ref, i in pairs[n : n + 2]:
            first = [ref[i + k, 0:8].astype(jnp.float32) for k in range(2)]
            last = [ref[i + k, 24:32].astype(jnp.float32) for k in range(2)]
            heads.append(jnp.where(lower, first[0], pltpu.roll(first[1], HALF, 0)))
            tails.append(jnp.where(lower, pltpu.roll(last[0], HALF, 0), last[1]))
        head_ref[n * 8 : n * 8 + 16] = jnp.concatenate(heads, 0).astype(jnp.bfloat16)
        tail_ref[n * 8 : n * 8 + 16] = jnp.concatenate(tails, 0).astype(jnp.bfloat16)


def bias_kernel(table_ref, index_ref, gain_in, bias, gain_ref):
    gain_ref[...] = gain_in[...]
    lat = lax.axis_index("lat")
    lane = lax.broadcasted_iota(jnp.int32, (8, 128), 1)
    first = lane < WTOK
    key_row = (lane % WTOK) // WIN
    off_north = (lat == 0) & (key_row < HALF)
    off_south = (lat == lax.axis_size("lat") - 1) & (key_row >= HALF)
    tables = []
    for h in range(HEADS):
        parts = [table_ref[h : h + 1, c : c + 128] for c in (0, BIAS_ROWS - 128)]
        tables.append([jnp.broadcast_to(part, (8, 128)) for part in parts])
    for a in range(2):
        off = off_north if a == 0 else off_south
        for i in range(0, QROWS, 8):
            at = (QROWS if a == 0 else 0) + i
            idx = index_ref[at : at + 8, :]
            idx = jnp.concatenate([idx, idx], axis=1)
            high = idx >= 128
            inner = jnp.where(high, idx - (BIAS_ROWS - 128), idx)
            for h4 in range(4):
                found = []
                for h in (h4, h4 + 4):
                    lo = jnp.take_along_axis(tables[h][0], inner, axis=1)
                    hi = jnp.take_along_axis(tables[h][1], inner, axis=1)
                    found.append(jnp.where(high, hi, lo))
                value = jnp.where(first, found[0], found[1])
                to = a * 128 + h4 * QROWS + i
                bias[to : to + 8, :] = jnp.where(off, masked_score, value)


W_STEP = 256


def cap_kernel(x_ref, gain_ref, w_ref, out_ref, normed, qkv):
    n = SLOT_TOKENS
    gain = gain_ref[...]
    for i in range(0, SLOT_TOKENS, 32):
        normed[i : i + 32] = norm_rows(x_ref[i : i + 32].astype(jnp.float32), gain).astype(jnp.bfloat16)
    pick = (lax.broadcasted_iota(jnp.int32, (8, 128), 1) == 0).astype(jnp.bfloat16)
    first = lax.dot_general(
        pick, x_ref[:, 0:128], (((1,), (1,)), ((), ())), preferred_element_type=jnp.float32
    )
    empty = jnp.where(first[0:1] > EMPTY_ABOVE, masked_score, 0.0)
    for j in range(3 * HW // W_STEP):
        at = slice(j * W_STEP, j * W_STEP + W_STEP)
        part = jnp.dot(normed[...], w_ref[:, at], preferred_element_type=jnp.float32)
        qkv[:, at] = part.astype(jnp.bfloat16)
    low = lax.broadcasted_iota(jnp.int32, (n, 128), 1) < HD
    for pair in range(HEADS // 2):
        at = pair * 128
        q = qkv[:, at : at + 128] * jnp.bfloat16(HD ** (-0.5))
        k = qkv[:, HW + at : HW + at + 128]
        v = qkv[:, 2 * HW + at : 2 * HW + at + 128]
        mixed = []
        for half in range(2):
            mine = low if half == 0 else jnp.logical_not(low)
            qh = jnp.where(mine, q, jnp.zeros_like(q))
            s = lax.dot_general(qh, k, (((1,), (1,)), ((), ())), preferred_element_type=jnp.float32)
            s = s + empty
            raised = jnp.exp(s - jnp.max(s, axis=-1, keepdims=True))
            both = jnp.dot(raised.astype(jnp.bfloat16), v, preferred_element_type=jnp.float32)
            mixed.append(both * (1.0 / jnp.sum(raised, axis=-1, keepdims=True)))
        out_ref[:, at : at + 128] = jnp.where(low, mixed[0], mixed[1]).astype(jnp.bfloat16)


def project(xs, xq, w_ref, qs, kv):
    for j in range(3 * HW // W_STEP):
        at = slice(j * W_STEP, j * W_STEP + W_STEP)
        if j * W_STEP < HW:
            qs[:, at] = jnp.dot(xq[...], w_ref[:, at], preferred_element_type=jnp.float32).astype(jnp.bfloat16)
        else:
            to = slice(j * W_STEP - HW, j * W_STEP - HW + W_STEP)
            kv[:, to] = jnp.dot(xs[...], w_ref[:, at], preferred_element_type=jnp.float32).astype(jnp.bfloat16)


def attend(qs, kv, bias, scores, weights, wout):
    count = qs.shape[0] // QROWS
    head = lax.broadcasted_iota(jnp.int32, (QROWS, HW), 1) // HD % 4
    blank = jnp.zeros((WTOK, HW // 2), jnp.bfloat16)

    def two_groups(x):
        top = jnp.concatenate([x[:, : HW // 2], blank], 1)
        low = jnp.concatenate([blank, x[:, HW // 2 :]], 1)
        return jnp.concatenate([top, low], 0)

    for n in range(count):
        q = qs[n * QROWS : n * QROWS + QROWS] * jnp.bfloat16(HD ** (-0.5))
        spread = jnp.concatenate([jnp.where(head == h, q, jnp.zeros_like(q)) for h in range(4)], 0)
        k = two_groups(kv[n * WTOK : n * WTOK + WTOK, 0:HW])
        s = lax.dot_general(spread, k, (((1,), (1,)), ((), ())), preferred_element_type=jnp.float32)
        a = n // (count // 2)
        scores[n * 128 : n * 128 + 128] = s + bias[a * 128 : a * 128 + 128]
    left = lax.broadcasted_iota(jnp.int32, (128, 128), 1) < WTOK
    for n in range(count):
        s = scores[n * 128 : n * 128 + 128]
        top0 = jnp.max(jnp.where(left, s, -jnp.inf), axis=-1, keepdims=True)
        top1 = jnp.max(jnp.where(left, -jnp.inf, s), axis=-1, keepdims=True)
        raised = jnp.exp(s - jnp.where(left, top0, top1))
        sum0 = jnp.sum(jnp.where(left, raised, 0.0), axis=-1, keepdims=True)
        sum1 = jnp.sum(jnp.where(left, 0.0, raised), axis=-1, keepdims=True)
        share = jnp.where(left, 1.0 / sum0, 1.0 / sum1)
        weights[n * 128 : n * 128 + 128] = (raised * share).astype(jnp.bfloat16)
    for n in range(count):
        v = two_groups(kv[n * WTOK : n * WTOK + WTOK, HW : 2 * HW])
        o = jnp.dot(weights[n * 128 : n * 128 + 128], v, preferred_element_type=jnp.float32)
        total = o[0:QROWS]
        for h in range(1, 4):
            total = jnp.where(head == h, o[h * QROWS : h * QROWS + QROWS], total)
        wout[n] = total


def place(blocks, per_row, r, n, xs, xq):
    a, wr = r // WIN, r % WIN
    both = jnp.concatenate(blocks, 0).astype(jnp.bfloat16)
    to = (a * per_row + n) * WTOK + wr * WIN
    xs[to : to + 16] = both
    if (wr >= HALF) == (a == 0):
        to = (a * per_row + n) * QROWS + (wr % HALF) * WIN
        xq[to : to + 16] = both


INNER = 3
OUTER = 2


def inner_kernel(
    own_ref, north_ref, south_ref, gain_ref, bias, w_ref, wout, rims_ref, xs, xq, kv, qs, scores, weights,
):
    gain = gain_ref[...]
    lower = lax.broadcasted_iota(jnp.int32, (8, D), 0) < HALF
    rows = [(north_ref, i) for i in range(HALF)] + [(own_ref, i) for i in range(RH)]
    rows += [(south_ref, i) for i in range(HALF)]
    for r in range(0, RH + WIN, 2):
        turned = []
        for ref, i in rows[r : r + 2]:
            normed = norm_rows(ref[i].astype(jnp.float32), gain)
            turned.append([pltpu.roll(normed[j * 8 : j * 8 + 8], HALF, 0) for j in range(4)])
        for n in range(INNER):
            place([jnp.where(lower, row[n], row[n + 1]) for row in turned], INNER, r, n, xs, xq)
        for side in range(2):
            both = jnp.concatenate([row[3 * side] for row in turned], 0)
            rims_ref[side, r * 8 : r * 8 + 16] = both.astype(jnp.bfloat16)
    project(xs, xq, w_ref, qs, kv)
    attend(qs, kv, bias, scores, weights, wout)


def outer_kernel(
    left_ref, right_ref, rims_ref, inner_ref, gain_ref, bias, hot_ref, w_ref,
    out_ref, cap_ref, undo_ref, xs, xq, kv, qs, scores, weights, wout, edges, full,
):
    gain = gain_ref[...]
    lat = lax.axis_index("lat")

    polar = (lat == 0) | (lat == lax.axis_size("lat") - 1)
    undo = jnp.transpose(hot_ref[...].astype(jnp.float32))
    undo_ref[...] = jnp.where(polar, undo, 0.0).astype(jnp.bfloat16)

    for side, ref in enumerate((left_ref, right_ref)):
        for i in range(0, 64, 32):
            edges[side, i : i + 32] = norm_rows(ref[i : i + 32].astype(jnp.float32), gain)
    lower = lax.broadcasted_iota(jnp.int32, (8, D), 0) < HALF
    for r in range(0, RH + WIN, 2):
        lo = edges[0, r * 4 : r * 4 + 8]
        hi = edges[1, r * 4 : r * 4 + 8]
        lows, highs = [lo, pltpu.roll(lo, HALF, 0)], [pltpu.roll(hi, HALF, 0), hi]
        heads = rims_ref[0, r * 8 : r * 8 + 16].astype(jnp.float32)
        tails = rims_ref[1, r * 8 : r * 8 + 16].astype(jnp.float32)
        place([jnp.where(lower, lows[k], heads[k * 8 : k * 8 + 8]) for k in range(2)], OUTER, r, 0, xs, xq)
        place([jnp.where(lower, tails[k * 8 : k * 8 + 8], highs[k]) for k in range(2)], OUTER, r, 1, xs, xq)
    project(xs, xq, w_ref, qs, kv)
    attend(qs, kv, bias, scores, weights, wout)

    lower = lax.broadcasted_iota(jnp.int32, (8, HW), 0) < HALF
    for r in range(RH):
        a, wr = r // HALF, r % HALF
        at = slice(wr * WIN, wr * WIN + WIN)
        parts = [wout[a * OUTER, at]]
        parts += [inner_ref[a * INNER + n, at] for n in range(INNER)]
        parts += [wout[a * OUTER + 1, at]]
        turned = [pltpu.roll(part, HALF, 0) for part in parts]
        for j in range(4):
            to = r * RW + j * 8
            full[to : to + 8] = jnp.where(lower, turned[j], turned[j + 1])
    out_ref[...] = full[...].astype(jnp.bfloat16)
    cap_ref[...] = jnp.where(lat == 0, full[0:CAP_TOKENS], full[CAP_TOKENS:])


def join_kernel(win_ref, back_ref, undo_ref, out_in, out_ref, mixed, sem):
    cap = jnp.dot(undo_ref[...], back_ref[...], preferred_element_type=jnp.float32)
    mixed[...] = (win_ref[...] + cap).astype(jnp.bfloat16)
    start = jnp.where(lax.axis_index("lat") == 0, 0, CAP_TOKENS)
    copy = pltpu.make_async_copy(mixed, out_ref.at[pl.ds(pl.multiple_of(start, CAP_TOKENS), CAP_TOKENS)], sem)
    copy.start()
    copy.wait()


def sds(shape, dtype):
    return jax.ShapeDtypeStruct(shape, dtype)


def call(kernel, outs, ins, out_specs, scratch, vmem, flops, nbytes, trans=0, aliases=None):
    return pl.pallas_call(
        kernel,
        out_shape=outs,
        in_specs=ins,
        out_specs=out_specs,
        scratch_shapes=scratch,
        compiler_params=pltpu.CompilerParams(vmem_limit_bytes=vmem),
        input_output_aliases=aliases or {},
        cost_estimate=pl.CostEstimate(flops=flops, bytes_accessed=nbytes, transcendentals=trans),
    )


def exchange(block):
    return lax.all_to_all(block, "lon", split_axis=0, concat_axis=0, tiled=True)


def layer(tokens, ln_gain, w_qkv, bias_table, bias_index, cap_group):
    lat_count = lax.axis_size("lat")
    lon_count = lax.axis_size("lon")
    bf16, f32 = jnp.bfloat16, jnp.float32
    gain = ln_gain.reshape(1, D)
    groups = cap_group.transpose(0, 2, 3, 1)

    packed, hot = call(
        pack_kernel, (sds((SLOT_TOKENS, D), bf16), sds((SLOT_TOKENS, CAP_TOKENS), bf16)),
        [aspec(), hspec()], (hspec(), hspec()),
        [
            SMEM((2, CAP, 1, TILE_COLS), jnp.int32),
            VMEM((CAP, RW, D), bf16),
            VMEM((SLOT_TOKENS, D), bf16),
            VMEM((SLOT_TOKENS, CAP_TOKENS), bf16),
            pltpu.SemaphoreType.DMA,
            pltpu.SemaphoreType.DMA,
            pltpu.SemaphoreType.DMA((SLOT_TOKENS // PACK_STEP + 1,)),
        ],
        PACK_VMEM, 4 << 30, 1 << 20,
    )(groups, tokens)
    arrived = exchange(packed.reshape(lon_count, MOST * TW, D)).reshape(SLOT_TOKENS, D)

    down = [(i, i + 1) for i in range(lat_count - 1)]
    up = [(i + 1, i) for i in range(lat_count - 1)]
    east = [(i, (i + 1) % lon_count) for i in range(lon_count)]
    west = [((i + 1) % lon_count, i) for i in range(lon_count)]
    tied, _ = lax.optimization_barrier((tokens, packed))
    north = lax.ppermute(tied[RH - HALF :], "lat", down)
    south = lax.ppermute(tied[:HALF], "lat", up)
    bias, gain = call(
        bias_kernel, (sds((2 * 128, 128), f32), sds((1, D), f32)), [vspec()] * 3, (vspec(), vspec()), [],
        SOME_VMEM, 1 << 18, 1 << 18,
    )(bias_table, bias_index, gain)
    side = sds(((RH + WIN) * HALF, D), bf16)
    head, tail = call(
        edge_kernel, (side, side), [vspec()] * 3, (vspec(), vspec()), [],
        SOME_VMEM, 4 << 30, 3 << 19,
    )(tokens, north, south)
    left = lax.ppermute(tail, "lon", east)
    right = lax.ppermute(head, "lon", west)

    cap_result = call(
        cap_kernel, sds((SLOT_TOKENS, HW), bf16),
        [vspec()] * 3, vspec(),
        [VMEM((SLOT_TOKENS, D), bf16), VMEM((SLOT_TOKENS, 3 * HW), bf16)],
        SOME_VMEM, 1100 << 20, 4 << 20, 1 << 19,
    )(arrived, gain, w_qkv)
    returned = exchange(cap_result.reshape(lon_count, MOST * TW, HW)).reshape(SLOT_TOKENS, HW)

    def scratch(count):
        return [
            VMEM((count * WTOK, D), bf16),
            VMEM((count * QROWS, D), bf16),
            VMEM((count * WTOK, 2 * HW), bf16),
            VMEM((count * QROWS, HW), bf16),
            VMEM((count * 128, 128), f32),
            VMEM((count * 128, 128), bf16),
        ]

    inner, rims = call(
        inner_kernel,
        (sds((2 * INNER, QROWS, HW), f32), sds((2, (RH + WIN) * 8, D), bf16)),
        [vspec()] * 6, (vspec(), vspec()), scratch(2 * INNER),
        SOME_VMEM, 1400 << 20, 5 << 20, 1 << 17,
    )(tokens, north, south, gain, bias, w_qkv)
    win_out, cap_rows, undo = call(
        outer_kernel,
        (sds((RH * RW, HW), bf16), sds((CAP_TOKENS, HW), f32), sds((CAP_TOKENS, SLOT_TOKENS), bf16)),
        [vspec()] * 8, (vspec(),) * 3,
        scratch(2 * OUTER)
        + [VMEM((2 * OUTER, QROWS, HW), f32), VMEM((2, 64, D), f32), VMEM((RH * RW, HW), f32)],
        SOME_VMEM, 900 << 20, 5 << 20, 1 << 17,
    )(left, right, rims, inner, gain, bias, hot, w_qkv)
    mixed = call(
        join_kernel, sds((RH * RW, HW), bf16),
        [vspec()] * 3 + [aspec()], aspec(),
        [VMEM((CAP_TOKENS, HW), bf16), pltpu.SemaphoreType.DMA],
        8 << 20, 2 * CAP_TOKENS * SLOT_TOKENS * HW, 1 << 19, aliases={3: 0},
    )(cap_rows, returned, undo, win_out)
    return mixed.reshape(RH, RW, HW)


def solution(mesh):
    placed = (P("lat", "lon", None), P(), P(), P(), P(), P(None, "lon", None, None))
    return jax.shard_map(layer, mesh=mesh, in_specs=placed, out_specs=P("lat", "lon", None), check_vma=False)
```

```python
import jax
import jax.numpy as jnp
from jax import lax
from jax.experimental import pallas as pl
from jax.experimental.pallas import tpu as pltpu
from jax.sharding import PartitionSpec as P


D = 1024
HEADS = 8
HD = 64
WIN = 8
TW = 4
CAP = 4
RH = 8
RW = 32
HW = 512
HALF = 4
BIAS_ROWS = 225
TILES_DEV = 32
TILE_COLS = RW // TW
GROUPS = 32
MOST = 2
SLOT_TOKENS = GROUPS * MOST * TW
CAP_TOKENS = CAP * RW
WTOK = WIN * WIN
QROWS = HALF * WIN

epsilon = 1e-05
masked_score = -1e30
EMPTY = 128.0
EMPTY_ABOVE = 64.0

ALL_VMEM = 67043328
PACK_VMEM = ALL_VMEM - 409600
SOME_VMEM = 24 << 20

VMEM = pltpu.VMEM
SMEM = pltpu.SMEM


def vspec():
    return pl.BlockSpec(memory_space=VMEM)


def aspec():
    return pl.BlockSpec(memory_space=pl.ANY)


def hspec():
    return pl.BlockSpec(memory_space=pltpu.HBM)


def norm_rows(values, gain):
    center = jnp.mean(values, axis=-1, keepdims=True)
    shifted = values - center
    spread = jnp.mean(jnp.square(shifted), axis=-1, keepdims=True)
    return shifted * lax.rsqrt(spread + epsilon) * gain


def slot_rows(group_ref, pole, lane):
    tile = lane // TW
    names = [group_ref[pole, t // TILE_COLS, 0, t % TILE_COLS] for t in range(TILES_DEV)]
    group = jnp.zeros_like(lane)
    for t in range(TILES_DEV):
        group = jnp.where(tile == t, names[t], group)
    rank = jnp.zeros_like(lane)
    for t in range(TILES_DEV):
        same = (group == names[t]) & (tile > t)
        rank = rank + same.astype(jnp.int32)
    return (group * MOST + rank) * TW + lane % TW


PACK_STEP = 64


def pack_kernel(names_ref, tokens_ref, send_ref, hot_ref, group_ref, rows, out, hot, name_sem, sem, out_sem):
    north = lax.axis_index("lat") == 0
    pole = jnp.where(north, 0, 1)
    start = jnp.where(north, 0, RH - CAP)
    names = pltpu.make_async_copy(names_ref, group_ref, name_sem)
    names.start()
    copy = pltpu.make_async_copy(tokens_ref.at[pl.ds(start, CAP)], rows, sem)
    copy.start()
    names.wait()
    lane = lax.broadcasted_iota(jnp.int32, (8, CAP_TOKENS), 1)
    slot = slot_rows(group_ref, pole, lane)[0:1]
    copy.wait()
    x = rows[...].reshape(CAP_TOKENS, D)
    sends = []
    for n in range(SLOT_TOKENS // PACK_STEP):
        at = pl.ds(n * PACK_STEP, PACK_STEP)
        hit = lax.broadcasted_iota(jnp.int32, (PACK_STEP, CAP_TOKENS), 0) + n * PACK_STEP == slot
        here = hit.astype(jnp.float32)
        filled = jnp.max(here, axis=1, keepdims=True) > 0.5
        here = here.astype(jnp.bfloat16)
        hot[at, :] = here
        moved = jnp.dot(here, x, preferred_element_type=jnp.float32)
        out[at, :] = jnp.where(filled, moved, EMPTY).astype(jnp.bfloat16)
        sends.append(pltpu.make_async_copy(out.at[at], send_ref.at[at], out_sem.at[n]))
        sends[n].start()
    sends.append(pltpu.make_async_copy(hot, hot_ref, out_sem.at[len(sends)]))
    sends[-1].start()
    for send in sends:
        send.wait()


def edge_kernel(own_ref, north_ref, south_ref, near_ref, far_ref):
    even = lax.rem(lax.axis_index("lon"), 2) == 0
    lower = lax.broadcasted_iota(jnp.int32, (8, D), 0) < HALF
    pairs = [(north_ref, 0), (north_ref, 2)]
    pairs += [(own_ref, i) for i in range(0, RH, 2)]
    pairs += [(south_ref, 0), (south_ref, 2)]
    for n in range(0, len(pairs), 2):
        heads, tails = [], []
        for ref, i in pairs[n : n + 2]:
            first = [ref[i + k, 0:8].astype(jnp.float32) for k in range(2)]
            last = [ref[i + k, 24:32].astype(jnp.float32) for k in range(2)]
            heads.append(jnp.where(lower, first[0], pltpu.roll(first[1], HALF, 0)))
            tails.append(jnp.where(lower, pltpu.roll(last[0], HALF, 0), last[1]))
        head, tail = jnp.concatenate(heads, 0), jnp.concatenate(tails, 0)
        near_ref[n * 8 : n * 8 + 16] = jnp.where(even, tail, head).astype(jnp.bfloat16)
        far_ref[n * 8 : n * 8 + 16] = jnp.where(even, head, tail).astype(jnp.bfloat16)


def bias_kernel(table_ref, index_ref, gain_in, bias, gain_ref):
    gain_ref[...] = gain_in[...]
    lat = lax.axis_index("lat")
    lane = lax.broadcasted_iota(jnp.int32, (8, 128), 1)
    first = lane < WTOK
    key_row = (lane % WTOK) // WIN
    off_north = (lat == 0) & (key_row < HALF)
    off_south = (lat == lax.axis_size("lat") - 1) & (key_row >= HALF)
    tables = []
    for h in range(HEADS):
        parts = [table_ref[h : h + 1, c : c + 128] for c in (0, BIAS_ROWS - 128)]
        tables.append([jnp.broadcast_to(part, (8, 128)) for part in parts])
    for a in range(2):
        off = off_north if a == 0 else off_south
        for i in range(0, QROWS, 8):
            at = (QROWS if a == 0 else 0) + i
            idx = index_ref[at : at + 8, :]
            idx = jnp.concatenate([idx, idx], axis=1)
            high = idx >= 128
            inner = jnp.where(high, idx - (BIAS_ROWS - 128), idx)
            for h4 in range(4):
                found = []
                for h in (h4, h4 + 4):
                    lo = jnp.take_along_axis(tables[h][0], inner, axis=1)
                    hi = jnp.take_along_axis(tables[h][1], inner, axis=1)
                    found.append(jnp.where(high, hi, lo))
                value = jnp.where(first, found[0], found[1])
                to = a * 128 + h4 * QROWS + i
                bias[to : to + 8, :] = jnp.where(off, masked_score, value)


W_STEP = 256


def cap_kernel(x_ref, gain_ref, w_ref, out_ref, normed, qkv):
    n = SLOT_TOKENS
    gain = gain_ref[...]
    for i in range(0, SLOT_TOKENS, 32):
        normed[i : i + 32] = norm_rows(x_ref[i : i + 32].astype(jnp.float32), gain).astype(jnp.bfloat16)
    pick = (lax.broadcasted_iota(jnp.int32, (8, 128), 1) == 0).astype(jnp.bfloat16)
    first = lax.dot_general(
        pick, x_ref[:, 0:128], (((1,), (1,)), ((), ())), preferred_element_type=jnp.float32
    )
    empty = jnp.where(first[0:1] > EMPTY_ABOVE, masked_score, 0.0)
    for j in range(3 * HW // W_STEP):
        at = slice(j * W_STEP, j * W_STEP + W_STEP)
        part = jnp.dot(normed[...], w_ref[:, at], preferred_element_type=jnp.float32)
        qkv[:, at] = part.astype(jnp.bfloat16)
    low = lax.broadcasted_iota(jnp.int32, (n, 128), 1) < HD
    for pair in range(HEADS // 2):
        at = pair * 128
        q = qkv[:, at : at + 128] * jnp.bfloat16(HD ** (-0.5))
        k = qkv[:, HW + at : HW + at + 128]
        v = qkv[:, 2 * HW + at : 2 * HW + at + 128]
        mixed = []
        for half in range(2):
            mine = low if half == 0 else jnp.logical_not(low)
            qh = jnp.where(mine, q, jnp.zeros_like(q))
            s = lax.dot_general(qh, k, (((1,), (1,)), ((), ())), preferred_element_type=jnp.float32)
            s = s + empty
            raised = jnp.exp(s - jnp.max(s, axis=-1, keepdims=True))
            both = jnp.dot(raised.astype(jnp.bfloat16), v, preferred_element_type=jnp.float32)
            mixed.append(both * (1.0 / jnp.sum(raised, axis=-1, keepdims=True)))
        out_ref[:, at : at + 128] = jnp.where(low, mixed[0], mixed[1]).astype(jnp.bfloat16)


def project(xs, xq, w_ref, qs, kv):
    for j in range(3 * HW // W_STEP):
        at = slice(j * W_STEP, j * W_STEP + W_STEP)
        if j * W_STEP < HW:
            qs[:, at] = jnp.dot(xq[...], w_ref[:, at], preferred_element_type=jnp.float32).astype(jnp.bfloat16)
        else:
            to = slice(j * W_STEP - HW, j * W_STEP - HW + W_STEP)
            kv[:, to] = jnp.dot(xs[...], w_ref[:, at], preferred_element_type=jnp.float32).astype(jnp.bfloat16)


def attend(qs, kv, bias, scores, weights, wout):
    count = qs.shape[0] // QROWS
    head = lax.broadcasted_iota(jnp.int32, (QROWS, HW), 1) // HD % 4
    blank = jnp.zeros((WTOK, HW // 2), jnp.bfloat16)

    def two_groups(x):
        top = jnp.concatenate([x[:, : HW // 2], blank], 1)
        low = jnp.concatenate([blank, x[:, HW // 2 :]], 1)
        return jnp.concatenate([top, low], 0)

    for n in range(count):
        q = qs[n * QROWS : n * QROWS + QROWS] * jnp.bfloat16(HD ** (-0.5))
        spread = jnp.concatenate([jnp.where(head == h, q, jnp.zeros_like(q)) for h in range(4)], 0)
        k = two_groups(kv[n * WTOK : n * WTOK + WTOK, 0:HW])
        s = lax.dot_general(spread, k, (((1,), (1,)), ((), ())), preferred_element_type=jnp.float32)
        a = n // (count // 2)
        scores[n * 128 : n * 128 + 128] = s + bias[a * 128 : a * 128 + 128]
    left = lax.broadcasted_iota(jnp.int32, (128, 128), 1) < WTOK
    for n in range(count):
        s = scores[n * 128 : n * 128 + 128]
        top0 = jnp.max(jnp.where(left, s, -jnp.inf), axis=-1, keepdims=True)
        top1 = jnp.max(jnp.where(left, -jnp.inf, s), axis=-1, keepdims=True)
        raised = jnp.exp(s - jnp.where(left, top0, top1))
        sum0 = jnp.sum(jnp.where(left, raised, 0.0), axis=-1, keepdims=True)
        sum1 = jnp.sum(jnp.where(left, 0.0, raised), axis=-1, keepdims=True)
        share = jnp.where(left, 1.0 / sum0, 1.0 / sum1)
        weights[n * 128 : n * 128 + 128] = (raised * share).astype(jnp.bfloat16)
    for n in range(count):
        v = two_groups(kv[n * WTOK : n * WTOK + WTOK, HW : 2 * HW])
        o = jnp.dot(weights[n * 128 : n * 128 + 128], v, preferred_element_type=jnp.float32)
        total = o[0:QROWS]
        for h in range(1, 4):
            total = jnp.where(head == h, o[h * QROWS : h * QROWS + QROWS], total)
        wout[n] = total


def place(blocks, per_row, r, n, xs, xq):
    a, wr = r // WIN, r % WIN
    both = jnp.concatenate(blocks, 0).astype(jnp.bfloat16)
    to = (a * per_row + n) * WTOK + wr * WIN
    xs[to : to + 16] = both
    if (wr >= HALF) == (a == 0):
        to = (a * per_row + n) * QROWS + (wr % HALF) * WIN
        xq[to : to + 16] = both


INNER = 3
OUTER = 2


def inner_kernel(
    own_ref, north_ref, south_ref, gain_ref, bias, w_ref, wout, rims_ref, xs, xq, kv, qs, scores, weights,
):
    gain = gain_ref[...]
    lower = lax.broadcasted_iota(jnp.int32, (8, D), 0) < HALF
    rows = [(north_ref, i) for i in range(HALF)] + [(own_ref, i) for i in range(RH)]
    rows += [(south_ref, i) for i in range(HALF)]
    for r in range(0, RH + WIN, 2):
        turned = []
        for ref, i in rows[r : r + 2]:
            normed = norm_rows(ref[i].astype(jnp.float32), gain)
            turned.append([pltpu.roll(normed[j * 8 : j * 8 + 8], HALF, 0) for j in range(4)])
        for n in range(INNER):
            place([jnp.where(lower, row[n], row[n + 1]) for row in turned], INNER, r, n, xs, xq)
        for side in range(2):
            both = jnp.concatenate([row[3 * side] for row in turned], 0)
            rims_ref[side, r * 8 : r * 8 + 16] = both.astype(jnp.bfloat16)
    project(xs, xq, w_ref, qs, kv)
    attend(qs, kv, bias, scores, weights, wout)


def outer_kernel(
    near_ref, far_ref, rims_ref, inner_ref, gain_ref, bias, hot_ref, w_ref,
    out_ref, cap_ref, undo_ref, xs, xq, kv, qs, scores, weights, wout, edges, full,
):
    gain = gain_ref[...]
    lat = lax.axis_index("lat")

    polar = (lat == 0) | (lat == lax.axis_size("lat") - 1)
    undo = jnp.transpose(hot_ref[...].astype(jnp.float32))
    undo_ref[...] = jnp.where(polar, undo, 0.0).astype(jnp.bfloat16)

    even = lax.rem(lax.axis_index("lon"), 2) == 0
    for i in range(0, 64, 32):
        near = norm_rows(near_ref[i : i + 32].astype(jnp.float32), gain)
        far = norm_rows(far_ref[i : i + 32].astype(jnp.float32), gain)
        edges[0, i : i + 32] = jnp.where(even, far, near)
        edges[1, i : i + 32] = jnp.where(even, near, far)
    lower = lax.broadcasted_iota(jnp.int32, (8, D), 0) < HALF
    for r in range(0, RH + WIN, 2):
        lo = edges[0, r * 4 : r * 4 + 8]
        hi = edges[1, r * 4 : r * 4 + 8]
        lows, highs = [lo, pltpu.roll(lo, HALF, 0)], [pltpu.roll(hi, HALF, 0), hi]
        heads = rims_ref[0, r * 8 : r * 8 + 16].astype(jnp.float32)
        tails = rims_ref[1, r * 8 : r * 8 + 16].astype(jnp.float32)
        place([jnp.where(lower, lows[k], heads[k * 8 : k * 8 + 8]) for k in range(2)], OUTER, r, 0, xs, xq)
        place([jnp.where(lower, tails[k * 8 : k * 8 + 8], highs[k]) for k in range(2)], OUTER, r, 1, xs, xq)
    project(xs, xq, w_ref, qs, kv)
    attend(qs, kv, bias, scores, weights, wout)

    lower = lax.broadcasted_iota(jnp.int32, (8, HW), 0) < HALF
    for r in range(RH):
        a, wr = r // HALF, r % HALF
        at = slice(wr * WIN, wr * WIN + WIN)
        parts = [wout[a * OUTER, at]]
        parts += [inner_ref[a * INNER + n, at] for n in range(INNER)]
        parts += [wout[a * OUTER + 1, at]]
        turned = [pltpu.roll(part, HALF, 0) for part in parts]
        for j in range(4):
            to = r * RW + j * 8
            full[to : to + 8] = jnp.where(lower, turned[j], turned[j + 1])
    out_ref[...] = full[...].astype(jnp.bfloat16)
    cap_ref[...] = jnp.where(lat == 0, full[0:CAP_TOKENS], full[CAP_TOKENS:])


def join_kernel(win_ref, back_ref, undo_ref, out_in, out_ref, mixed, sem):
    cap = jnp.dot(undo_ref[...], back_ref[...], preferred_element_type=jnp.float32)
    mixed[...] = (win_ref[...] + cap).astype(jnp.bfloat16)
    start = jnp.where(lax.axis_index("lat") == 0, 0, CAP_TOKENS)
    copy = pltpu.make_async_copy(mixed, out_ref.at[pl.ds(pl.multiple_of(start, CAP_TOKENS), CAP_TOKENS)], sem)
    copy.start()
    copy.wait()


def sds(shape, dtype):
    return jax.ShapeDtypeStruct(shape, dtype)


def call(kernel, outs, ins, out_specs, scratch, vmem, flops, nbytes, trans=0, aliases=None):
    return pl.pallas_call(
        kernel,
        out_shape=outs,
        in_specs=ins,
        out_specs=out_specs,
        scratch_shapes=scratch,
        compiler_params=pltpu.CompilerParams(vmem_limit_bytes=vmem),
        input_output_aliases=aliases or {},
        cost_estimate=pl.CostEstimate(flops=flops, bytes_accessed=nbytes, transcendentals=trans),
    )


def exchange(block):
    return lax.all_to_all(block, "lon", split_axis=0, concat_axis=0, tiled=True)


def layer(tokens, ln_gain, w_qkv, bias_table, bias_index, cap_group):
    lat_count = lax.axis_size("lat")
    lon_count = lax.axis_size("lon")
    bf16, f32 = jnp.bfloat16, jnp.float32
    gain = ln_gain.reshape(1, D)
    groups = cap_group.transpose(0, 2, 3, 1)

    packed, hot = call(
        pack_kernel, (sds((SLOT_TOKENS, D), bf16), sds((SLOT_TOKENS, CAP_TOKENS), bf16)),
        [aspec(), hspec()], (hspec(), hspec()),
        [
            SMEM((2, CAP, 1, TILE_COLS), jnp.int32),
            VMEM((CAP, RW, D), bf16),
            VMEM((SLOT_TOKENS, D), bf16),
            VMEM((SLOT_TOKENS, CAP_TOKENS), bf16),
            pltpu.SemaphoreType.DMA,
            pltpu.SemaphoreType.DMA,
            pltpu.SemaphoreType.DMA((SLOT_TOKENS // PACK_STEP + 1,)),
        ],
        PACK_VMEM, 4 << 30, 1 << 20,
    )(groups, tokens)
    arrived = exchange(packed.reshape(lon_count, MOST * TW, D)).reshape(SLOT_TOKENS, D)

    down = [(i, i + 1) for i in range(lat_count - 1)]
    up = [(i + 1, i) for i in range(lat_count - 1)]
    pairs = [(i, i + 1 - 2 * (i % 2)) for i in range(lon_count)]
    across = [(i, (i - 1 + 2 * (i % 2)) % lon_count) for i in range(lon_count)]
    tied, _ = lax.optimization_barrier((tokens, packed))
    north = lax.ppermute(tied[RH - HALF :], "lat", down)
    south = lax.ppermute(tied[:HALF], "lat", up)
    bias, gain = call(
        bias_kernel, (sds((2 * 128, 128), f32), sds((1, D), f32)), [vspec()] * 3, (vspec(), vspec()), [],
        SOME_VMEM, 1 << 18, 1 << 18,
    )(bias_table, bias_index, gain)
    side = sds(((RH + WIN) * HALF, D), bf16)
    near, far = call(
        edge_kernel, (side, side), [vspec()] * 3, (vspec(), vspec()), [],
        SOME_VMEM, 4 << 30, 3 << 19,
    )(tokens, north, south)
    far = lax.ppermute(far, "lon", across)
    near = lax.ppermute(near, "lon", pairs)

    cap_result = call(
        cap_kernel, sds((SLOT_TOKENS, HW), bf16),
        [vspec()] * 3, vspec(),
        [VMEM((SLOT_TOKENS, D), bf16), VMEM((SLOT_TOKENS, 3 * HW), bf16)],
        SOME_VMEM, 1100 << 20, 4 << 20, 1 << 19,
    )(arrived, gain, w_qkv)
    returned = exchange(cap_result.reshape(lon_count, MOST * TW, HW)).reshape(SLOT_TOKENS, HW)

    def scratch(count):
        return [
            VMEM((count * WTOK, D), bf16),
            VMEM((count * QROWS, D), bf16),
            VMEM((count * WTOK, 2 * HW), bf16),
            VMEM((count * QROWS, HW), bf16),
            VMEM((count * 128, 128), f32),
            VMEM((count * 128, 128), bf16),
        ]

    inner, rims = call(
        inner_kernel,
        (sds((2 * INNER, QROWS, HW), f32), sds((2, (RH + WIN) * 8, D), bf16)),
        [vspec()] * 6, (vspec(), vspec()), scratch(2 * INNER),
        SOME_VMEM, 1400 << 20, 5 << 20, 1 << 17,
    )(tokens, north, south, gain, bias, w_qkv)
    win_out, cap_rows, undo = call(
        outer_kernel,
        (sds((RH * RW, HW), bf16), sds((CAP_TOKENS, HW), f32), sds((CAP_TOKENS, SLOT_TOKENS), bf16)),
        [vspec()] * 8, (vspec(),) * 3,
        scratch(2 * OUTER)
        + [VMEM((2 * OUTER, QROWS, HW), f32), VMEM((2, 64, D), f32), VMEM((RH * RW, HW), f32)],
        SOME_VMEM, 900 << 20, 5 << 20, 1 << 17,
    )(near, far, rims, inner, gain, bias, hot, w_qkv)
    mixed = call(
        join_kernel, sds((RH * RW, HW), bf16),
        [vspec()] * 3 + [aspec()], aspec(),
        [VMEM((CAP_TOKENS, HW), bf16), pltpu.SemaphoreType.DMA],
        8 << 20, 2 * CAP_TOKENS * SLOT_TOKENS * HW, 1 << 19, aliases={3: 0},
    )(cap_rows, returned, undo, win_out)
    return mixed.reshape(RH, RW, HW)


def solution(mesh):
    placed = (P("lat", "lon", None), P(), P(), P(), P(), P(None, "lon", None, None))
    return jax.shard_map(layer, mesh=mesh, in_specs=placed, out_specs=P("lat", "lon", None), check_vma=False)
```

```python
import jax
import jax.numpy as jnp
from jax import lax
from jax.experimental import pallas as pl
from jax.experimental.pallas import tpu as pltpu
from jax.sharding import PartitionSpec as P


D = 1024
HEADS = 8
HD = 64
WIN = 8
TW = 4
CAP = 4
RH = 8
RW = 32
HW = 512
HALF = 4
BIAS_ROWS = 225
TILES_DEV = 32
TILE_COLS = RW // TW
GROUPS = 32
MOST = 2
SLOT_TOKENS = GROUPS * MOST * TW
CAP_TOKENS = CAP * RW
WTOK = WIN * WIN
QROWS = HALF * WIN

epsilon = 1e-05
masked_score = -1e30
EMPTY = 128.0
EMPTY_ABOVE = 64.0

ALL_VMEM = 67043328
PACK_VMEM = ALL_VMEM - 409600
SOME_VMEM = 24 << 20

VMEM = pltpu.VMEM
SMEM = pltpu.SMEM


def vspec():
    return pl.BlockSpec(memory_space=VMEM)


def aspec():
    return pl.BlockSpec(memory_space=pl.ANY)


def hspec():
    return pl.BlockSpec(memory_space=pltpu.HBM)


def norm_rows(values, gain):
    center = jnp.mean(values, axis=-1, keepdims=True)
    shifted = values - center
    spread = jnp.mean(jnp.square(shifted), axis=-1, keepdims=True)
    return shifted * lax.rsqrt(spread + epsilon) * gain


def slot_rows(group_ref, pole, lane):
    tile = lane // TW
    names = [group_ref[pole, t // TILE_COLS, 0, t % TILE_COLS] for t in range(TILES_DEV)]
    group = jnp.zeros_like(lane)
    for t in range(TILES_DEV):
        group = jnp.where(tile == t, names[t], group)
    rank = jnp.zeros_like(lane)
    for t in range(TILES_DEV):
        same = (group == names[t]) & (tile > t)
        rank = rank + same.astype(jnp.int32)
    return (group * MOST + rank) * TW + lane % TW


PACK_STEP = 64


def pack_kernel(names_ref, tokens_ref, send_ref, hot_ref, group_ref, rows, out, hot, name_sem, sem, out_sem):
    north = lax.axis_index("lat") == 0
    pole = jnp.where(north, 0, 1)
    start = jnp.where(north, 0, RH - CAP)
    names = pltpu.make_async_copy(names_ref, group_ref, name_sem)
    names.start()
    copy = pltpu.make_async_copy(tokens_ref.at[pl.ds(start, CAP)], rows, sem)
    copy.start()
    names.wait()
    lane = lax.broadcasted_iota(jnp.int32, (8, CAP_TOKENS), 1)
    slot = slot_rows(group_ref, pole, lane)[0:1]
    copy.wait()
    x = rows[...].reshape(CAP_TOKENS, D)
    sends = []
    for n in range(SLOT_TOKENS // PACK_STEP):
        at = pl.ds(n * PACK_STEP, PACK_STEP)
        hit = lax.broadcasted_iota(jnp.int32, (PACK_STEP, CAP_TOKENS), 0) + n * PACK_STEP == slot
        here = hit.astype(jnp.float32)
        filled = jnp.max(here, axis=1, keepdims=True) > 0.5
        here = here.astype(jnp.bfloat16)
        hot[at, :] = here
        moved = jnp.dot(here, x, preferred_element_type=jnp.float32)
        out[at, :] = jnp.where(filled, moved, EMPTY).astype(jnp.bfloat16)
        sends.append(pltpu.make_async_copy(out.at[at], send_ref.at[at], out_sem.at[n]))
        sends[n].start()
    sends.append(pltpu.make_async_copy(hot, hot_ref, out_sem.at[len(sends)]))
    sends[-1].start()
    for send in sends:
        send.wait()


def edge_kernel(own_ref, north_ref, south_ref, near_ref, far_ref):
    even = lax.rem(lax.axis_index("lon"), 2) == 0
    lower = lax.broadcasted_iota(jnp.int32, (8, D), 0) < HALF
    pairs = [(north_ref, 0), (north_ref, 2)]
    pairs += [(own_ref, i) for i in range(0, RH, 2)]
    pairs += [(south_ref, 0), (south_ref, 2)]
    for n in range(0, len(pairs), 2):
        heads, tails = [], []
        for ref, i in pairs[n : n + 2]:
            first = [ref[i + k, 0:8].astype(jnp.float32) for k in range(2)]
            last = [ref[i + k, 24:32].astype(jnp.float32) for k in range(2)]
            heads.append(jnp.where(lower, first[0], pltpu.roll(first[1], HALF, 0)))
            tails.append(jnp.where(lower, pltpu.roll(last[0], HALF, 0), last[1]))
        head, tail = jnp.concatenate(heads, 0), jnp.concatenate(tails, 0)
        near_ref[n * 8 : n * 8 + 16] = jnp.where(even, tail, head).astype(jnp.bfloat16)
        far_ref[n * 8 : n * 8 + 16] = jnp.where(even, head, tail).astype(jnp.bfloat16)


def bias_kernel(table_ref, index_ref, gain_in, bias, gain_ref):
    gain_ref[...] = gain_in[...]
    lat = lax.axis_index("lat")
    lane = lax.broadcasted_iota(jnp.int32, (8, 128), 1)
    first = lane < WTOK
    key_row = (lane % WTOK) // WIN
    off_north = (lat == 0) & (key_row < HALF)
    off_south = (lat == lax.axis_size("lat") - 1) & (key_row >= HALF)
    tables = []
    for h in range(HEADS):
        parts = [table_ref[h : h + 1, c : c + 128] for c in (0, BIAS_ROWS - 128)]
        tables.append([jnp.broadcast_to(part, (8, 128)) for part in parts])
    for a in range(2):
        off = off_north if a == 0 else off_south
        for i in range(0, QROWS, 8):
            at = (QROWS if a == 0 else 0) + i
            idx = index_ref[at : at + 8, :]
            idx = jnp.concatenate([idx, idx], axis=1)
            high = idx >= 128
            inner = jnp.where(high, idx - (BIAS_ROWS - 128), idx)
            for h4 in range(4):
                found = []
                for h in (h4, h4 + 4):
                    lo = jnp.take_along_axis(tables[h][0], inner, axis=1)
                    hi = jnp.take_along_axis(tables[h][1], inner, axis=1)
                    found.append(jnp.where(high, hi, lo))
                value = jnp.where(first, found[0], found[1])
                to = a * 128 + h4 * QROWS + i
                bias[to : to + 8, :] = jnp.where(off, masked_score, value)


W_STEP = 256


def cap_kernel(x_ref, gain_ref, w_ref, out_ref, normed, qkv):
    n = SLOT_TOKENS
    gain = gain_ref[...]
    for i in range(0, SLOT_TOKENS, 32):
        normed[i : i + 32] = norm_rows(x_ref[i : i + 32].astype(jnp.float32), gain).astype(jnp.bfloat16)
    pick = (lax.broadcasted_iota(jnp.int32, (8, 128), 1) == 0).astype(jnp.bfloat16)
    first = lax.dot_general(
        pick, x_ref[:, 0:128], (((1,), (1,)), ((), ())), preferred_element_type=jnp.float32
    )
    empty = jnp.where(first[0:1] > EMPTY_ABOVE, masked_score, 0.0)
    for j in range(3 * HW // W_STEP):
        at = slice(j * W_STEP, j * W_STEP + W_STEP)
        part = jnp.dot(normed[...], w_ref[:, at], preferred_element_type=jnp.float32)
        qkv[:, at] = part.astype(jnp.bfloat16)
    low = lax.broadcasted_iota(jnp.int32, (n, 128), 1) < HD
    for pair in range(HEADS // 2):
        at = pair * 128
        q = qkv[:, at : at + 128] * jnp.bfloat16(HD ** (-0.5))
        k = qkv[:, HW + at : HW + at + 128]
        v = qkv[:, 2 * HW + at : 2 * HW + at + 128]
        mixed = []
        for half in range(2):
            mine = low if half == 0 else jnp.logical_not(low)
            qh = jnp.where(mine, q, jnp.zeros_like(q))
            s = lax.dot_general(qh, k, (((1,), (1,)), ((), ())), preferred_element_type=jnp.float32)
            s = s + empty
            raised = jnp.exp(s - jnp.max(s, axis=-1, keepdims=True))
            both = jnp.dot(raised.astype(jnp.bfloat16), v, preferred_element_type=jnp.float32)
            mixed.append(both * (1.0 / jnp.sum(raised, axis=-1, keepdims=True)))
        out_ref[:, at : at + 128] = jnp.where(low, mixed[0], mixed[1]).astype(jnp.bfloat16)


def project(xs, xq, w_ref, qs, kv):
    for j in range(3 * HW // W_STEP):
        at = slice(j * W_STEP, j * W_STEP + W_STEP)
        if j * W_STEP < HW:
            qs[:, at] = jnp.dot(xq[...], w_ref[:, at], preferred_element_type=jnp.float32).astype(jnp.bfloat16)
        else:
            to = slice(j * W_STEP - HW, j * W_STEP - HW + W_STEP)
            kv[:, to] = jnp.dot(xs[...], w_ref[:, at], preferred_element_type=jnp.float32).astype(jnp.bfloat16)


def attend(qs, kv, bias, scores, weights, wout):
    count = qs.shape[0] // QROWS
    head = lax.broadcasted_iota(jnp.int32, (QROWS, HW), 1) // HD % 4
    blank = jnp.zeros((WTOK, HW // 2), jnp.bfloat16)

    def two_groups(x):
        top = jnp.concatenate([x[:, : HW // 2], blank], 1)
        low = jnp.concatenate([blank, x[:, HW // 2 :]], 1)
        return jnp.concatenate([top, low], 0)

    for n in range(count):
        q = qs[n * QROWS : n * QROWS + QROWS] * jnp.bfloat16(HD ** (-0.5))
        spread = jnp.concatenate([jnp.where(head == h, q, jnp.zeros_like(q)) for h in range(4)], 0)
        k = two_groups(kv[n * WTOK : n * WTOK + WTOK, 0:HW])
        s = lax.dot_general(spread, k, (((1,), (1,)), ((), ())), preferred_element_type=jnp.float32)
        a = n // (count // 2)
        scores[n * 128 : n * 128 + 128] = s + bias[a * 128 : a * 128 + 128]
    left = lax.broadcasted_iota(jnp.int32, (128, 128), 1) < WTOK
    for n in range(count):
        s = scores[n * 128 : n * 128 + 128]
        top0 = jnp.max(jnp.where(left, s, -jnp.inf), axis=-1, keepdims=True)
        top1 = jnp.max(jnp.where(left, -jnp.inf, s), axis=-1, keepdims=True)
        raised = jnp.exp(s - jnp.where(left, top0, top1))
        sum0 = jnp.sum(jnp.where(left, raised, 0.0), axis=-1, keepdims=True)
        sum1 = jnp.sum(jnp.where(left, 0.0, raised), axis=-1, keepdims=True)
        share = jnp.where(left, 1.0 / sum0, 1.0 / sum1)
        weights[n * 128 : n * 128 + 128] = (raised * share).astype(jnp.bfloat16)
    for n in range(count):
        v = two_groups(kv[n * WTOK : n * WTOK + WTOK, HW : 2 * HW])
        o = jnp.dot(weights[n * 128 : n * 128 + 128], v, preferred_element_type=jnp.float32)
        total = o[0:QROWS]
        for h in range(1, 4):
            total = jnp.where(head == h, o[h * QROWS : h * QROWS + QROWS], total)
        wout[n] = total


def place(blocks, per_row, r, n, xs, xq):
    a, wr = r // WIN, r % WIN
    both = jnp.concatenate(blocks, 0).astype(jnp.bfloat16)
    to = (a * per_row + n) * WTOK + wr * WIN
    xs[to : to + 16] = both
    if (wr >= HALF) == (a == 0):
        to = (a * per_row + n) * QROWS + (wr % HALF) * WIN
        xq[to : to + 16] = both


INNER = 3
OUTER = 2


def inner_kernel(
    own_ref, north_ref, south_ref, gain_ref, bias, hot_ref, w_ref, wout, rims_ref, undo_ref, xs, xq, kv, qs, scores, weights,
):
    gain = gain_ref[...]
    lat = lax.axis_index("lat")

    polar = (lat == 0) | (lat == lax.axis_size("lat") - 1)
    undo = jnp.transpose(hot_ref[...].astype(jnp.float32))
    undo_ref[...] = jnp.where(polar, undo, 0.0).astype(jnp.bfloat16)

    lower = lax.broadcasted_iota(jnp.int32, (8, D), 0) < HALF
    rows = [(north_ref, i) for i in range(HALF)] + [(own_ref, i) for i in range(RH)]
    rows += [(south_ref, i) for i in range(HALF)]
    for r in range(0, RH + WIN, 2):
        turned = []
        for ref, i in rows[r : r + 2]:
            normed = norm_rows(ref[i].astype(jnp.float32), gain)
            turned.append([pltpu.roll(normed[j * 8 : j * 8 + 8], HALF, 0) for j in range(4)])
        for n in range(INNER):
            place([jnp.where(lower, row[n], row[n + 1]) for row in turned], INNER, r, n, xs, xq)
        for side in range(2):
            both = jnp.concatenate([row[3 * side] for row in turned], 0)
            rims_ref[side, r * 8 : r * 8 + 16] = both.astype(jnp.bfloat16)
    project(xs, xq, w_ref, qs, kv)
    attend(qs, kv, bias, scores, weights, wout)


def outer_kernel(
    near_ref, far_ref, rims_ref, inner_ref, gain_ref, bias, w_ref,
    out_ref, cap_ref, xs, xq, kv, qs, scores, weights, wout, edges, full,
):
    gain = gain_ref[...]
    lat = lax.axis_index("lat")
    even = lax.rem(lax.axis_index("lon"), 2) == 0
    for i in range(0, 64, 32):
        near = norm_rows(near_ref[i : i + 32].astype(jnp.float32), gain)
        far = norm_rows(far_ref[i : i + 32].astype(jnp.float32), gain)
        edges[0, i : i + 32] = jnp.where(even, far, near)
        edges[1, i : i + 32] = jnp.where(even, near, far)
    lower = lax.broadcasted_iota(jnp.int32, (8, D), 0) < HALF
    for r in range(0, RH + WIN, 2):
        lo = edges[0, r * 4 : r * 4 + 8]
        hi = edges[1, r * 4 : r * 4 + 8]
        lows, highs = [lo, pltpu.roll(lo, HALF, 0)], [pltpu.roll(hi, HALF, 0), hi]
        heads = rims_ref[0, r * 8 : r * 8 + 16].astype(jnp.float32)
        tails = rims_ref[1, r * 8 : r * 8 + 16].astype(jnp.float32)
        place([jnp.where(lower, lows[k], heads[k * 8 : k * 8 + 8]) for k in range(2)], OUTER, r, 0, xs, xq)
        place([jnp.where(lower, tails[k * 8 : k * 8 + 8], highs[k]) for k in range(2)], OUTER, r, 1, xs, xq)
    project(xs, xq, w_ref, qs, kv)
    attend(qs, kv, bias, scores, weights, wout)

    lower = lax.broadcasted_iota(jnp.int32, (8, HW), 0) < HALF
    for r in range(RH):
        a, wr = r // HALF, r % HALF
        at = slice(wr * WIN, wr * WIN + WIN)
        parts = [wout[a * OUTER, at]]
        parts += [inner_ref[a * INNER + n, at] for n in range(INNER)]
        parts += [wout[a * OUTER + 1, at]]
        turned = [pltpu.roll(part, HALF, 0) for part in parts]
        for j in range(4):
            to = r * RW + j * 8
            full[to : to + 8] = jnp.where(lower, turned[j], turned[j + 1])
    out_ref[...] = full[...].astype(jnp.bfloat16)
    cap_ref[...] = jnp.where(lat == 0, full[0:CAP_TOKENS], full[CAP_TOKENS:])


def join_kernel(win_ref, back_ref, undo_ref, out_in, out_ref, mixed, sem):
    cap = jnp.dot(undo_ref[...], back_ref[...], preferred_element_type=jnp.float32)
    mixed[...] = (win_ref[...] + cap).astype(jnp.bfloat16)
    start = jnp.where(lax.axis_index("lat") == 0, 0, CAP_TOKENS)
    copy = pltpu.make_async_copy(mixed, out_ref.at[pl.ds(pl.multiple_of(start, CAP_TOKENS), CAP_TOKENS)], sem)
    copy.start()
    copy.wait()


def sds(shape, dtype):
    return jax.ShapeDtypeStruct(shape, dtype)


def call(kernel, outs, ins, out_specs, scratch, vmem, flops, nbytes, trans=0, aliases=None):
    return pl.pallas_call(
        kernel,
        out_shape=outs,
        in_specs=ins,
        out_specs=out_specs,
        scratch_shapes=scratch,
        compiler_params=pltpu.CompilerParams(vmem_limit_bytes=vmem),
        input_output_aliases=aliases or {},
        cost_estimate=pl.CostEstimate(flops=flops, bytes_accessed=nbytes, transcendentals=trans),
    )


def exchange(block):
    return lax.all_to_all(block, "lon", split_axis=0, concat_axis=0, tiled=True)


def layer(tokens, ln_gain, w_qkv, bias_table, bias_index, cap_group):
    lat_count = lax.axis_size("lat")
    lon_count = lax.axis_size("lon")
    bf16, f32 = jnp.bfloat16, jnp.float32
    gain = ln_gain.reshape(1, D)
    groups = cap_group.transpose(0, 2, 3, 1)

    packed, hot = call(
        pack_kernel, (sds((SLOT_TOKENS, D), bf16), sds((SLOT_TOKENS, CAP_TOKENS), bf16)),
        [aspec(), hspec()], (hspec(), hspec()),
        [
            SMEM((2, CAP, 1, TILE_COLS), jnp.int32),
            VMEM((CAP, RW, D), bf16),
            VMEM((SLOT_TOKENS, D), bf16),
            VMEM((SLOT_TOKENS, CAP_TOKENS), bf16),
            pltpu.SemaphoreType.DMA,
            pltpu.SemaphoreType.DMA,
            pltpu.SemaphoreType.DMA((SLOT_TOKENS // PACK_STEP + 1,)),
        ],
        PACK_VMEM, 4 << 30, 1 << 20,
    )(groups, tokens)
    arrived = exchange(packed.reshape(lon_count, MOST * TW, D)).reshape(SLOT_TOKENS, D)

    down = [(i, i + 1) for i in range(lat_count - 1)]
    up = [(i + 1, i) for i in range(lat_count - 1)]
    pairs = [(i, i + 1 - 2 * (i % 2)) for i in range(lon_count)]
    across = [(i, (i - 1 + 2 * (i % 2)) % lon_count) for i in range(lon_count)]
    tied, _ = lax.optimization_barrier((tokens, packed))
    north = lax.ppermute(tied[RH - HALF :], "lat", down)
    south = lax.ppermute(tied[:HALF], "lat", up)
    bias, gain = call(
        bias_kernel, (sds((2 * 128, 128), f32), sds((1, D), f32)), [vspec()] * 3, (vspec(), vspec()), [],
        SOME_VMEM, 1 << 18, 1 << 18,
    )(bias_table, bias_index, gain)
    side = sds(((RH + WIN) * HALF, D), bf16)
    near, far = call(
        edge_kernel, (side, side), [vspec()] * 3, (vspec(), vspec()), [],
        SOME_VMEM, 4 << 30, 3 << 19,
    )(tokens, north, south)
    far = lax.ppermute(far, "lon", across)
    near = lax.ppermute(near, "lon", pairs)

    cap_result = call(
        cap_kernel, sds((SLOT_TOKENS, HW), bf16),
        [vspec()] * 3, vspec(),
        [VMEM((SLOT_TOKENS, D), bf16), VMEM((SLOT_TOKENS, 3 * HW), bf16)],
        SOME_VMEM, 1100 << 20, 4 << 20, 1 << 19,
    )(arrived, gain, w_qkv)
    returned = exchange(cap_result.reshape(lon_count, MOST * TW, HW)).reshape(SLOT_TOKENS, HW)

    def scratch(count):
        return [
            VMEM((count * WTOK, D), bf16),
            VMEM((count * QROWS, D), bf16),
            VMEM((count * WTOK, 2 * HW), bf16),
            VMEM((count * QROWS, HW), bf16),
            VMEM((count * 128, 128), f32),
            VMEM((count * 128, 128), bf16),
        ]

    inner, rims, undo = call(
        inner_kernel,
        (
            sds((2 * INNER, QROWS, HW), f32), sds((2, (RH + WIN) * 8, D), bf16),
            sds((CAP_TOKENS, SLOT_TOKENS), bf16),
        ),
        [vspec()] * 7, (vspec(),) * 3, scratch(2 * INNER),
        SOME_VMEM, 1400 << 20, 5 << 20, 1 << 17,
    )(tokens, north, south, gain, bias, hot, w_qkv)
    win_out, cap_rows = call(
        outer_kernel,
        (sds((RH * RW, HW), bf16), sds((CAP_TOKENS, HW), f32)),
        [vspec()] * 7, (vspec(),) * 2,
        scratch(2 * OUTER)
        + [VMEM((2 * OUTER, QROWS, HW), f32), VMEM((2, 64, D), f32), VMEM((RH * RW, HW), f32)],
        SOME_VMEM, 900 << 20, 5 << 20, 1 << 17,
    )(near, far, rims, inner, gain, bias, w_qkv)
    mixed = call(
        join_kernel, sds((RH * RW, HW), bf16),
        [vspec()] * 3 + [aspec()], aspec(),
        [VMEM((CAP_TOKENS, HW), bf16), pltpu.SemaphoreType.DMA],
        8 << 20, 2 * CAP_TOKENS * SLOT_TOKENS * HW, 1 << 19, aliases={3: 0},
    )(cap_rows, returned, undo, win_out)
    return mixed.reshape(RH, RW, HW)


def solution(mesh):
    placed = (P("lat", "lon", None), P(), P(), P(), P(), P(None, "lon", None, None))
    return jax.shard_map(layer, mesh=mesh, in_specs=placed, out_specs=P("lat", "lon", None), check_vma=False)
```
